128 devices in a mesh: atoms: 32 (over y, x, core), grid: 4 (over z).
Axes of the slice: x: 4, y: 4, z: 4, core: 2. Of those that a mesh axis runs over, the one named last changes fastest.
Arguments:
- column_blocks: bfloat16 [1024, 32, 256], P('atoms'), may hold values from -1 to 1
- onsite: bfloat16 [1024, 256], P('atoms'), may hold values from -1 to 1
- neighbor_ids: int32 [1024, 32], P('atoms'), may hold values from 0 to 1023, as said below
- task_atoms: int32 [512, 32], P(('atoms', 'grid')), may hold values from 0 to 1023, as said below
- chem_shift: float32 [512], P(('atoms', 'grid')), may hold values from -0.6 to 0.6
- basis_values: bfloat16 [512, 512, 1024], P(('atoms', 'grid')), may hold values from -0.59765625 to 0.59765625
- box_start: int32 [512], P(('atoms', 'grid')), may hold values from 0 to 252
- box_row: int32 [512], P(('atoms', 'grid')), may hold values from 0 to 16
- box_col: int32 [512], P(('atoms', 'grid')), may hold values from 0 to 112
Outputs:
- density_cols: bfloat16 [512, 512, 128], P(('atoms', 'grid'))
- rho: float32 [256, 32, 128], P('grid')
The draws below stay inside these ranges and needn't reach their ends.
Inputs may be any that keep to these rules, and one draw needn't show every extreme that they name: `task_atoms`: row a of a device's block of 4 tasks, task t, names 8 atoms from each of 4 devices' columns. The atoms named by one device's tasks are all different; at most 8 of them lie in one device's columns, and some device's columns hold exactly 8 of them. `neighbor_ids`: an atom's 32 entries are different atoms, never the atom itself.
All inputs are finite; a program needn't handle non-finite values. Where the reference program divides by a largest or mean magnitude, that divisor is 1e-20 or more.
Results may differ from the reference program's by a relative error of at most 0.007.
Values may be sent and summed in bfloat16 or wider, within the bound.
A program may use at most 64 MiB of HBM per device.

```python
import math
import jax
import jax.numpy as jnp
import numpy as np
from jax import lax

BS = 16
KNB = 32
PICK = 8
SPAN = 4
ITERS = 3
BOXP = 4
BOX_ROWS = 16
BOX_COLS = 16
GRID_ROWS = 32
GRID_COLS = 128
PL_SLAB = 64
ATOM_DEV = 32
TASK_DEV = 4
NNB = 32
ORDER = 512
CENTRAL = 128
BOX_POINTS = 1024
NA = 1024
TASKS = 512
PLANES = 256
N_ATOMS = 32
N_GRID = 4


def draw_column_blocks(key, part):
    scale_key, sign_key, level_key, spread_key, keep_key = jax.random.split(jax.random.fold_in(key, 53), 5)
    scale = jnp.exp(jax.random.uniform(scale_key, (NA, KNB, 1, 1), jnp.float32, math.log(0.003), 0.0))
    signs = jnp.where(jax.random.bernoulli(sign_key, 0.5, (NA, KNB, BS)), 1.0, -1.0).astype(jnp.float32)
    levels = jax.random.uniform(level_key, (NA, KNB, BS), jnp.float32, 0.5, 1.0)
    spread = jnp.clip(0.1 * jax.random.normal(spread_key, (NA, KNB, BS, BS), jnp.float32), -0.4, 0.4)
    keep = jax.random.bernoulli(keep_key, 0.3, (NA, KNB, BS, BS))
    identity = jnp.eye(BS, dtype=jnp.float32)
    diagonal_part = identity[None, None, :, :] * (signs * levels)[:, :, :, None]
    off_part = (1.0 - identity)[None, None, :, :] * jnp.where(keep, spread, 0.0)
    blocks = scale * (diagonal_part + off_part)
    return blocks.reshape(NA, KNB, BS * BS).astype(jnp.bfloat16)


def draw_onsite(key, part):
    first_key, second_key, third_key = jax.random.split(jax.random.fold_in(key, 37), 3)
    coupling = jnp.clip(0.025 * jax.random.normal(first_key, (NA, BS, BS), jnp.float32), -0.1, 0.1)
    magnitude = jax.random.uniform(second_key, (NA, BS), jnp.float32, 0.2, 0.6)
    upward = jax.random.bernoulli(third_key, 0.5, (NA, BS))
    levels = jnp.where(upward, magnitude, -magnitude)
    identity = jnp.eye(BS, dtype=jnp.float32)[None, :, :]
    matrix_full = (1.0 - identity) * coupling + levels[:, :, None] * identity
    return matrix_full.reshape(NA, BS * BS).astype(jnp.bfloat16)


def draw_neighbor_ids(key, part):
    half_window = (ATOM_DEV - 1) // 2
    offsets = np.array([(dq, dl) for dq in range(1 - SPAN, SPAN) for dl in range(-half_window, half_window + 1) if (dq, dl) != (0, 0)], dtype=np.int32)
    keys_all = jax.random.split(jax.random.fold_in(key, 11), NA)
    chosen = jax.vmap(lambda single: jax.random.permutation(single, offsets.shape[0])[:KNB])(keys_all)
    shift_dev = jnp.asarray(offsets[:, 0])[chosen]
    shift_local = jnp.asarray(offsets[:, 1])[chosen]
    atom_index = jnp.arange(NA, dtype=jnp.int32)
    holder = atom_index // ATOM_DEV
    within = atom_index % ATOM_DEV
    result = (holder[:, None] + shift_dev) % N_ATOMS * ATOM_DEV + (within[:, None] + shift_local) % ATOM_DEV
    return result.astype(jnp.int32)


def draw_task_atoms(key, part):
    device_count = TASKS // TASK_DEV
    first_key, second_key = jax.random.split(jax.random.fold_in(key, 23))
    base_dev = jax.random.randint(first_key, (device_count,), 0, N_ATOMS)
    base_local = jax.random.randint(second_key, (device_count,), 0, ATOM_DEV)
    task_index = jnp.arange(TASK_DEV, dtype=jnp.int32)[None, :, None, None]
    span_index = jnp.arange(SPAN, dtype=jnp.int32)[None, None, :, None]
    pick_index = jnp.arange(PICK, dtype=jnp.int32)[None, None, None, :]
    holder = (base_dev[:, None, None, None] + SPAN * task_index + span_index) % N_ATOMS
    within = (base_local[:, None, None, None] + PICK * task_index + pick_index) % ATOM_DEV
    result = holder * ATOM_DEV + within
    return result.reshape(TASKS, NNB).astype(jnp.int32)


def touch_ends(entries, rng, low, high):
    place = [jax.random.randint(jax.random.fold_in(rng, axis), (), 0, length) for axis, length in enumerate(entries.shape)]
    main_axis = entries.shape.index(max(entries.shape))
    beside = place[:main_axis] + [(place[main_axis] + 1) % entries.shape[main_axis]] + place[main_axis + 1:]
    return entries.at[tuple(place)].set(low).at[tuple(beside)].set(high)


def steps_of(own_key, extent, cuts, smallest, largest):
    def one(axis_at, blocks):
        draws = jax.random.uniform(jax.random.fold_in(jax.random.fold_in(own_key, 6), axis_at), (blocks,), jnp.float32, smallest / len(cuts), largest / len(cuts))
        return jnp.repeat(jnp.exp(draws), extent[axis_at] // blocks).reshape((-1,) + (1,) * (len(extent) - axis_at - 1))

    loudness = one(*cuts[0])
    for cut in cuts[1:]:
        loudness = loudness * one(*cut)
    return loudness


def scatter_about(stream_key, shape, scale, limit, pieces=(), held_as=jnp.bfloat16):
    factor_of = steps_of(stream_key, shape, pieces, -0.22, 0.18) if pieces else 1.0
    entries = jax.random.normal(stream_key, shape, jnp.float32) * scale * factor_of
    return jnp.minimum(jnp.maximum(entries, -limit), limit).astype(held_as)


def setup_inputs(seed: int = 0) -> dict:
    seeds = jax.random.split(jax.random.key(seed), 10)
    column_blocks = draw_column_blocks(jax.random.fold_in(seeds[9], 71), 0)
    onsite = draw_onsite(jax.random.fold_in(seeds[9], 71), 0)
    neighbor_ids = draw_neighbor_ids(jax.random.fold_in(seeds[9], 71), 0)
    task_atoms = draw_task_atoms(jax.random.fold_in(seeds[9], 71), 0)
    chem_shift = jnp.clip(jax.random.uniform(seeds[4], (TASKS,), jnp.float32, -0.6, 0.6) * steps_of(seeds[4], (TASKS,), ((0, 128),), -0.4, 0.0), -0.6, 0.6)
    basis_values = scatter_about(seeds[5], (TASKS, ORDER, BOX_POINTS), 0.1, 0.59765625, ((0, 128),))
    box_start = touch_ends(jax.random.randint(seeds[6], (TASKS,), 0, PLANES - BOXP + 1), jax.random.fold_in(seeds[6], 1), 0, PLANES - BOXP).astype(jnp.int32)
    box_row = touch_ends(jax.random.randint(seeds[7], (TASKS,), 0, GRID_ROWS - BOX_ROWS + 1), jax.random.fold_in(seeds[7], 1), 0, GRID_ROWS - BOX_ROWS).astype(jnp.int32)
    box_col = touch_ends(jax.random.randint(seeds[8], (TASKS,), 0, GRID_COLS - BOX_COLS + 1), jax.random.fold_in(seeds[8], 1), 0, GRID_COLS - BOX_COLS).astype(jnp.int32)
    return {"column_blocks": column_blocks, "onsite": onsite, "neighbor_ids": neighbor_ids, "task_atoms": task_atoms, "chem_shift": chem_shift, "basis_values": basis_values, "box_start": box_start, "box_row": box_row, "box_col": box_col}


exact_mode = lax.Precision.HIGHEST


def assemble(columns_in, onsite_in, links_in, members, offset):
    count = members.shape[0]
    matched = (links_in[None, :, :] == members[:, None, None]).astype(jnp.float32)
    blocks = columns_in.astype(jnp.float32).reshape(count, KNB, BS, BS)
    coupled = jnp.einsum("ijk,jkab->iajb", matched, blocks, precision=exact_mode)
    diagonal_part = jnp.einsum("ij,jab->iajb", jnp.eye(count, dtype=jnp.float32), onsite_in.astype(jnp.float32).reshape(count, BS, BS), precision=exact_mode)
    whole = (coupled + diagonal_part).reshape(count * BS, count * BS)
    return 0.5 * (whole + whole.T) - offset * jnp.eye(count * BS, dtype=jnp.float32)


def sign_columns(matrix):
    order_size = matrix.shape[0]
    identity = jnp.eye(order_size, dtype=jnp.float32)
    bound = jnp.max(jnp.sum(jnp.abs(matrix), axis=1)) + 1e-6
    iterate = (matrix / bound).astype(jnp.bfloat16)
    for iteration in range(ITERS - 1):
        squared = jnp.dot(iterate, iterate, preferred_element_type=jnp.float32)
        factor = (1.5 * identity - 0.5 * squared).astype(jnp.bfloat16)
        iterate = jnp.dot(iterate, factor, preferred_element_type=jnp.float32).astype(jnp.bfloat16)
    squared = jnp.dot(iterate, iterate[:, :CENTRAL], preferred_element_type=jnp.float32)
    factor = (1.5 * identity[:, :CENTRAL] - 0.5 * squared).astype(jnp.bfloat16)
    last_product = jnp.dot(iterate, factor, preferred_element_type=jnp.float32)
    return (0.5 * (identity[:, :CENTRAL] - last_product)).astype(jnp.bfloat16)


def collocate(density, basis_rows):
    weights = lax.dot_general(density, basis_rows, (((0,), (0,)), ((), ())), preferred_element_type=jnp.float32)
    values = jnp.sum(weights * basis_rows[:CENTRAL].astype(jnp.float32), axis=0)
    return values.reshape(BOXP, BOX_ROWS, BOX_COLS)


def reference(column_blocks, onsite, neighbor_ids, task_atoms, chem_shift, basis_values, box_start, box_row, box_col):
    def one_task(members):
        atom_ids, offset, basis_rows = members
        matrix = assemble(column_blocks[atom_ids], onsite[atom_ids], neighbor_ids[atom_ids], atom_ids, offset)
        density = sign_columns(matrix)
        return density, collocate(density, basis_rows)

    density_cols, boxes = lax.map(one_task, (task_atoms, chem_shift, basis_values))

    def add_box(index, grid_now):
        corner = (box_start[index].astype(jnp.int32), box_row[index].astype(jnp.int32), box_col[index].astype(jnp.int32))
        current = lax.dynamic_slice(grid_now, corner, (BOXP, BOX_ROWS, BOX_COLS))
        return lax.dynamic_update_slice(grid_now, current + boxes[index], corner)

    empty_grid = jnp.zeros((PL_SLAB * N_GRID, GRID_ROWS, GRID_COLS), jnp.float32)
    rho = lax.fori_loop(0, TASKS, add_box, empty_grid)
    return density_cols, rho
```

```python
import jax, jax.numpy as jnp
from jax import lax
from jax.experimental import pallas as pl
from jax.experimental.pallas import tpu as pltpu
from jax.sharding import Mesh
from jax.sharding import PartitionSpec as P

F32, BF16, I32 = jnp.float32, jnp.bfloat16, jnp.int32
BS, KNB, NNB, ORDER, CENTRAL, POINTS, ITERS = 16, 32, 32, 512, 128, 1024, 3


def iota(shape, dim):
    return lax.broadcasted_iota(I32, shape, dim)


def fill_constants(perm, spread):
    rows, cols = iota((ORDER, ORDER), 0), iota((ORDER, ORDER), 1)
    hit = (rows // BS == cols % NNB) & (rows % BS == cols // NNB)
    perm[...] = hit.astype(F32).astype(BF16)
    point, lane = iota((POINTS, 128), 0), iota((POINTS, 128), 1)
    spread[...] = (lane == 64 * (point // 512) + point % 16).astype(F32).astype(BF16)


def task_density(atoms, shift, blocks, onsite, ids, perm, mixed, work):
    lane = iota((NNB, 128), 1)
    row32 = iota((NNB, 256), 0)
    for g in range(4):
        picks = []
        for jj in range(8):
            j = 8 * g + jj
            hit = (ids[j : j + 1, :] == atoms) & (lane // KNB == jj % 4)
            hit = hit.astype(F32)
            none = jnp.zeros((NNB, 128), F32)
            picks.append(jnp.concatenate([hit, none] if jj < 4 else [none, hit], axis=1))
        pick = jnp.concatenate(picks, axis=0).astype(BF16)
        found = jnp.dot(pick, blocks(g), preferred_element_type=F32)
        parts = []
        for jj in range(8):
            j = 8 * g + jj
            part = found[NNB * jj : NNB * (jj + 1)]
            parts.append(part + jnp.where(row32 == j, onsite[j : j + 1, :].astype(F32), 0.0))
        for half in range(2):
            tiles = [p[:, 128 * half : 128 * (half + 1)] for p in parts]
            for step in (1, 2, 4):
                low = (lane // (BS * step)) % 2 == 0
                fresh = list(tiles)
                for p in range(8):
                    if p & step:
                        continue
                    q = p + step
                    fresh[p] = jnp.where(low, tiles[p], pltpu.roll(tiles[q], BS * step, 1))
                    fresh[q] = jnp.where(low, pltpu.roll(tiles[p], 128 - BS * step, 1), tiles[q])
                tiles = fresh
            for a in range(8):
                mixed[pl.ds((8 * half + a) * NNB, NNB), pl.ds(128 * g, 128)] = tiles[a].astype(BF16)
    whole = jnp.dot(perm[...], mixed[...], preferred_element_type=F32)
    eye = (iota((ORDER, ORDER), 0) == iota((ORDER, ORDER), 1))
    matrix = 0.5 * (whole + whole.T) - jnp.where(eye, shift, 0.0)
    bound = jnp.max(jnp.sum(jnp.abs(matrix), axis=0, keepdims=True), axis=1, keepdims=True) + 1e-6
    work[...] = (matrix * (1.0 / bound)).astype(BF16)

    def step(_, carry):
        x = work[...]
        squared = jnp.dot(x, x, preferred_element_type=F32)
        diag = iota((ORDER, ORDER), 0) == iota((ORDER, ORDER), 1)
        factor = (jnp.where(diag, 1.5, 0.0) - 0.5 * squared).astype(BF16)
        work[...] = jnp.dot(x, factor, preferred_element_type=F32).astype(BF16)
        return carry

    lax.fori_loop(0, ITERS - 1, step, 0)
    x = work[...]
    narrow = iota((ORDER, CENTRAL), 0) == iota((ORDER, CENTRAL), 1)
    squared = jnp.dot(x, x[:, :CENTRAL], preferred_element_type=F32)
    factor = (jnp.where(narrow, 1.5, 0.0) - 0.5 * squared).astype(BF16)
    last = jnp.dot(x, factor, preferred_element_type=F32)
    return (0.5 * (jnp.where(narrow, 1.0, 0.0) - last)).astype(BF16)


def task_box(density, basis, spread):
    weights = lax.dot_general(density, basis[...], (((0,), (0,)), ((), ())), preferred_element_type=F32)
    values = jnp.sum(weights * basis[:CENTRAL].astype(F32), axis=0, keepdims=True)
    values = values.astype(BF16).astype(F32)
    rows, points = iota((32, POINTS), 0), iota((32, POINTS), 1)
    laid = jnp.where((points // 16) % 32 == rows, values, 0.0).astype(BF16)
    return jnp.dot(laid, spread[...], preferred_element_type=F32)


def compute_kernel(shift_ref, atoms_ref, blocks_ref, onsite_ref, hi_ref, lo_ref, basis_ref, dens_ref, box_ref, perm, spread, mixed, work, total):
    t = pl.program_id(0)

    @pl.when(t == 0)
    def _():
        fill_constants(perm, spread)
        total[...] = jnp.zeros_like(total)

    ids = hi_ref[...].astype(F32) * 32.0 + lo_ref[...].astype(F32)
    density = task_density(
        atoms_ref[0], shift_ref[t],
        lambda g: blocks_ref[pl.ds(8 * g, 8)].reshape(256, 256),
        onsite_ref, ids, perm, mixed, work)
    dens_ref[0] = density
    placed = task_box(density, basis_ref.at[0], spread)
    total[...] += pltpu.roll(placed, 16 * t, 1)

    @pl.when(t == pl.num_programs(0) - 1)
    def _():
        box_ref[...] = total[...].astype(BF16)


def compute(shift, atoms, blocks, onsite, hi, lo, basis):
    tasks = atoms.shape[0]
    return pl.pallas_call(
        compute_kernel,
        grid=(tasks,),
        out_shape=(
            jax.ShapeDtypeStruct((tasks, ORDER, CENTRAL), BF16),
            jax.ShapeDtypeStruct((32, 128), BF16),
        ),
        in_specs=[
            pl.BlockSpec(memory_space=pltpu.SMEM),
            pl.BlockSpec((1, NNB, 128), lambda t: (t, 0, 0)),
            pl.BlockSpec((NNB, KNB, 256), lambda t: (t, 0, 0)),
            pl.BlockSpec((NNB, 256), lambda t: (t, 0)),
            pl.BlockSpec((NNB, 128), lambda t: (t, 0)),
            pl.BlockSpec((NNB, 128), lambda t: (t, 0)),
            pl.BlockSpec((1, ORDER, POINTS), lambda t: (t, 0, 0)),
        ],
        out_specs=(
            pl.BlockSpec((1, ORDER, CENTRAL), lambda t: (t, 0, 0)),
            pl.BlockSpec((32, 128), lambda t: (0, 0)),
        ),
        scratch_shapes=[
            pltpu.VMEM((ORDER, ORDER), BF16),
            pltpu.VMEM((POINTS, 128), BF16),
            pltpu.VMEM((ORDER, ORDER), BF16),
            pltpu.VMEM((ORDER, ORDER), BF16),
            pltpu.VMEM((32, 128), F32),
        ],
        compiler_params=pltpu.CompilerParams(vmem_limit_bytes=50 << 20),
    )(shift, atoms, blocks, onsite, hi, lo, basis)


AXES = ("atoms_0", "atoms_1", "atoms_2", "grid")


def linear_place():
    y, x, c, z = (lax.axis_index(a) for a in AXES)
    return ((y * 4 + x) * 2 + c) * 4 + z


def place_of(p):
    return (p // 32, (p // 8) % 4, (p // 4) % 2, p % 4)


def share_kernel(box_ref, where_ref, boxes_ref, wheres_ref, send_a, recv_a, send_b, recv_b):
    me = linear_place()
    count = boxes_ref.shape[0]
    barrier = pltpu.get_barrier_semaphore()

    def greet(d, carry):
        pl.semaphore_signal(barrier, inc=1, device_id=place_of((me + d) % count), device_id_type=pl.DeviceIdType.MESH)
        return carry

    lax.fori_loop(1, count, greet, 0)
    pl.semaphore_wait(barrier, count - 1)

    def send(d, carry):
        peer = place_of((me + d) % count)
        pltpu.make_async_remote_copy(box_ref, boxes_ref.at[me], send_a, recv_a, device_id=peer, device_id_type=pl.DeviceIdType.MESH).start()
        pltpu.make_async_remote_copy(where_ref, wheres_ref.at[me], send_b, recv_b, device_id=peer, device_id_type=pl.DeviceIdType.MESH).start()
        return carry

    lax.fori_loop(1, count, send, 0)
    boxes_ref[me] = box_ref[...]
    wheres_ref[me] = where_ref[...]
    others = pl.ds(0, count - 1)
    for sem in (send_a, recv_a):
        pltpu.make_async_copy(boxes_ref.at[others], boxes_ref.at[others], sem).wait()
    for sem in (send_b, recv_b):
        pltpu.make_async_copy(wheres_ref.at[others], wheres_ref.at[others], sem).wait()


def share(box, where, count):
    vmem = pl.BlockSpec(memory_space=pltpu.VMEM)
    return pl.pallas_call(
        share_kernel,
        out_shape=(
            jax.ShapeDtypeStruct((count, *box.shape), box.dtype),
            jax.ShapeDtypeStruct((count, *where.shape), where.dtype),
        ),
        in_specs=[vmem, vmem],
        out_specs=(vmem, vmem),
        scratch_shapes=[pltpu.SemaphoreType.DMA] * 4,
        compiler_params=pltpu.CompilerParams(collective_id=1, has_side_effects=True),
    )(box, where)


def add_kernel(where_ref, boxes_ref, out_ref, picked, grid, sem):
    slab = lax.axis_index("grid")
    first = slab * 64 - 3
    count = boxes_ref.shape[0] * 4
    grid[...] = jnp.zeros_like(grid)

    def note(b, found):
        start = where_ref[b // 4, 0, b % 4] - first
        picked[found] = b
        return found + ((start >= 0) & (start < 67)).astype(I32)

    found = lax.fori_loop(0, count, note, 0, unroll=8)
    lane = iota((32, 128), 1)

    def add(n, carry):
        b = picked[n]
        who, t = b // 4, b % 4
        start = where_ref[who, 0, t] - first
        row = where_ref[who, 0, t + 4]
        col = where_ref[who, 0, t + 8]
        box = boxes_ref[who].astype(F32)
        inside = (lane >= col) & (lane < col + 16)
        for h in range(2):
            moved = pltpu.roll(box, (col + 128 - 64 * h - 16 * t) % 128, 1)
            moved = jnp.where(inside, moved, 0.0)
            for k in range(2):
                grid[start + 2 * h + k, pl.ds(row, 16), :] += moved[16 * k : 16 * (k + 1)]
        return carry

    lax.fori_loop(0, found, add, 0)
    copy = pltpu.make_async_copy(grid.at[pl.ds(3, 64)], out_ref, sem)
    copy.start()
    copy.wait()


def add_boxes(wheres, boxes):
    return pl.pallas_call(
        add_kernel,
        out_shape=jax.ShapeDtypeStruct((64, 32, 128), F32),
        in_specs=[pl.BlockSpec(memory_space=pltpu.SMEM), pl.BlockSpec(memory_space=pltpu.VMEM)],
        out_specs=pl.BlockSpec(memory_space=pl.ANY),
        scratch_shapes=[
            pltpu.SMEM((boxes.shape[0] * 4 + 1,), I32),
            pltpu.VMEM((70, 32, 128), F32),
            pltpu.SemaphoreType.DMA,
        ],
    )(wheres, boxes)


def on_device(column_blocks, onsite, neighbor_ids, task_atoms, chem_shift, basis_values, box_start, box_row, box_col):
    ids = jnp.tile(neighbor_ids, (1, 4))
    mine = jnp.concatenate(
        [column_blocks.reshape(32, -1), onsite, (ids // 32).astype(BF16), (ids % 32).astype(BF16)], axis=1
    )
    everyone = lax.all_gather(mine, AXES[:3], axis=0, tiled=True)
    chosen = task_atoms.reshape(-1)[:, None] == jnp.arange(everyone.shape[0], dtype=I32)[None, :]
    got = jnp.dot(chosen.astype(BF16), everyone, preferred_element_type=F32).astype(BF16)
    blocks = got[:, :8192].reshape(128, 32, 256)
    atoms = jnp.broadcast_to(task_atoms.astype(F32)[:, :, None], (*task_atoms.shape, 128))
    density, box = compute(chem_shift, atoms, blocks, got[:, 8192:8448], got[:, 8448:8576], got[:, 8576:], basis_values)
    where = jnp.concatenate([box_start, box_row, box_col])
    where = jnp.pad(where, (0, 128 - where.shape[0]))[None, :]
    boxes, wheres = share(box, where, 128)
    return density, add_boxes(wheres, boxes)


def solution(mesh):
    torus = Mesh(mesh.devices.reshape(4, 4, 2, mesh.shape["grid"]), AXES)
    atoms, both = P(AXES[:3]), P(AXES)
    return jax.shard_map(
        on_device,
        mesh=torus,
        in_specs=(atoms, atoms, atoms, both, both, both, both, both, both),
        out_specs=(both, P("grid")),
        check_vma=False,
    )
```

```python
import jax, jax.numpy as jnp
from jax import lax
from jax.experimental import pallas as pl
from jax.experimental.pallas import tpu as pltpu
from jax.sharding import Mesh
from jax.sharding import PartitionSpec as P

F32, BF16, I32 = jnp.float32, jnp.bfloat16, jnp.int32
BS, KNB, NNB, ORDER, CENTRAL, POINTS, ITERS = 16, 32, 32, 512, 128, 1024, 3


def iota(shape, dim):
    return lax.broadcasted_iota(I32, shape, dim)


def fill_constants(perm, spread):
    rows, cols = iota((ORDER, ORDER), 0), iota((ORDER, ORDER), 1)
    hit = (rows // BS == cols % NNB) & (rows % BS == cols // NNB)
    perm[...] = hit.astype(F32).astype(BF16)
    point, lane = iota((POINTS, 128), 0), iota((POINTS, 128), 1)
    spread[...] = (lane == 64 * (point // 512) + point % 16).astype(F32).astype(BF16)


def task_density(atoms, shift, blocks, onsite, ids, perm, mixed, work):
    lane = iota((NNB, 128), 1)
    row32 = iota((NNB, 256), 0)
    for g in range(4):
        picks = []
        for jj in range(8):
            j = 8 * g + jj
            hit = (ids[j : j + 1, :] == atoms) & (lane // KNB == jj % 4)
            hit = hit.astype(F32)
            none = jnp.zeros((NNB, 128), F32)
            picks.append(jnp.concatenate([hit, none] if jj < 4 else [none, hit], axis=1))
        pick = jnp.concatenate(picks, axis=0).astype(BF16)
        found = jnp.dot(pick, blocks(g), preferred_element_type=F32)
        parts = []
        for jj in range(8):
            j = 8 * g + jj
            part = found[NNB * jj : NNB * (jj + 1)]
            parts.append(part + jnp.where(row32 == j, onsite[j : j + 1, :].astype(F32), 0.0))
        for half in range(2):
            tiles = [p[:, 128 * half : 128 * (half + 1)] for p in parts]
            for step in (1, 2, 4):
                low = (lane // (BS * step)) % 2 == 0
                fresh = list(tiles)
                for p in range(8):
                    if p & step:
                        continue
                    q = p + step
                    fresh[p] = jnp.where(low, tiles[p], pltpu.roll(tiles[q], BS * step, 1))
                    fresh[q] = jnp.where(low, pltpu.roll(tiles[p], 128 - BS * step, 1), tiles[q])
                tiles = fresh
            for a in range(8):
                mixed[pl.ds((8 * half + a) * NNB, NNB), pl.ds(128 * g, 128)] = tiles[a].astype(BF16)
    whole = jnp.dot(perm[...], mixed[...], preferred_element_type=F32)
    eye = (iota((ORDER, ORDER), 0) == iota((ORDER, ORDER), 1))
    matrix = 0.5 * (whole + whole.T) - jnp.where(eye, shift, 0.0)
    bound = jnp.max(jnp.sum(jnp.abs(matrix), axis=0, keepdims=True), axis=1, keepdims=True) + 1e-6
    work[...] = (matrix * (1.0 / bound)).astype(BF16)

    def step(_, carry):
        x = work[...]
        squared = jnp.dot(x, x, preferred_element_type=F32)
        diag = iota((ORDER, ORDER), 0) == iota((ORDER, ORDER), 1)
        factor = (jnp.where(diag, 1.5, 0.0) - 0.5 * squared).astype(BF16)
        work[...] = jnp.dot(x, factor, preferred_element_type=F32).astype(BF16)
        return carry

    lax.fori_loop(0, ITERS - 1, step, 0)
    x = work[...]
    narrow = iota((ORDER, CENTRAL), 0) == iota((ORDER, CENTRAL), 1)
    squared = jnp.dot(x, x[:, :CENTRAL], preferred_element_type=F32)
    factor = (jnp.where(narrow, 1.5, 0.0) - 0.5 * squared).astype(BF16)
    last = jnp.dot(x, factor, preferred_element_type=F32)
    return (0.5 * (jnp.where(narrow, 1.0, 0.0) - last)).astype(BF16)


def task_box(density, basis, spread):
    weights = lax.dot_general(density, basis[...], (((0,), (0,)), ((), ())), preferred_element_type=F32)
    values = jnp.sum(weights * basis[:CENTRAL].astype(F32), axis=0, keepdims=True)
    values = values.astype(BF16).astype(F32)
    rows, points = iota((32, POINTS), 0), iota((32, POINTS), 1)
    laid = jnp.where((points // 16) % 32 == rows, values, 0.0).astype(BF16)
    return jnp.dot(laid, spread[...], preferred_element_type=F32)


def compute_kernel(shift_ref, atoms_ref, got_ref, gots_ref, basis_ref, dens_ref, box_ref, perm, spread, mixed, work, total):
    t = pl.program_id(0)

    @pl.when(t == 0)
    def _():
        fill_constants(perm, spread)
        total[...] = jnp.zeros_like(total)

    def small(h, c):
        return jnp.concatenate([gots_ref[h, c, half, 0] for half in range(2)], axis=0)

    def blocks(g):
        half, first = g // 2, 8 * (g % 2)
        tiles = [
            jnp.concatenate([got_ref[h, c, half, 0, first + j] for c in range(2)], axis=1)
            for j in range(8)
            for h in range(2)
        ]
        return jnp.concatenate(tiles, axis=0)

    onsite = jnp.concatenate([small(0, 0), small(0, 1)], axis=1)
    ids = small(1, 0).astype(F32) * 32.0 + small(1, 1).astype(F32)
    density = task_density(atoms_ref[0], shift_ref[t], blocks, onsite, ids, perm, mixed, work)
    dens_ref[0] = density
    placed = task_box(density, basis_ref.at[0], spread)
    total[...] += pltpu.roll(placed, 16 * t, 1)

    @pl.when(t == pl.num_programs(0) - 1)
    def _():
        box_ref[...] = total[...].astype(BF16)


def compute(shift, atoms, got, gots, basis):
    tasks = atoms.shape[0]
    return pl.pallas_call(
        compute_kernel,
        grid=(tasks,),
        out_shape=(
            jax.ShapeDtypeStruct((tasks, ORDER, CENTRAL), BF16),
            jax.ShapeDtypeStruct((32, 128), BF16),
        ),
        in_specs=[
            pl.BlockSpec(memory_space=pltpu.SMEM),
            pl.BlockSpec((1, NNB, 128), lambda t: (t, 0, 0)),
            pl.BlockSpec((2, 2, 2, 1, 16, 16, 128), lambda t: (0, 0, 0, t, 0, 0, 0)),
            pl.BlockSpec((2, 2, 2, 1, 16, 128), lambda t: (0, 0, 0, t, 0, 0)),
            pl.BlockSpec((1, ORDER, POINTS), lambda t: (t, 0, 0)),
        ],
        out_specs=(
            pl.BlockSpec((1, ORDER, CENTRAL), lambda t: (t, 0, 0)),
            pl.BlockSpec((32, 128), lambda t: (0, 0)),
        ),
        scratch_shapes=[
            pltpu.VMEM((ORDER, ORDER), BF16),
            pltpu.VMEM((POINTS, 128), BF16),
            pltpu.VMEM((ORDER, ORDER), BF16),
            pltpu.VMEM((ORDER, ORDER), BF16),
            pltpu.VMEM((32, 128), F32),
        ],
        compiler_params=pltpu.CompilerParams(vmem_limit_bytes=50 << 20),
    )(shift, atoms, got, gots, basis)


AXES = ("atoms_0", "atoms_1", "atoms_2", "grid")


def linear_place():
    y, x, c, z = (lax.axis_index(a) for a in AXES)
    return ((y * 4 + x) * 2 + c) * 4 + z


def place_of(p):
    return (p // 32, (p // 8) % 4, (p // 4) % 2, p % 4)


def share_kernel(box_ref, where_ref, boxes_ref, wheres_ref, send_a, recv_a, send_b, recv_b):
    me = linear_place()
    count = boxes_ref.shape[0]
    barrier = pltpu.get_barrier_semaphore()

    def greet(d, carry):
        pl.semaphore_signal(barrier, inc=1, device_id=place_of((me + d) % count), device_id_type=pl.DeviceIdType.MESH)
        return carry

    lax.fori_loop(1, count, greet, 0)
    pl.semaphore_wait(barrier, count - 1)

    def send(d, carry):
        peer = place_of((me + d) % count)
        pltpu.make_async_remote_copy(box_ref, boxes_ref.at[me], send_a, recv_a, device_id=peer, device_id_type=pl.DeviceIdType.MESH).start()
        pltpu.make_async_remote_copy(where_ref, wheres_ref.at[me], send_b, recv_b, device_id=peer, device_id_type=pl.DeviceIdType.MESH).start()
        return carry

    lax.fori_loop(1, count, send, 0)
    boxes_ref[me] = box_ref[...]
    wheres_ref[me] = where_ref[...]
    others = pl.ds(0, count - 1)
    for sem in (send_a, recv_a):
        pltpu.make_async_copy(boxes_ref.at[others], boxes_ref.at[others], sem).wait()
    for sem in (send_b, recv_b):
        pltpu.make_async_copy(wheres_ref.at[others], wheres_ref.at[others], sem).wait()


def share(box, where, count):
    vmem = pl.BlockSpec(memory_space=pltpu.VMEM)
    return pl.pallas_call(
        share_kernel,
        out_shape=(
            jax.ShapeDtypeStruct((count, *box.shape), box.dtype),
            jax.ShapeDtypeStruct((count, *where.shape), where.dtype),
        ),
        in_specs=[vmem, vmem],
        out_specs=(vmem, vmem),
        scratch_shapes=[pltpu.SemaphoreType.DMA] * 4,
        compiler_params=pltpu.CompilerParams(collective_id=1, has_side_effects=True),
    )(box, where)


def add_kernel(where_ref, boxes_ref, out_ref, picked, grid, sem):
    slab = lax.axis_index("grid")
    first = slab * 64 - 3
    count = boxes_ref.shape[0] * 4
    grid[...] = jnp.zeros_like(grid)

    def note(b, found):
        start = where_ref[b // 4, 0, b % 4] - first
        picked[found] = b
        return found + ((start >= 0) & (start < 67)).astype(I32)

    found = lax.fori_loop(0, count, note, 0, unroll=8)
    lane = iota((32, 128), 1)

    def add(n, carry):
        b = picked[n]
        who, t = b // 4, b % 4
        start = where_ref[who, 0, t] - first
        row = where_ref[who, 0, t + 4]
        col = where_ref[who, 0, t + 8]
        box = boxes_ref[who].astype(F32)
        inside = (lane >= col) & (lane < col + 16)
        for h in range(2):
            moved = pltpu.roll(box, (col + 128 - 64 * h - 16 * t) % 128, 1)
            moved = jnp.where(inside, moved, 0.0)
            for k in range(2):
                grid[start + 2 * h + k, pl.ds(row, 16), :] += moved[16 * k : 16 * (k + 1)]
        return carry

    lax.fori_loop(0, found, add, 0)
    copy = pltpu.make_async_copy(grid.at[pl.ds(3, 64)], out_ref, sem)
    copy.start()
    copy.wait()


def add_boxes(wheres, boxes):
    return pl.pallas_call(
        add_kernel,
        out_shape=jax.ShapeDtypeStruct((64, 32, 128), F32),
        in_specs=[pl.BlockSpec(memory_space=pltpu.SMEM), pl.BlockSpec(memory_space=pltpu.VMEM)],
        out_specs=pl.BlockSpec(memory_space=pl.ANY),
        scratch_shapes=[
            pltpu.SMEM((boxes.shape[0] * 4 + 1,), I32),
            pltpu.VMEM((70, 32, 128), F32),
            pltpu.SemaphoreType.DMA,
        ],
    )(wheres, boxes)


MESH = pl.DeviceIdType.MESH


def gather_kernel(blocks_ref, small_ref, atoms_ref, got_ref, gots_ref, held, flat, wants_v, wants_s, to_sib, to_z, rows_sib, rows_z,
                  own_sem, sib_send, send_sem, recv_sem, want_send, want_recv, move_sem, z_send, z_recv, zs_send, zs_recv):
    y, x, c, z = (lax.axis_index(a) for a in AXES)
    h, o = z % 2, 1 - c
    here = (y, x, c, z)
    sibling = (y, x, o, z)
    up, down = (z + 1) % 4, (z + 3) % 4
    z_peers = [(y, x, c, up), (y, x, o, up), (y, x, c, down), (y, x, o, down)]

    def ring(f, dp, dq):
        if f == 0:
            return ((y + dq) % 4, (x + dp) % 4, c, z)
        return ((y + dp) % 4, (x + dq) % 4, c, z)

    def unit(f, dp, dq, s):
        place = ring(f, dp, dq)
        return ((place[0] * 4 + place[1]) * 2 + s) * 2 + f

    barrier = pltpu.get_barrier_semaphore()
    peers = [ring(0, 1, 0), ring(0, 3, 0), ring(0, 0, 1), ring(0, 0, 3), sibling] + z_peers
    for peer in peers:
        pl.semaphore_signal(barrier, inc=1, device_id=peer, device_id_type=MESH)

    half_k = pl.ds(pl.multiple_of(16 * h, 16), 16)
    mine = pl.ds(pl.multiple_of(128 * c, 128), 128)
    theirs = pl.ds(pl.multiple_of(128 * o, 128), 128)
    for f in range(2):
        u = unit(f, 0, 0, c)
        pltpu.make_async_copy(blocks_ref.at[pl.ds(16 * f, 16), half_k, mine], held.at[u, pl.ds(0, 16)], own_sem.at[f]).start()
        pltpu.make_async_copy(small_ref.at[2 * h + c, f], held.at[u, 16], own_sem.at[f]).start()
    pl.semaphore_wait(barrier, len(peers))
    for f in range(2):
        u = unit(f, 0, 0, c)
        pltpu.make_async_remote_copy(blocks_ref.at[pl.ds(16 * f, 16), half_k, theirs], held.at[u, pl.ds(0, 16)], sib_send, recv_sem.at[u], device_id=sibling, device_id_type=MESH).start()
        pltpu.make_async_remote_copy(small_ref.at[2 * h + o, f], held.at[u, 16], sib_send, recv_sem.at[u], device_id=sibling, device_id_type=MESH).start()

    def send(f, u, dp, dq):
        pltpu.make_async_remote_copy(held.at[u], held.at[u], send_sem, recv_sem.at[u], device_id=ring(f, dp, dq), device_id_type=MESH).start()

    def arrived(u):
        pltpu.make_async_copy(held.at[u], held.at[u], recv_sem.at[u]).wait()

    def near(f, u):
        send(f, u, 1, 0)
        send(f, u, 3, 0)

    def far(f, u):
        send(f, u, 0, 1)
        send(f, u, 0, 3)

    for f in range(2):
        u = unit(f, 0, 0, c)
        pltpu.make_async_copy(held.at[u], held.at[u], own_sem.at[f]).wait()
        near(f, u)
    for f in range(2):
        u = unit(f, 0, 0, o)
        arrived(u)
        near(f, u)
    want_to = [z_peers[2], z_peers[3], z_peers[0], z_peers[1], sibling]
    for slot, peer in enumerate(want_to):
        pltpu.make_async_remote_copy(atoms_ref, wants_v.at[slot], want_send, want_recv, device_id=peer, device_id_type=MESH).start()
    for s in (c, o):
        for f in range(2):
            far(f, unit(f, 0, 0, s))

    def take_near(first):
        s = c if first else o
        for f in range(2):
            u = unit(f, 3, 0, s)
            arrived(u)
            if first:
                send(f, u, 1, 0)
            far(f, u)
            u = unit(f, 1, 0, s)
            arrived(u)
            if not first:
                send(f, u, 3, 0)
            far(f, u)

    def take_far(dp, first):
        s = c if first else o
        for f in range(2):
            u = unit(f, dp, 3, s)
            arrived(u)
            if first:
                send(f, u, 0, 1)
            u = unit(f, dp, 1, s)
            arrived(u)
            if not first:
                send(f, u, 0, 3)

    take_near(True)
    take_near(False)
    take_far(0, True)
    take_far(0, False)
    for s in (c, o):
        for f in range(2):
            u = unit(f, 2, 0, s)
            arrived(u)
            far(f, u)
    for dp in (3, 1, 2):
        take_far(dp, True)
        take_far(dp, False)
    for dp in range(4):
        for f in range(2):
            for s in (c, o):
                arrived(unit(f, dp, 2, s))

    others = pl.ds(0, 5)
    pltpu.make_async_copy(wants_v.at[others], wants_v.at[others], want_recv).wait()
    moved = pltpu.make_async_copy(wants_v.at[others], wants_s.at[others], move_sem.at[0])
    moved.start()
    own = pltpu.make_async_copy(atoms_ref, wants_s.at[5], move_sem.at[1])
    own.start()

    for u in range(64):
        flat[pl.ds(16 * u, 16), :] = held[u, 16].astype(F32)
    moved.wait()
    own.wait()

    def pick(slot, t, j):
        atom = wants_s[slot, t, j]
        return held[atom // 16, atom % 16]

    rows_f = pl.ds(0, 8)
    for t in range(4):
        for i in range(4):
            base = 16 * (i // 2)

            def one(r, carry, i=i, t=t, base=base):
                to_z[i, 16 * t + r] = pick(i, t, base + r)
                return carry

            lax.fori_loop(0, 16, one, 0, unroll=16)
            pltpu.make_async_remote_copy(to_z.at[i, pl.ds(16 * t, 16)], got_ref.at[h, c, pl.ds(64 * (i // 2) + 16 * t, 16)], z_send, z_recv.at[i, t], device_id=z_peers[i], device_id_type=MESH).start()
    for half in range(2):
        for t in range(4):
            def two(r, carry, t=t, half=half):
                at = 64 * half + 16 * t + r
                to_sib[at] = pick(4, t, 16 * half + r)
                got_ref[h, c, at] = pick(5, t, 16 * half + r)
                return carry

            lax.fori_loop(0, 16, two, 0, unroll=16)
    pltpu.make_async_remote_copy(to_sib, got_ref.at[h, c], zs_send.at[0], z_recv.at[4, 0], device_id=sibling, device_id_type=MESH).start()

    def line(slot, t, j):
        atom = wants_s[slot, t, j]
        return flat[pl.ds(atom, 1), :]

    for i in range(4):
        for t in range(4):
            for_rows = [line(i, t, 16 * (i // 2) + r) for r in range(16)]
            rows_z[i, pl.ds(16 * t, 16), :] = jnp.concatenate(for_rows, axis=0).astype(BF16)
        pltpu.make_async_remote_copy(rows_z.at[i], gots_ref.at[h, c, pl.ds(64 * (i // 2), 64)], zs_send.at[1], zs_recv.at[i], device_id=z_peers[i], device_id_type=MESH).start()
    for half in range(2):
        for t in range(4):
            at = pl.ds(64 * half + 16 * t, 16)
            for_rows = [line(4, t, 16 * half + r) for r in range(16)]
            rows_sib[at, :] = jnp.concatenate(for_rows, axis=0).astype(BF16)
            for_rows = [line(5, t, 16 * half + r) for r in range(16)]
            gots_ref[h, c, at, :] = jnp.concatenate(for_rows, axis=0).astype(BF16)
    pltpu.make_async_remote_copy(rows_sib, gots_ref.at[h, c], zs_send.at[2], zs_recv.at[4], device_id=sibling, device_id_type=MESH).start()

    def done(ref, sem):
        pltpu.make_async_copy(ref, ref, sem).wait()

    for i in range(4):
        core = c if i % 2 == 0 else o
        part = pl.ds(64 * (i // 2), 64)
        for t in range(4):
            done(got_ref.at[1 - h, core, pl.ds(64 * (i // 2) + 16 * t, 16)], z_recv.at[i, t])
        done(gots_ref.at[1 - h, core, part], zs_recv.at[i])
    done(got_ref.at[h, o], z_recv.at[4, 0])
    done(gots_ref.at[h, o], zs_recv.at[4])
    done(held.at[pl.ds(0, 2)], sib_send)
    done(held.at[pl.ds(0, 60)], send_sem)
    done(wants_v.at[others], want_send)
    done(to_z, z_send)
    done(to_sib, zs_send.at[0])
    done(rows_z, zs_send.at[1])
    done(rows_sib, zs_send.at[2])


def gather(blocks, small, atoms):
    any_space = pl.BlockSpec(memory_space=pl.ANY)
    vmem = pl.BlockSpec(memory_space=pltpu.VMEM)
    dma = pltpu.SemaphoreType.DMA
    return pl.pallas_call(
        gather_kernel,
        out_shape=(
            jax.ShapeDtypeStruct((2, 2, 128, 16, 128), BF16),
            jax.ShapeDtypeStruct((2, 2, 128, 128), BF16),
        ),
        in_specs=[any_space, any_space, vmem],
        out_specs=(vmem, vmem),
        scratch_shapes=[
            pltpu.VMEM((64, 17, 16, 128), BF16),
            pltpu.VMEM((1024, 128), F32),
            pltpu.VMEM((5, 4, 32), I32),
            pltpu.SMEM((6, 4, 32), I32),
            pltpu.VMEM((128, 16, 128), BF16),
            pltpu.VMEM((4, 64, 16, 128), BF16),
            pltpu.VMEM((128, 128), BF16),
            pltpu.VMEM((4, 64, 128), BF16),
            dma((2,)), dma, dma, dma((64,)), dma, dma, dma((2,)), dma, dma((5, 4)), dma((3,)), dma((5,)),
        ],
        compiler_params=pltpu.CompilerParams(collective_id=0, has_side_effects=True, vmem_limit_bytes=50 << 20),
    )(blocks, small, atoms)


def small_rows(onsite, neighbor_ids):
    ids = jnp.tile(neighbor_ids, (1, 4))
    pieces = jnp.stack([onsite[:, :128], onsite[:, 128:], (ids // 32).astype(BF16), (ids % 32).astype(BF16)])
    return pieces.reshape(4, 2, 16, 128)


def on_device(column_blocks, onsite, neighbor_ids, task_atoms, chem_shift, basis_values, box_start, box_row, box_col):
    got, gots = gather(column_blocks, small_rows(onsite, neighbor_ids), task_atoms)
    got = got.reshape(2, 2, 2, 4, 16, 16, 128)
    gots = gots.reshape(2, 2, 2, 4, 16, 128)
    atoms = jnp.broadcast_to(task_atoms.astype(F32)[:, :, None], (*task_atoms.shape, 128))
    density, box = compute(chem_shift, atoms, got, gots, basis_values)
    where = jnp.concatenate([box_start, box_row, box_col])
    where = jnp.pad(where, (0, 128 - where.shape[0]))[None, :]
    boxes, wheres = share(box, where, 128)
    return density, add_boxes(wheres, boxes)


def solution(mesh):
    torus = Mesh(mesh.devices.reshape(4, 4, 2, mesh.shape["grid"]), AXES)
    atoms, both = P(AXES[:3]), P(AXES)
    return jax.shard_map(
        on_device,
        mesh=torus,
        in_specs=(atoms, atoms, atoms, both, both, both, both, both, both),
        out_specs=(both, P("grid")),
        check_vma=False,
    )
```

```python
import jax
import jax.numpy as jnp
from jax import lax
from jax.experimental import pallas as pl
from jax.experimental.pallas import tpu as pltpu
from jax.sharding import Mesh
from jax.sharding import PartitionSpec as P

F32, BF16, I32 = jnp.float32, jnp.bfloat16, jnp.int32
BS, KNB, NNB, ORDER, CENTRAL, POINTS, ITERS = 16, 32, 32, 512, 128, 1024, 3
SLAB, ROWS, COLS = 64, 32, 128
DEVICES, TASKS = 128, 4
AXES = ("atoms_0", "atoms_1", "atoms_2", "grid")
MESH = pl.DeviceIdType.MESH


def iota(shape, dim):
    return lax.broadcasted_iota(I32, shape, dim)


def fill_constants(perm):
    rows, cols = iota((ORDER, ORDER), 0), iota((ORDER, ORDER), 1)
    hit = (rows // BS == cols % NNB) & (rows % BS == cols // NNB)
    perm[...] = hit.astype(F32).astype(BF16)


def task_density(atoms, shift, blocks, onsite, ids, perm, mixed, work):
    lane = iota((NNB, 128), 1)
    row32 = iota((NNB, 256), 0)
    for g in range(4):
        picks = []
        for jj in range(8):
            j = 8 * g + jj
            hit = (ids[j : j + 1, :] == atoms) & (lane // KNB == jj % 4)
            hit = hit.astype(F32)
            none = jnp.zeros((NNB, 128), F32)
            picks.append(jnp.concatenate([hit, none] if jj < 4 else [none, hit], axis=1))
        pick = jnp.concatenate(picks, axis=0).astype(BF16)
        found = jnp.dot(pick, blocks(g), preferred_element_type=F32)
        parts = []
        for jj in range(8):
            j = 8 * g + jj
            part = found[NNB * jj : NNB * (jj + 1)]
            parts.append(part + jnp.where(row32 == j, onsite[j : j + 1, :].astype(F32), 0.0))
        for half in range(2):
            tiles = [p[:, 128 * half : 128 * (half + 1)] for p in parts]
            for step in (1, 2, 4):
                low = (lane // (BS * step)) % 2 == 0
                fresh = list(tiles)
                for p in range(8):
                    if p & step:
                        continue
                    q = p + step
                    fresh[p] = jnp.where(low, tiles[p], pltpu.roll(tiles[q], BS * step, 1))
                    fresh[q] = jnp.where(low, pltpu.roll(tiles[p], 128 - BS * step, 1), tiles[q])
                tiles = fresh
            for a in range(8):
                mixed[pl.ds((8 * half + a) * NNB, NNB), pl.ds(128 * g, 128)] = tiles[a].astype(BF16)
    whole = jnp.dot(perm[...], mixed[...], preferred_element_type=F32)
    eye = iota((ORDER, ORDER), 0) == iota((ORDER, ORDER), 1)
    matrix = 0.5 * (whole + whole.T) - jnp.where(eye, shift, 0.0)
    bound = jnp.max(jnp.sum(jnp.abs(matrix), axis=0, keepdims=True), axis=1, keepdims=True) + 1e-6
    work[...] = (matrix * (1.0 / bound)).astype(BF16)

    def step(_, carry):
        x = work[...]
        squared = jnp.dot(x, x, preferred_element_type=F32)
        diag = iota((ORDER, ORDER), 0) == iota((ORDER, ORDER), 1)
        factor = (jnp.where(diag, 1.5, 0.0) - 0.5 * squared).astype(BF16)
        work[...] = jnp.dot(x, factor, preferred_element_type=F32).astype(BF16)
        return carry

    lax.fori_loop(0, ITERS - 1, step, 0)
    x = work[...]
    narrow = iota((ORDER, CENTRAL), 0) == iota((ORDER, CENTRAL), 1)
    squared = jnp.dot(x, x[:, :CENTRAL], preferred_element_type=F32)
    factor = (jnp.where(narrow, 1.5, 0.0) - 0.5 * squared).astype(BF16)
    last = jnp.dot(x, factor, preferred_element_type=F32)
    return (0.5 * (jnp.where(narrow, 1.0, 0.0) - last)).astype(BF16)


def task_box(density, basis):
    weights = lax.dot_general(density, basis[...], (((0,), (0,)), ((), ())), preferred_element_type=F32)
    values = jnp.sum(weights * basis[:CENTRAL].astype(F32), axis=0, keepdims=True)
    box = jnp.concatenate([values[:, 128 * l : 128 * (l + 1)] for l in range(8)], axis=0)
    row, lane = iota((8, 128), 0), iota((8, 128), 1)
    for step in (1, 2, 4):
        high_row, high_lane = (row // step) % 2 == 1, (lane // (BS * step)) % 2 == 1
        from_below = pltpu.roll(pltpu.roll(box, 8 - step, 0), BS * step, 1)
        from_above = pltpu.roll(pltpu.roll(box, step, 0), 128 - BS * step, 1)
        crossed = jnp.where(high_row, from_above, from_below)
        box = jnp.where(high_row == high_lane, box, crossed)
    return box.astype(BF16)


def slab_list(wheres, first):
    rows = wheres[...].astype(F32)
    lane = iota((DEVICES, 128), 1)
    start = rows - first
    hit = ((start >= 0) & (start < SLAB + 3) & (lane < TASKS)).astype(F32)
    below = (iota((DEVICES, DEVICES), 1) < iota((DEVICES, DEVICES), 0)).astype(F32).astype(BF16)
    before = jnp.dot(below, hit.astype(BF16), preferred_element_type=F32)
    totals = jnp.sum(hit, axis=0, keepdims=True)
    turned = rows.T
    slots = iota((DEVICES, 512), 1).astype(F32)
    base = jnp.zeros((1, 1), F32)
    listed = jnp.zeros((8, 512), F32)
    line = iota((8, 128), 0)
    device = iota((8, 128), 1).astype(F32)
    for t in range(TASKS):
        chosen = (before[:, t : t + 1] + base == slots) & (hit[:, t : t + 1] > 0.5)
        values = jnp.where(line == 3, device, jnp.where(line == 4, float(t), 0.0))
        for v in range(3):
            values = jnp.where(line == v, turned[4 * v + t : 4 * v + t + 1, :], values)
        listed += jnp.dot(values.astype(BF16), chosen.astype(F32).astype(BF16), preferred_element_type=F32)
        base = base + totals[:, t : t + 1]
    row, slot = iota((8, 512), 0), iota((8, 512), 1).astype(F32)
    used = slot < base
    listed = jnp.where(row == 0, jnp.where(used, listed - first, SLAB + 6.0), listed)
    return jnp.where(row == 5, base, listed).astype(I32)


def main_kernel(blocks_ref, onsite_ref, ids_ref, atoms_ref, shift_ref, basis_ref, start_ref, row_ref, col_ref,
                dens_ref, boxes_ref, list_ref,
                held, flat, got, gots, to_sib, to_z, rows_f, rows_sib, rows_z, small, onsite_v, ids_v, atoms_v, basis_v,
                wants_v, wants_s, shift_s, where_s, where_v, wheres, own_box, perm, mixed, work,
                load_sem, basis_sem, own_sem, sib_send, send_sem, recv_sem, want_send, want_recv, move_sem, z_send, z_recv, zs_send, zs_recv,
                where_send, where_recv, box_send, box_recv):
    y, x, c, z = (lax.axis_index(a) for a in AXES)
    h, o = z % 2, 1 - c
    me = ((y * 4 + x) * 2 + c) * 4 + z
    sibling = (y, x, o, z)
    up, down = (z + 1) % 4, (z + 3) % 4
    z_peers = [(y, x, c, up), (y, x, o, up), (y, x, c, down), (y, x, o, down)]

    def ring(f, dp, dq):
        if f == 0:
            return ((y + dq) % 4, (x + dp) % 4, c, z)
        return ((y + dp) % 4, (x + dq) % 4, c, z)

    def unit(f, dp, dq, s):
        place = ring(f, dp, dq)
        return ((place[0] * 4 + place[1]) * 2 + s) * 2 + f

    def done(ref, sem):
        pltpu.make_async_copy(ref, ref, sem).wait()

    def for_others(act):
        def block(b, carry, skip=0):
            for d in range(skip, 8):
                act(((y + b // 4) % 4, (x + b % 4) % 4, (c + d // 4) % 2, (z + d % 4) % 4))
            return carry

        lax.fori_loop(1, 16, block, 0)
        block(0, 0, 1)

    barrier = pltpu.get_barrier_semaphore()
    for_others(lambda peer: pl.semaphore_signal(barrier, inc=1, device_id=peer, device_id_type=MESH))

    half_k = pl.ds(pl.multiple_of(16 * h, 16), 16)
    mine = pl.ds(pl.multiple_of(128 * c, 128), 128)
    theirs = pl.ds(pl.multiple_of(128 * o, 128), 128)
    loads = [
        pltpu.make_async_copy(onsite_ref, onsite_v, load_sem.at[0]),
        pltpu.make_async_copy(ids_ref, ids_v, load_sem.at[1]),
        pltpu.make_async_copy(atoms_ref, atoms_v, load_sem.at[2]),
        pltpu.make_async_copy(atoms_ref, wants_s.at[5], load_sem.at[3]),
        pltpu.make_async_copy(shift_ref, shift_s, load_sem.at[4]),
        pltpu.make_async_copy(start_ref, where_s.at[0], load_sem.at[5]),
        pltpu.make_async_copy(row_ref, where_s.at[1], load_sem.at[6]),
        pltpu.make_async_copy(col_ref, where_s.at[2], load_sem.at[7]),
    ]
    for load in loads:
        load.start()
    for f in range(2):
        u = unit(f, 0, 0, c)
        pltpu.make_async_copy(blocks_ref.at[pl.ds(16 * f, 16), half_k, mine], held.at[u, pl.ds(0, 16)], own_sem.at[f]).start()
    loads[0].wait()
    loads[1].wait()
    tiled = jnp.concatenate([ids_v[...]] * 4, axis=1)
    small[0] = onsite_v[:, :128].reshape(2, 16, 128)
    small[1] = onsite_v[:, 128:].reshape(2, 16, 128)
    small[2] = (tiled // 32).astype(F32).astype(BF16).reshape(2, 16, 128)
    small[3] = (tiled % 32).astype(F32).astype(BF16).reshape(2, 16, 128)
    for f in range(2):
        u = unit(f, 0, 0, c)
        pltpu.make_async_copy(small.at[2 * h + c, f], held.at[u, 16], own_sem.at[f]).start()
    pl.semaphore_wait(barrier, DEVICES - 1)
    for f in range(2):
        u = unit(f, 0, 0, c)
        pltpu.make_async_remote_copy(blocks_ref.at[pl.ds(16 * f, 16), half_k, theirs], held.at[u, pl.ds(0, 16)], sib_send, recv_sem.at[u], device_id=sibling, device_id_type=MESH).start()
        pltpu.make_async_remote_copy(small.at[2 * h + o, f], held.at[u, 16], sib_send, recv_sem.at[u], device_id=sibling, device_id_type=MESH).start()

    def send(f, u, dp, dq):
        pltpu.make_async_remote_copy(held.at[u], held.at[u], send_sem, recv_sem.at[u], device_id=ring(f, dp, dq), device_id_type=MESH).start()

    def arrived(u):
        done(held.at[u], recv_sem.at[u])

    def near(f, u):
        send(f, u, 1, 0)
        send(f, u, 3, 0)

    def far(f, u):
        send(f, u, 0, 1)
        send(f, u, 0, 3)

    for f in range(2):
        u = unit(f, 0, 0, c)
        done(held.at[u], own_sem.at[f])
        near(f, u)
    for f in range(2):
        u = unit(f, 0, 0, o)
        arrived(u)
        near(f, u)
    for s in (c, o):
        for f in range(2):
            far(f, unit(f, 0, 0, s))
    for load in loads[2:]:
        load.wait()
    for i in range(TASKS):
        pltpu.make_async_copy(basis_ref.at[i], basis_v.at[i], basis_sem.at[i]).start()
    want_to = [z_peers[2], z_peers[3], z_peers[0], z_peers[1], sibling]
    for slot, peer in enumerate(want_to):
        pltpu.make_async_remote_copy(atoms_v, wants_v.at[slot], want_send, want_recv, device_id=peer, device_id_type=MESH).start()
    lane1 = iota((1, 128), 1)
    where = jnp.zeros((1, 128), I32)
    for v in range(3):
        for t in range(TASKS):
            where = jnp.where(lane1 == 4 * v + t, where_s[v, t], where)
    where_v[...] = where
    wheres[pl.ds(me, 1), :] = where
    fill_constants(perm)

    def take_near(first):
        s = c if first else o
        for f in range(2):
            u = unit(f, 3, 0, s)
            arrived(u)
            if first:
                send(f, u, 1, 0)
            far(f, u)
            u = unit(f, 1, 0, s)
            arrived(u)
            if not first:
                send(f, u, 3, 0)
            far(f, u)

    def take_far(dp, first):
        s = c if first else o
        for f in range(2):
            u = unit(f, dp, 3, s)
            arrived(u)
            if first:
                send(f, u, 0, 1)
            u = unit(f, dp, 1, s)
            arrived(u)
            if not first:
                send(f, u, 0, 3)

    take_near(True)
    take_near(False)
    for_others(lambda peer: pltpu.make_async_remote_copy(where_v, wheres.at[pl.ds(me, 1)], where_send, where_recv, device_id=peer, device_id_type=MESH).start())
    take_far(0, True)
    take_far(0, False)
    for s in (c, o):
        for f in range(2):
            u = unit(f, 2, 0, s)
            arrived(u)
            far(f, u)
    for dp in (3, 1, 2):
        take_far(dp, True)
        take_far(dp, False)
    others = pl.ds(0, 5)
    done(wants_v.at[others], want_recv)
    moved = pltpu.make_async_copy(wants_v.at[others], wants_s.at[others], move_sem)
    moved.start()
    for dp in range(4):
        for f in range(2):
            for s in (c, o):
                arrived(unit(f, dp, 2, s))
    for u in range(64):
        flat[pl.ds(16 * u, 16), :] = held[u, 16].astype(F32)
    moved.wait()

    def pick(slot, t, j):
        atom = wants_s[slot, t, j]
        return held[atom // 16, atom % 16], flat[pl.ds(atom, 1), :]

    for t in range(TASKS):
        for i in range(4):
            part = i // 2

            def one(r, carry, i=i, t=t, part=part):
                to_z[i, 16 * t + r], rows_f[i, pl.ds(16 * t + r, 1), :] = pick(i, t, 16 * part + r)
                return carry

            lax.fori_loop(0, 16, one, 0, unroll=True)
            rows_z[i, pl.ds(16 * t, 16), :] = rows_f[i, pl.ds(16 * t, 16), :].astype(BF16)
            at = pl.ds(64 * part + 16 * t, 16)
            pltpu.make_async_remote_copy(to_z.at[i, pl.ds(16 * t, 16)], got.at[h, c, at], z_send, z_recv.at[i, t], device_id=z_peers[i], device_id_type=MESH).start()
            pltpu.make_async_remote_copy(rows_z.at[i, pl.ds(16 * t, 16)], gots.at[h, c, at], zs_send.at[1], zs_recv.at[i, t], device_id=z_peers[i], device_id_type=MESH).start()
    for t in range(TASKS):
        for part in range(2):
            first = 64 * part + 16 * t

            def two(r, carry, t=t, part=part, first=first):
                to_sib[first + r], rows_f[4, pl.ds(16 * part + r, 1), :] = pick(4, t, 16 * part + r)
                return carry

            def three(r, carry, t=t, part=part, first=first):
                got[h, c, first + r], rows_f[5, pl.ds(16 * part + r, 1), :] = pick(5, t, 16 * part + r)
                return carry

            lax.fori_loop(0, 16, two, 0, unroll=True)
            at = pl.ds(first, 16)
            rows_sib[at, :] = rows_f[4, pl.ds(16 * part, 16), :].astype(BF16)
            pltpu.make_async_remote_copy(to_sib.at[at], got.at[h, c, at], zs_send.at[0], z_recv.at[4, t], device_id=sibling, device_id_type=MESH).start()
            pltpu.make_async_remote_copy(rows_sib.at[at], gots.at[h, c, at], zs_send.at[2], zs_recv.at[4, t], device_id=sibling, device_id_type=MESH).start()
            lax.fori_loop(0, 16, three, 0, unroll=True)
            gots[h, c, at, :] = rows_f[5, pl.ds(16 * part, 16), :].astype(BF16)

    done(wheres.at[pl.ds(0, DEVICES - 1)], where_recv)
    list_ref[...] = slab_list(wheres, (z * SLAB - 3).astype(F32))

    def task(t, carry):
        for i in range(4):
            done(got.at[0, 0, pl.ds(0, 16)], z_recv.at[i, t])
            done(gots.at[0, 0, pl.ds(0, 16)], zs_recv.at[i, t])
        done(got.at[0, 0, pl.ds(0, 32)], z_recv.at[4, t])
        done(gots.at[0, 0, pl.ds(0, 32)], zs_recv.at[4, t])

        def rows(hh, cc):
            return jnp.concatenate([gots[hh, cc, pl.ds(pl.multiple_of(64 * part + 16 * t, 16), 16), :] for part in range(2)], axis=0)

        def blocks(g):
            first = 64 * (g // 2) + 16 * t + 8 * (g % 2)
            tiles = [
                jnp.concatenate([got[hh, cc, first + j] for cc in range(2)], axis=1)
                for j in range(8)
                for hh in range(2)
            ]
            return jnp.concatenate(tiles, axis=0)

        onsite = jnp.concatenate([rows(0, 0), rows(0, 1)], axis=1)
        ids = rows(1, 0).astype(F32) * 32.0 + rows(1, 1).astype(F32)
        eye = iota((NNB, NNB), 0) == iota((NNB, NNB), 1)
        atoms = jnp.sum(jnp.where(eye, atoms_v[pl.ds(t, 1), :].astype(F32), 0.0), axis=1, keepdims=True)
        density = task_density(atoms, shift_s[t], blocks, onsite, ids, perm, mixed, work)
        dens_ref[t] = density
        done(basis_v.at[0], basis_sem.at[t])
        box = task_box(density, basis_v.at[t])
        own_box[t] = box
        boxes_ref[me, t] = box
        for_others(lambda peer: pltpu.make_async_remote_copy(own_box.at[t], boxes_ref.at[me, t], box_send, box_recv.at[t], device_id=peer, device_id_type=MESH).start())
        return carry

    lax.fori_loop(0, TASKS, task, 0)
    for t in range(TASKS):
        done(boxes_ref.at[pl.ds(0, DEVICES - 1), t], box_recv.at[t])
    done(boxes_ref.at[pl.ds(0, DEVICES - 1)], box_send)
    done(held.at[pl.ds(0, 2)], sib_send)
    done(held.at[pl.ds(0, 60)], send_sem)
    done(wants_v.at[others], want_send)
    done(wheres.at[pl.ds(0, DEVICES - 1)], where_send)
    done(to_z, z_send)
    done(to_sib, zs_send.at[0])
    done(rows_z, zs_send.at[1])
    done(rows_sib, zs_send.at[2])


def run_main(*args):
    any_space = pl.BlockSpec(memory_space=pl.ANY)
    vmem = pl.BlockSpec(memory_space=pltpu.VMEM)
    dma = pltpu.SemaphoreType.DMA
    return pl.pallas_call(
        main_kernel,
        out_shape=(
            jax.ShapeDtypeStruct((TASKS, ORDER, CENTRAL), BF16),
            jax.ShapeDtypeStruct((DEVICES, TASKS, 8, 128), BF16),
            jax.ShapeDtypeStruct((8, 512), I32),
        ),
        in_specs=[any_space] * 9,
        out_specs=(vmem, vmem, vmem),
        scratch_shapes=[
            pltpu.VMEM((64, 17, 16, 128), BF16),
            pltpu.VMEM((1024, 128), F32),
            pltpu.VMEM((2, 2, 128, 16, 128), BF16),
            pltpu.VMEM((2, 2, 128, 128), BF16),
            pltpu.VMEM((128, 16, 128), BF16),
            pltpu.VMEM((4, 64, 16, 128), BF16),
            pltpu.VMEM((6, 64, 128), F32),
            pltpu.VMEM((128, 128), BF16),
            pltpu.VMEM((4, 64, 128), BF16),
            pltpu.VMEM((4, 2, 16, 128), BF16),
            pltpu.VMEM((32, 256), BF16),
            pltpu.VMEM((32, 32), I32),
            pltpu.VMEM((TASKS, NNB), I32),
            pltpu.VMEM((TASKS, ORDER, POINTS), BF16),
            pltpu.VMEM((5, TASKS, NNB), I32),
            pltpu.SMEM((6, TASKS, NNB), I32),
            pltpu.SMEM((TASKS,), F32),
            pltpu.SMEM((3, TASKS), I32),
            pltpu.VMEM((1, 128), I32),
            pltpu.VMEM((DEVICES, 128), I32),
            pltpu.VMEM((TASKS, 8, 128), BF16),
            pltpu.VMEM((ORDER, ORDER), BF16),
            pltpu.VMEM((ORDER, ORDER), BF16),
            pltpu.VMEM((ORDER, ORDER), BF16),
            dma((8,)), dma((TASKS,)), dma((2,)), dma, dma, dma((64,)), dma, dma, dma, dma, dma((5, TASKS)), dma((3,)), dma((5, TASKS)),
            dma, dma, dma, dma((TASKS,)),
        ],
        compiler_params=pltpu.CompilerParams(collective_id=0, has_side_effects=True, vmem_limit_bytes=56 << 20),
    )(*args)


def add_kernel(list_ref, boxes_ref, dens_ref, out_ref, dens_out, grid, sem, dens_sem):
    through = pltpu.make_async_copy(dens_ref, dens_out, dens_sem)
    through.start()
    grid[...] = jnp.zeros_like(grid)
    lane = iota((8, 128), 1)

    def add(n, carry):
        for m in range(4):
            at = 4 * n + m
            start, row, col = list_ref[0, at], list_ref[1, at], list_ref[2, at]
            box = boxes_ref[list_ref[3, at], list_ref[4, at]].astype(F32)
            inside = (lane >= col) & (lane < col + 16)
            for l in range(8):
                moved = jnp.where(inside, pltpu.roll(box, (col + 128 - 16 * l) % 128, 1), 0.0)
                grid[start + l // 2, pl.ds(row + 8 * (l % 2), 8), :] += moved
        return carry

    lax.fori_loop(0, (list_ref[5, 0] + 3) // 4, add, 0)
    copy = pltpu.make_async_copy(grid.at[pl.ds(3, SLAB)], out_ref, sem)
    copy.start()
    copy.wait()
    through.wait()


def add_boxes(listed, boxes, dens):
    any_space = pl.BlockSpec(memory_space=pl.ANY)
    vmem = pl.BlockSpec(memory_space=pltpu.VMEM)
    return pl.pallas_call(
        add_kernel,
        out_shape=(
            jax.ShapeDtypeStruct((SLAB, ROWS, COLS), F32),
            jax.ShapeDtypeStruct(dens.shape, dens.dtype),
        ),
        in_specs=[pl.BlockSpec(memory_space=pltpu.SMEM), vmem, vmem],
        out_specs=(any_space, any_space),
        scratch_shapes=[
            pltpu.VMEM((SLAB + 10, ROWS, COLS), F32),
            pltpu.SemaphoreType.DMA,
            pltpu.SemaphoreType.DMA,
        ],
    )(listed, boxes, dens)


def on_device(*args):
    dens, boxes, listed = run_main(*args)
    rho, dens = add_boxes(listed, boxes, dens)
    return dens, rho


def solution(mesh):
    torus = Mesh(mesh.devices.reshape(4, 4, 2, mesh.shape["grid"]), AXES)
    atoms, both = P(AXES[:3]), P(AXES)
    return jax.shard_map(
        on_device,
        mesh=torus,
        in_specs=(atoms, atoms, atoms, both, both, both, both, both, both),
        out_specs=(both, P("grid")),
        check_vma=False,
    )
```

```python
import jax
import jax.numpy as jnp
from jax import lax
from jax.experimental import pallas as pl
from jax.experimental.pallas import tpu as pltpu
from jax.sharding import Mesh
from jax.sharding import PartitionSpec as P

F32, BF16, I32 = jnp.float32, jnp.bfloat16, jnp.int32
BS, KNB, NNB, ORDER, CENTRAL, POINTS, ITERS = 16, 32, 32, 512, 128, 1024, 3
SLAB, ROWS, COLS = 64, 32, 128
DEVICES, TASKS = 128, 4
AXES = ("atoms_0", "atoms_1", "atoms_2", "grid")
MESH = pl.DeviceIdType.MESH


def iota(shape, dim):
    return lax.broadcasted_iota(I32, shape, dim)


def fill_constants(perm):
    rows, cols = iota((ORDER, ORDER), 0), iota((ORDER, ORDER), 1)
    hit = (rows // BS == cols % NNB) & (rows % BS == cols // NNB)
    perm[...] = hit.astype(F32).astype(BF16)


def assemble(atoms_of, ids_of, onsite_of, tile_of, shift_of, perm, found, mixed, whole, pair, start):
    keep = {}
    lane = iota((NNB, 128), 1)

    def prepare():
        keep["ids"], keep["onsite"], keep["atoms"] = ids_of(), onsite_of(), atoms_of()

    def find(g):
        picks = []
        for jj in range(8):
            j = 8 * g + jj
            hit = (keep["ids"][j : j + 1, :] == keep["atoms"]) & (lane // KNB == jj % 4)
            hit = hit.astype(F32)
            none = jnp.zeros((NNB, 128), F32)
            picks.append(jnp.concatenate([hit, none] if jj < 4 else [none, hit], axis=1))
        pick = jnp.concatenate(picks, axis=0).astype(BF16)
        tiles = [jnp.concatenate([tile_of(8 * g + j, h, 0), tile_of(8 * g + j, h, 1)], axis=1) for j in range(8) for h in range(2)]
        got = jnp.dot(pick, jnp.concatenate(tiles, axis=0), preferred_element_type=F32)
        row = iota((8, 256), 0)
        for jj in range(8):
            j = 8 * g + jj
            part = got[NNB * jj : NNB * (jj + 1)]
            own = 8 * (j // 8)
            line = part[own : own + 8] + jnp.where(row == j % 8, keep["onsite"][j : j + 1, :], 0.0)
            pieces = [part[:own]] * (own > 0) + [line] + [part[own + 8 :]] * (own + 8 < NNB)
            found[g, pl.ds(NNB * jj, NNB), :] = jnp.concatenate(pieces, axis=0).astype(BF16)

    def turn(g, half):
        block = lane // BS
        tiles = []
        for j in range(8):
            tile = found[g, pl.ds(NNB * j, NNB), pl.ds(128 * half, 128)]
            tiles.append(pltpu.roll(tile, BS * j, 1) if j else tile)
        tiles = [tiles[-q % 8] for q in range(8)]
        for step in (1, 2, 4):
            odd = (block // step) % 2 == 1
            tiles = [jnp.where(odd, tiles[(q - step) % 8], tiles[q]) for q in range(8)]
        for a in range(8):
            tile = pltpu.roll(tiles[a], 128 - BS * a, 1) if a else tiles[a]
            mixed[pl.ds((8 * half + a) * NNB, NNB), pl.ds(128 * g, 128)] = tile

    def order():
        whole[...] = jnp.dot(perm[...], mixed[...], preferred_element_type=F32).astype(BF16)

    def fold(r):
        rows = pl.ds(128 * r, 128)
        twice = whole[rows, :].astype(F32) + whole[:, rows].T.astype(F32)
        eye = iota((128, 128), 0) == iota((128, 128), 1)
        low, high = 128 * r, 128 * (r + 1)
        diagonal = twice[:, low:high] - jnp.where(eye, 2.0 * shift_of(), 0.0)
        pieces = [twice[:, :low]] * (r > 0) + [diagonal] + [twice[:, high:]] * (r < 3)
        twice = jnp.concatenate(pieces, axis=1)
        pair[rows, :] = twice
        part = jnp.sum(jnp.abs(twice).reshape(16, 8, ORDER), axis=0)
        keep["sum"] = part if r == 0 else keep["sum"] + part

    def limit():
        sums = jnp.sum(keep["sum"], axis=0, keepdims=True)
        bound = 0.5 * jnp.max(sums, axis=1, keepdims=True) + 1e-6
        keep["scale"] = 0.5 / bound

    def scale(r):
        rows = pl.ds(128 * r, 128)
        start[rows, :] = (pair[rows, :] * keep["scale"]).astype(BF16)

    steps = [prepare]
    for g in range(4):
        steps += [lambda g=g: find(g)] + [lambda g=g, half=half: turn(g, half) for half in range(2)]
    steps += [order]
    steps += [lambda r=r: fold(r) for r in range(4)] + [limit]
    return steps, [lambda r=r: scale(r) for r in range(4)]


def less_half(product, first):
    pieces = []
    width = product.shape[1]
    for r in range(ORDER // 128):
        rows = product[128 * r : 128 * (r + 1)]
        lead = 128 * r - first
        if 0 <= lead < width:
            eye = iota((128, 128), 0) == iota((128, 128), 1)
            cut = jnp.where(eye, 1.5, 0.0) - 0.5 * rows[:, lead : lead + 128]
            parts = [-0.5 * rows[:, :lead]] * (lead > 0) + [cut] + [-0.5 * rows[:, lead + 128 :]] * (lead + 128 < width)
            pieces.append(jnp.concatenate(parts, axis=1))
        else:
            pieces.append(-0.5 * rows)
    return jnp.concatenate(pieces, axis=0).astype(BF16)


def iterate(start, middle, late, factor, narrow, set_density, basis_of, set_box):
    keep = {}

    def square(source):
        factor[...] = less_half(jnp.dot(source[...], source[...], preferred_element_type=F32), 0)

    def multiply(source, target):
        target[...] = jnp.dot(source[...], factor[...], preferred_element_type=F32).astype(BF16)

    def last_factor():
        narrow[...] = less_half(jnp.dot(late[...], late[:, :CENTRAL], preferred_element_type=F32), 0)

    def last_product():
        last = jnp.dot(late[...], narrow[...], preferred_element_type=F32)
        eye = iota((CENTRAL, CENTRAL), 0) == iota((CENTRAL, CENTRAL), 1)
        top = 0.5 * (jnp.where(eye, 1.0, 0.0) - last[:CENTRAL])
        density = jnp.concatenate([top, 0.5 * (0.0 - last[CENTRAL:])], axis=0).astype(BF16)
        set_density(density)
        keep["density"] = density.T

    def collocate(n):
        basis = basis_of()
        cols = pl.ds(512 * n, 512)
        weights = jnp.dot(keep["density"], basis[:, cols], preferred_element_type=F32)
        part = jnp.sum(weights * basis[:CENTRAL, cols].astype(F32), axis=0, keepdims=True)
        keep.setdefault("values", []).append(part)

    def finish():
        set_box(pack_box(jnp.concatenate(keep["values"], axis=1)))

    early = [lambda: square(start), lambda: multiply(start, middle)]
    rest = [lambda: square(middle), lambda: multiply(middle, late), last_factor, last_product]
    rest += [lambda n=n: collocate(n) for n in range(2)] + [finish]
    return early, rest


def interleaved(first, second):
    marks = [((k + 0.5) / len(first), 0, k) for k in range(len(first))] + [((k + 0.5) / len(second), 1, k) for k in range(len(second))]
    for _, which, k in sorted(marks):
        (first, second)[which][k]()


def pack_box(values):
    box = jnp.concatenate([values[:, 128 * l : 128 * (l + 1)] for l in range(8)], axis=0)
    row, lane = iota((8, 128), 0), iota((8, 128), 1)
    for step in (1, 2, 4):
        high_row, high_lane = (row // step) % 2 == 1, (lane // (BS * step)) % 2 == 1
        from_below = pltpu.roll(pltpu.roll(box, 8 - step, 0), BS * step, 1)
        from_above = pltpu.roll(pltpu.roll(box, step, 0), 128 - BS * step, 1)
        crossed = jnp.where(high_row, from_above, from_below)
        box = jnp.where(high_row == high_lane, box, crossed)
    return box.astype(BF16)


def slab_list(wheres, first):
    rows = wheres[...].astype(F32)
    lane = iota((DEVICES, 128), 1)
    start = rows - first
    hit = ((start >= 0) & (start < SLAB + 3) & (lane < TASKS)).astype(F32)
    below = (iota((DEVICES, DEVICES), 1) < iota((DEVICES, DEVICES), 0)).astype(F32).astype(BF16)
    before = jnp.dot(below, hit.astype(BF16), preferred_element_type=F32)
    totals = jnp.sum(hit, axis=0, keepdims=True)
    turned = rows.T
    slots = iota((DEVICES, 512), 1).astype(F32)
    base = jnp.zeros((1, 1), F32)
    listed = jnp.zeros((8, 512), F32)
    line = iota((8, 128), 0)
    device = iota((8, 128), 1).astype(F32)
    for t in range(TASKS):
        chosen = (before[:, t : t + 1] + base == slots) & (hit[:, t : t + 1] > 0.5)
        values = jnp.where(line == 3, device, jnp.where(line == 4, float(t), 0.0))
        for v in range(3):
            values = jnp.where(line == v, turned[4 * v + t : 4 * v + t + 1, :], values)
        listed += jnp.dot(values.astype(BF16), chosen.astype(F32).astype(BF16), preferred_element_type=F32)
        base = base + totals[:, t : t + 1]
    row, slot = iota((8, 512), 0), iota((8, 512), 1).astype(F32)
    used = slot < base
    listed = jnp.where(row == 0, jnp.where(used, listed - first, SLAB + 6.0), listed)
    return jnp.where(row == 5, base, listed).astype(I32)


def main_kernel(blocks_ref, onsite_ref, ids_ref, atoms_ref, shift_ref, basis_ref, start_ref, row_ref, col_ref,
                dens_ref, boxes_ref, list_ref,
                held, flat, got, gots, to_sib, to_z, rows_f, rows_sib, rows_z, small, onsite_v, ids_v, atoms_v, basis_v,
                wants_v, wants_s, shift_s, where_s, where_v, wheres, own_box, perm, found, mixed, whole, pair, start, middle, late, factor, narrow,
                load_sem, basis_sem, own_sem, sib_send, send_sem, recv_sem, want_send, want_recv, move_sem, z_send, z_recv, zs_send, zs_recv,
                where_send, where_recv, over_send, over_recv, box_send, box_recv, pass_send, pass_recv):
    y, x, c, z = (lax.axis_index(a) for a in AXES)
    h, o = z % 2, 1 - c
    slot = c * 64 + (y * 4 + x) * 4 + z
    sibling = (y, x, o, z)
    up, down = (z + 1) % 4, (z + 3) % 4
    z_peers = [(y, x, c, up), (y, x, o, up), (y, x, c, down), (y, x, o, down)]

    def ring(f, dp, dq):
        if f == 0:
            return ((y + dq) % 4, (x + dp) % 4, c, z)
        return ((y + dp) % 4, (x + dq) % 4, c, z)

    def unit(f, dp, dq, s):
        place = ring(f, dp, dq)
        return ((place[0] * 4 + place[1]) * 2 + s) * 2 + f

    def done(ref, sem):
        pltpu.make_async_copy(ref, ref, sem).wait()

    def for_others(act, cores=1):
        def block(b, carry, skip=0):
            for d in range(skip, 4 * cores):
                act(((y + b // 4) % 4, (x + b % 4) % 4, (c + d // 4) % 2, (z + d % 4) % 4))
            return carry

        lax.fori_loop(1, 16, block, 0)
        block(0, 0, 1)

    barrier = pltpu.get_barrier_semaphore()
    for_others(lambda peer: pl.semaphore_signal(barrier, inc=1, device_id=peer, device_id_type=MESH), 2)

    half_k = pl.ds(pl.multiple_of(16 * h, 16), 16)
    mine = pl.ds(pl.multiple_of(128 * c, 128), 128)
    theirs = pl.ds(pl.multiple_of(128 * o, 128), 128)
    loads = [
        pltpu.make_async_copy(onsite_ref, onsite_v, load_sem.at[0]),
        pltpu.make_async_copy(ids_ref, ids_v, load_sem.at[1]),
        pltpu.make_async_copy(atoms_ref, atoms_v, load_sem.at[2]),
        pltpu.make_async_copy(shift_ref, shift_s, load_sem.at[3]),
        pltpu.make_async_copy(start_ref, where_s.at[0], load_sem.at[4]),
        pltpu.make_async_copy(row_ref, where_s.at[1], load_sem.at[5]),
        pltpu.make_async_copy(col_ref, where_s.at[2], load_sem.at[6]),
    ]
    for load in loads:
        load.start()
    for f in range(2):
        u = unit(f, 0, 0, c)
        pltpu.make_async_copy(blocks_ref.at[pl.ds(16 * f, 16), half_k, mine], held.at[pl.ds(17 * u, 16)], own_sem.at[f]).start()
    loads[0].wait()
    loads[1].wait()
    tiled = jnp.concatenate([ids_v[...]] * 4, axis=1)
    small[0] = onsite_v[:, :128].reshape(2, 16, 128)
    small[1] = onsite_v[:, 128:].reshape(2, 16, 128)
    small[2] = (tiled // 32).astype(F32).astype(BF16).reshape(2, 16, 128)
    small[3] = (tiled % 32).astype(F32).astype(BF16).reshape(2, 16, 128)
    for f in range(2):
        u = unit(f, 0, 0, c)
        pltpu.make_async_copy(small.at[2 * h + c, f], held.at[17 * u + 16], own_sem.at[f]).start()
    pl.semaphore_wait(barrier, DEVICES - 1)
    for f in range(2):
        u = unit(f, 0, 0, c)
        pltpu.make_async_remote_copy(blocks_ref.at[pl.ds(16 * f, 16), half_k, theirs], held.at[pl.ds(17 * u, 16)], sib_send, recv_sem.at[u], device_id=sibling, device_id_type=MESH).start()
        pltpu.make_async_remote_copy(small.at[2 * h + o, f], held.at[17 * u + 16], sib_send, recv_sem.at[u], device_id=sibling, device_id_type=MESH).start()

    def send(f, u, dp, dq):
        pltpu.make_async_remote_copy(held.at[pl.ds(17 * u, 17)], held.at[pl.ds(17 * u, 17)], send_sem, recv_sem.at[u], device_id=ring(f, dp, dq), device_id_type=MESH).start()

    def arrived(u):
        done(held.at[pl.ds(17 * u, 17)], recv_sem.at[u])

    def near(f, u):
        send(f, u, 1, 0)
        send(f, u, 3, 0)

    def far(f, u):
        send(f, u, 0, 1)
        send(f, u, 0, 3)

    for f in range(2):
        u = unit(f, 0, 0, c)
        done(held.at[pl.ds(17 * u, 17)], own_sem.at[f])
        near(f, u)
    for f in range(2):
        u = unit(f, 0, 0, o)
        arrived(u)
        near(f, u)
    for s in (c, o):
        for f in range(2):
            far(f, unit(f, 0, 0, s))
    for load in loads[2:]:
        load.wait()
    for i in range(TASKS):
        pltpu.make_async_copy(basis_ref.at[i], basis_v.at[i], basis_sem.at[i]).start()
    atoms = atoms_v[...]
    wants_v[5] = jnp.concatenate([atoms, atoms + lax.shift_right_logical(atoms, 4)], axis=1)
    want_to = [z_peers[2], z_peers[3], z_peers[0], z_peers[1], sibling]
    for slot_to, peer in enumerate(want_to):
        pltpu.make_async_remote_copy(wants_v.at[5], wants_v.at[slot_to], want_send, want_recv, device_id=peer, device_id_type=MESH).start()
    lane1 = iota((1, 128), 1)
    where = jnp.zeros((1, 128), I32)
    for v in range(3):
        for t in range(TASKS):
            where = jnp.where(lane1 == 4 * v + t, where_s[v, t], where)
    where_v[...] = where
    wheres[pl.ds(slot, 1), :] = where

    def take_near(first):
        s = c if first else o
        for f in range(2):
            u = unit(f, 3, 0, s)
            arrived(u)
            if first:
                send(f, u, 1, 0)
            far(f, u)
            u = unit(f, 1, 0, s)
            arrived(u)
            if not first:
                send(f, u, 3, 0)
            far(f, u)

    def take_far(dp, first):
        s = c if first else o
        for f in range(2):
            u = unit(f, dp, 3, s)
            arrived(u)
            if first:
                send(f, u, 0, 1)
            u = unit(f, dp, 1, s)
            arrived(u)
            if not first:
                send(f, u, 0, 3)

    take_near(True)
    take_near(False)
    take_far(0, True)
    take_far(0, False)
    for s in (c, o):
        for f in range(2):
            u = unit(f, 2, 0, s)
            arrived(u)
            far(f, u)
    for dp in (3, 1, 2):
        take_far(dp, True)
        take_far(dp, False)
    for_others(lambda peer: pltpu.make_async_remote_copy(where_v, wheres.at[pl.ds(slot, 1)], where_send, where_recv, device_id=peer, device_id_type=MESH).start())
    others = pl.ds(0, 5)
    done(wants_v.at[others], want_recv)
    moved = pltpu.make_async_copy(wants_v, wants_s, move_sem)
    moved.start()
    for dp in range(4):
        for f in range(2):
            for s in (c, o):
                arrived(unit(f, dp, 2, s))
    for u in range(64):
        flat[pl.ds(16 * u, 16), :] = held[17 * u + 16].astype(F32)
    moved.wait()

    def pick(slot, t, j):
        return held[wants_s[slot, t, j + NNB]], flat[pl.ds(wants_s[slot, t, j], 1), :]

    for t in range(TASKS):
        for i in range(4):
            part = i // 2

            def one(r, carry, i=i, t=t, part=part):
                to_z[i, 16 * t + r], rows_f[i, pl.ds(16 * t + r, 1), :] = pick(i, t, 16 * part + r)
                return carry

            lax.fori_loop(0, 16, one, 0, unroll=True)
            rows_z[i, pl.ds(16 * t, 16), :] = rows_f[i, pl.ds(16 * t, 16), :].astype(BF16)
            at = pl.ds(64 * part + 16 * t, 16)
            pltpu.make_async_remote_copy(to_z.at[i, pl.ds(16 * t, 16)], got.at[h, c, at], z_send, z_recv.at[i, t], device_id=z_peers[i], device_id_type=MESH).start()
            pltpu.make_async_remote_copy(rows_z.at[i, pl.ds(16 * t, 16)], gots.at[h, c, at], zs_send.at[1], zs_recv.at[i, t], device_id=z_peers[i], device_id_type=MESH).start()
    for t in range(TASKS):
        for part in range(2):
            first = 64 * part + 16 * t

            def two(r, carry, t=t, part=part, first=first):
                to_sib[first + r], rows_f[4, pl.ds(16 * part + r, 1), :] = pick(4, t, 16 * part + r)
                return carry

            def three(r, carry, t=t, part=part, first=first):
                got[h, c, first + r], rows_f[5, pl.ds(16 * part + r, 1), :] = pick(5, t, 16 * part + r)
                return carry

            lax.fori_loop(0, 16, two, 0, unroll=True)
            at = pl.ds(first, 16)
            rows_sib[at, :] = rows_f[4, pl.ds(16 * part, 16), :].astype(BF16)
            pltpu.make_async_remote_copy(to_sib.at[at], got.at[h, c, at], zs_send.at[0], z_recv.at[4, t], device_id=sibling, device_id_type=MESH).start()
            pltpu.make_async_remote_copy(rows_sib.at[at], gots.at[h, c, at], zs_send.at[2], zs_recv.at[4, t], device_id=sibling, device_id_type=MESH).start()
            lax.fori_loop(0, 16, three, 0, unroll=True)
            gots[h, c, at, :] = rows_f[5, pl.ds(16 * part, 16), :].astype(BF16)

    side = pl.ds(pl.multiple_of(64 * c, 64), 64)
    done(wheres.at[pl.ds(0, DEVICES // 2 - 1)], where_recv)
    pltpu.make_async_remote_copy(wheres.at[side], wheres.at[side], over_send, over_recv, device_id=sibling, device_id_type=MESH).start()
    fill_constants(perm)
    done(wheres.at[pl.ds(0, 64)], over_recv)
    list_ref[...] = slab_list(wheres, (z * SLAB - 3).astype(F32))

    def wait_task(t):
        for i in range(4):
            done(got.at[0, 0, pl.ds(0, 16)], z_recv.at[i, t])
            done(gots.at[0, 0, pl.ds(0, 16)], zs_recv.at[i, t])
        done(got.at[0, 0, pl.ds(0, 32)], z_recv.at[4, t])
        done(gots.at[0, 0, pl.ds(0, 32)], zs_recv.at[4, t])

    def assemble_task(t):
        def rows(hh, cc):
            return jnp.concatenate([gots[hh, cc, pl.ds(pl.multiple_of(64 * part + 16 * t, 16), 16), :] for part in range(2)], axis=0).astype(F32)

        def atoms_of():
            eye = iota((NNB, NNB), 0) == iota((NNB, NNB), 1)
            atoms = jnp.sum(jnp.where(eye, atoms_v[pl.ds(t, 1), :].astype(F32), 0.0), axis=1, keepdims=True)
            return jnp.broadcast_to(atoms, (NNB, 128))

        return assemble(
            atoms_of,
            lambda: rows(1, 0) * 32.0 + rows(1, 1),
            lambda: jnp.concatenate([rows(0, 0), rows(0, 1)], axis=1),
            lambda j, hh, cc: got[hh, cc, 64 * (j // 16) + 16 * t + j % 16],
            lambda: shift_s[t], perm, found, mixed, whole, pair, start)

    def iterate_task(t):
        def set_density(density):
            dens_ref[t] = density

        def set_box(box):
            own_box[t] = box
            boxes_ref[t, slot] = box

        return iterate(start, middle, late, factor, narrow, set_density, lambda: basis_v.at[t], set_box)

    def send_box(t):
        for_others(lambda peer: pltpu.make_async_remote_copy(own_box.at[t], boxes_ref.at[t, slot], box_send.at[t], box_recv.at[t], device_id=peer, device_id_type=MESH).start())

    def pass_box(t):
        done(boxes_ref.at[t, pl.ds(0, DEVICES // 2 - 1)], box_recv.at[t])
        side = pl.ds(64 * c, 64)
        pltpu.make_async_remote_copy(boxes_ref.at[t, side], boxes_ref.at[t, side], pass_send, pass_recv, device_id=sibling, device_id_type=MESH).start()

    wait_task(0)
    head, tail = assemble_task(0)
    for step in head + tail:
        step()

    def task(t, carry):
        wait_task(t + 1)
        done(basis_v.at[0], basis_sem.at[t])
        early, rest = iterate_task(t)
        head, tail = assemble_task(t + 1)
        steps = early + rest
        interleaved(steps, head)
        for step in tail:
            step()
        send_box(t)

        return carry

    lax.fori_loop(0, TASKS - 1, task, 0)
    done(basis_v.at[0], basis_sem.at[TASKS - 1])
    pass_box(0)
    pass_box(1)
    early, rest = iterate_task(TASKS - 1)
    for step in early + rest:
        step()
    send_box(TASKS - 1)
    pass_box(2)
    pass_box(3)
    half = pl.ds(0, DEVICES // 2 - 1)
    for t in range(TASKS):
        done(boxes_ref.at[t, half], box_send.at[t])
    for sem in (pass_recv, pass_send):
        done(boxes_ref.at[pl.ds(0, 2)], sem)
    done(held.at[pl.ds(0, 34)], sib_send)
    done(held.at[pl.ds(0, 1020)], send_sem)
    done(wants_v.at[others], want_send)
    done(wheres.at[pl.ds(0, DEVICES // 2 - 1)], where_send)
    done(wheres.at[pl.ds(0, 64)], over_send)
    done(to_z, z_send)
    done(to_sib, zs_send.at[0])
    done(rows_z, zs_send.at[1])
    done(rows_sib, zs_send.at[2])


def run_main(*args):
    any_space = pl.BlockSpec(memory_space=pl.ANY)
    vmem = pl.BlockSpec(memory_space=pltpu.VMEM)
    dma = pltpu.SemaphoreType.DMA
    return pl.pallas_call(
        main_kernel,
        out_shape=(
            jax.ShapeDtypeStruct((TASKS, ORDER, CENTRAL), BF16),
            jax.ShapeDtypeStruct((TASKS, DEVICES, 8, 128), BF16),
            jax.ShapeDtypeStruct((8, 512), I32),
        ),
        in_specs=[any_space] * 9,
        out_specs=(vmem, vmem, vmem),
        scratch_shapes=[
            pltpu.VMEM((64 * 17, 16, 128), BF16),
            pltpu.VMEM((1024, 128), F32),
            pltpu.VMEM((2, 2, 128, 16, 128), BF16),
            pltpu.VMEM((2, 2, 128, 128), BF16),
            pltpu.VMEM((128, 16, 128), BF16),
            pltpu.VMEM((4, 64, 16, 128), BF16),
            pltpu.VMEM((6, 64, 128), F32),
            pltpu.VMEM((128, 128), BF16),
            pltpu.VMEM((4, 64, 128), BF16),
            pltpu.VMEM((4, 2, 16, 128), BF16),
            pltpu.VMEM((32, 256), BF16),
            pltpu.VMEM((32, 32), I32),
            pltpu.VMEM((TASKS, NNB), I32),
            pltpu.VMEM((TASKS, ORDER, POINTS), BF16),
            pltpu.VMEM((6, TASKS, 2 * NNB), I32),
            pltpu.SMEM((6, TASKS, 2 * NNB), I32),
            pltpu.SMEM((TASKS,), F32),
            pltpu.SMEM((3, TASKS), I32),
            pltpu.VMEM((1, 128), I32),
            pltpu.VMEM((DEVICES, 128), I32),
            pltpu.VMEM((TASKS, 8, 128), BF16),
            pltpu.VMEM((ORDER, ORDER), BF16),
            pltpu.VMEM((4, 256, 256), BF16),
            pltpu.VMEM((ORDER, ORDER), BF16),
            pltpu.VMEM((ORDER, ORDER), BF16),
            pltpu.VMEM((ORDER, ORDER), F32),
            pltpu.VMEM((ORDER, ORDER), BF16),
            pltpu.VMEM((ORDER, ORDER), BF16),
            pltpu.VMEM((ORDER, ORDER), BF16),
            pltpu.VMEM((ORDER, ORDER), BF16),
            pltpu.VMEM((ORDER, CENTRAL), BF16),
            dma((7,)), dma((TASKS,)), dma((2,)), dma, dma, dma((64,)), dma, dma, dma, dma, dma((5, TASKS)), dma((3,)), dma((5, TASKS)),
            dma, dma, dma, dma, dma((TASKS,)), dma((TASKS,)), dma, dma,
        ],
        compiler_params=pltpu.CompilerParams(collective_id=0, has_side_effects=True, vmem_limit_bytes=56 << 20),
    )(*args)


def add_kernel(list_ref, boxes_ref, dens_ref, out_ref, dens_out, grid, sem, dens_sem):
    through = pltpu.make_async_copy(dens_ref, dens_out, dens_sem)
    through.start()
    grid[...] = jnp.zeros_like(grid)
    lane = iota((8, 128), 1)

    def add(n, carry):
        for m in range(4):
            at = 4 * n + m
            start, row, col = list_ref[0, at], list_ref[1, at], list_ref[2, at]
            box = boxes_ref[list_ref[4, at], list_ref[3, at]].astype(F32)
            inside = (lane >= col) & (lane < col + 16)
            places = [(start + l // 2, pl.ds(row + 8 * (l % 2), 8)) for l in range(8)]
            sums = []
            for l, (plane, rows) in enumerate(places):
                moved = jnp.where(inside, pltpu.roll(box, (col + 128 - 16 * l) % 128, 1), 0.0)
                sums.append(grid[plane, rows, :] + moved)
            for (plane, rows), total in zip(places, sums):
                grid[plane, rows, :] = total
        return carry

    lax.fori_loop(0, (list_ref[5, 0] + 3) // 4, add, 0)
    copy = pltpu.make_async_copy(grid.at[pl.ds(3, SLAB)], out_ref, sem)
    copy.start()
    copy.wait()
    through.wait()


def add_boxes(listed, boxes, dens):
    any_space = pl.BlockSpec(memory_space=pl.ANY)
    vmem = pl.BlockSpec(memory_space=pltpu.VMEM)
    return pl.pallas_call(
        add_kernel,
        out_shape=(
            jax.ShapeDtypeStruct((SLAB, ROWS, COLS), F32),
            jax.ShapeDtypeStruct(dens.shape, dens.dtype),
        ),
        in_specs=[pl.BlockSpec(memory_space=pltpu.SMEM), vmem, vmem],
        out_specs=(any_space, any_space),
        scratch_shapes=[
            pltpu.VMEM((SLAB + 10, ROWS, COLS), F32),
            pltpu.SemaphoreType.DMA,
            pltpu.SemaphoreType.DMA,
        ],
    )(listed, boxes, dens)


def on_device(*args):
    dens, boxes, listed = run_main(*args)
    rho, dens = add_boxes(listed, boxes, dens)
    return dens, rho


def solution(mesh):
    torus = Mesh(mesh.devices.reshape(4, 4, 2, mesh.shape["grid"]), AXES)
    atoms, both = P(AXES[:3]), P(AXES)
    return jax.shard_map(
        on_device,
        mesh=torus,
        in_specs=(atoms, atoms, atoms, both, both, both, both, both, both),
        out_specs=(both, P("grid")),
        check_vma=False,
    )
```

```python
import jax
import jax.numpy as jnp
from jax import lax
from jax.experimental import pallas as pl
from jax.experimental.pallas import tpu as pltpu
from jax.sharding import Mesh
from jax.sharding import PartitionSpec as P

F32, BF16, I32 = jnp.float32, jnp.bfloat16, jnp.int32
BS, KNB, NNB, ORDER, CENTRAL, POINTS, ITERS = 16, 32, 32, 512, 128, 1024, 3
SLAB, ROWS, COLS = 64, 32, 128
DEVICES, TASKS = 128, 4
AXES = ("atoms_0", "atoms_1", "atoms_2", "grid")
MESH = pl.DeviceIdType.MESH


def iota(shape, dim):
    return lax.broadcasted_iota(I32, shape, dim)


def fill_constants(perm):
    rows, cols = iota((ORDER, ORDER), 0), iota((ORDER, ORDER), 1)
    hit = (rows // BS == cols % NNB) & (rows % BS == cols // NNB)
    perm[...] = hit.astype(F32).astype(BF16)


def assemble(atoms_of, ids_of, onsite_of, tile_of, shift_of, perm, found, mixed, whole, pair, start):
    keep = {}
    lane = iota((NNB, 128), 1)

    def prepare():
        keep["ids"], keep["onsite"], keep["atoms"] = ids_of(), onsite_of(), atoms_of()

    def find(g):
        picks = []
        for jj in range(8):
            j = 8 * g + jj
            hit = (keep["ids"][j : j + 1, :] == keep["atoms"]) & (lane // KNB == jj % 4)
            hit = hit.astype(F32)
            none = jnp.zeros((NNB, 128), F32)
            picks.append(jnp.concatenate([hit, none] if jj < 4 else [none, hit], axis=1))
        pick = jnp.concatenate(picks, axis=0).astype(BF16)
        tiles = [jnp.concatenate([tile_of(8 * g + j, h, 0), tile_of(8 * g + j, h, 1)], axis=1) for j in range(8) for h in range(2)]
        got = jnp.dot(pick, jnp.concatenate(tiles, axis=0), preferred_element_type=F32)
        row = iota((8, 256), 0)
        for jj in range(8):
            j = 8 * g + jj
            part = got[NNB * jj : NNB * (jj + 1)]
            own = 8 * (j // 8)
            line = part[own : own + 8] + jnp.where(row == j % 8, keep["onsite"][j : j + 1, :], 0.0)
            pieces = [part[:own]] * (own > 0) + [line] + [part[own + 8 :]] * (own + 8 < NNB)
            found[g, pl.ds(NNB * jj, NNB), :] = jnp.concatenate(pieces, axis=0).astype(BF16)

    def turn(g, half):
        block = lane // BS
        tiles = []
        for j in range(8):
            tile = found[g, pl.ds(NNB * j, NNB), pl.ds(128 * half, 128)]
            tiles.append(pltpu.roll(tile, BS * j, 1) if j else tile)
        tiles = [tiles[-q % 8] for q in range(8)]
        for step in (1, 2, 4):
            odd = (block // step) % 2 == 1
            tiles = [jnp.where(odd, tiles[(q - step) % 8], tiles[q]) for q in range(8)]
        for a in range(8):
            tile = pltpu.roll(tiles[a], 128 - BS * a, 1) if a else tiles[a]
            mixed[pl.ds((8 * half + a) * NNB, NNB), pl.ds(128 * g, 128)] = tile

    def order():
        whole[...] = jnp.dot(perm[...], mixed[...], preferred_element_type=F32).astype(BF16)

    def fold(r):
        rows = pl.ds(128 * r, 128)
        twice = whole[rows, :].astype(F32) + whole[:, rows].T.astype(F32)
        eye = iota((128, 128), 0) == iota((128, 128), 1)
        low, high = 128 * r, 128 * (r + 1)
        diagonal = twice[:, low:high] - jnp.where(eye, 2.0 * shift_of(), 0.0)
        pieces = [twice[:, :low]] * (r > 0) + [diagonal] + [twice[:, high:]] * (r < 3)
        twice = jnp.concatenate(pieces, axis=1)
        pair[rows, :] = twice
        part = jnp.sum(jnp.abs(twice).reshape(16, 8, ORDER), axis=0)
        keep["sum"] = part if r == 0 else keep["sum"] + part

    def limit():
        sums = jnp.sum(keep["sum"], axis=0, keepdims=True)
        bound = 0.5 * jnp.max(sums, axis=1, keepdims=True) + 1e-6
        keep["scale"] = 0.5 / bound

    def scale(r):
        rows = pl.ds(128 * r, 128)
        start[rows, :] = (pair[rows, :] * keep["scale"]).astype(BF16)

    steps = [prepare]
    for g in range(4):
        steps += [lambda g=g: find(g)] + [lambda g=g, half=half: turn(g, half) for half in range(2)]
    steps += [order]
    steps += [lambda r=r: fold(r) for r in range(4)] + [limit]
    return steps, [lambda r=r: scale(r) for r in range(4)]


def less_half(product, first):
    pieces = []
    width = product.shape[1]
    for r in range(ORDER // 128):
        rows = product[128 * r : 128 * (r + 1)]
        lead = 128 * r - first
        if 0 <= lead < width:
            eye = iota((128, 128), 0) == iota((128, 128), 1)
            cut = jnp.where(eye, 1.5, 0.0) - 0.5 * rows[:, lead : lead + 128]
            parts = [-0.5 * rows[:, :lead]] * (lead > 0) + [cut] + [-0.5 * rows[:, lead + 128 :]] * (lead + 128 < width)
            pieces.append(jnp.concatenate(parts, axis=1))
        else:
            pieces.append(-0.5 * rows)
    return jnp.concatenate(pieces, axis=0).astype(BF16)


def iterate(start, middle, late, factor, narrow, set_density, basis_of, set_box):
    keep = {}

    def square(source):
        factor[...] = less_half(jnp.dot(source[...], source[...], preferred_element_type=F32), 0)

    def multiply(source, target):
        target[...] = jnp.dot(source[...], factor[...], preferred_element_type=F32).astype(BF16)

    def last_factor():
        narrow[...] = less_half(jnp.dot(late[...], late[:, :CENTRAL], preferred_element_type=F32), 0)

    def last_product():
        last = jnp.dot(late[...], narrow[...], preferred_element_type=F32)
        eye = iota((CENTRAL, CENTRAL), 0) == iota((CENTRAL, CENTRAL), 1)
        top = 0.5 * (jnp.where(eye, 1.0, 0.0) - last[:CENTRAL])
        density = jnp.concatenate([top, 0.5 * (0.0 - last[CENTRAL:])], axis=0).astype(BF16)
        set_density(density)
        keep["density"] = density.T

    def collocate(n):
        basis = basis_of()
        cols = pl.ds(512 * n, 512)
        weights = jnp.dot(keep["density"], basis[:, cols], preferred_element_type=F32)
        part = jnp.sum(weights * basis[:CENTRAL, cols].astype(F32), axis=0, keepdims=True)
        keep.setdefault("values", []).append(part)

    def finish():
        set_box(pack_box(jnp.concatenate(keep["values"], axis=1)))

    early = [lambda: square(start), lambda: multiply(start, middle)]
    rest = [lambda: square(middle), lambda: multiply(middle, late), last_factor, last_product]
    rest += [lambda n=n: collocate(n) for n in range(2)] + [finish]
    return early, rest


def interleaved(first, second):
    marks = [((k + 0.5) / len(first), 0, k) for k in range(len(first))] + [((k + 0.5) / len(second), 1, k) for k in range(len(second))]
    for _, which, k in sorted(marks):
        (first, second)[which][k]()


def pack_box(values):
    box = jnp.concatenate([values[:, 128 * l : 128 * (l + 1)] for l in range(8)], axis=0)
    row, lane = iota((8, 128), 0), iota((8, 128), 1)
    for step in (1, 2, 4):
        high_row, high_lane = (row // step) % 2 == 1, (lane // (BS * step)) % 2 == 1
        from_below = pltpu.roll(pltpu.roll(box, 8 - step, 0), BS * step, 1)
        from_above = pltpu.roll(pltpu.roll(box, step, 0), 128 - BS * step, 1)
        crossed = jnp.where(high_row, from_above, from_below)
        box = jnp.where(high_row == high_lane, box, crossed)
    return box.astype(BF16)


def slab_list(wheres, first):
    rows = wheres[...].astype(F32)
    lane = iota((DEVICES, 128), 1)
    start = rows - first
    hit = ((start >= 0) & (start < SLAB + 3) & (lane < TASKS)).astype(F32)
    below = (iota((DEVICES, DEVICES), 1) < iota((DEVICES, DEVICES), 0)).astype(F32).astype(BF16)
    before = jnp.dot(below, hit.astype(BF16), preferred_element_type=F32)
    totals = jnp.sum(hit, axis=0, keepdims=True)
    turned = rows.T
    slots = iota((DEVICES, 512), 1).astype(F32)
    base = jnp.zeros((1, 1), F32)
    listed = jnp.zeros((8, 512), F32)
    line = iota((8, 128), 0)
    device = iota((8, 128), 1).astype(F32)
    for t in range(TASKS):
        chosen = (before[:, t : t + 1] + base == slots) & (hit[:, t : t + 1] > 0.5)
        values = jnp.where(line == 3, device, jnp.where(line == 4, float(t), 0.0))
        for v in range(3):
            values = jnp.where(line == v, turned[4 * v + t : 4 * v + t + 1, :], values)
        listed += jnp.dot(values.astype(BF16), chosen.astype(F32).astype(BF16), preferred_element_type=F32)
        base = base + totals[:, t : t + 1]
    row, slot = iota((8, 512), 0), iota((8, 512), 1).astype(F32)
    base_row = (listed[0:1] - first) * ROWS + listed[1:2]
    lines = [jnp.where(slot[0:1] < base, base_row, (SLAB + 6.0) * ROWS), listed[2:3], listed[4:5] * DEVICES + listed[3:4], base]
    out = jnp.zeros((8, 512), F32)
    for v in range(4):
        out = jnp.where(row == v, lines[v], out)
    return out.astype(I32)


def main_kernel(blocks_ref, onsite_ref, ids_ref, atoms_ref, shift_ref, basis_ref, start_ref, row_ref, col_ref,
                dens_ref, boxes_ref, list_ref,
                held, flat, got, gots, to_sib, to_z, rows_f, rows_sib, rows_z, small, onsite_v, ids_v, atoms_v, basis_v,
                wants_v, wants_s, shift_s, where_s, wheres, perm, found, mixed, whole, pair, start, middle, late, factor, narrow,
                load_sem, basis_sem, own_sem, sib_send, send_sem, recv_sem, want_send, want_recv, move_sem, z_send, z_recv, zs_send, zs_recv,
                where_send, where_recv, box_send, box_recv):
    y, x, c, z = (lax.axis_index(a) for a in AXES)
    h, o = z % 2, 1 - c
    slot = c * 64 + y * 16 + x * 4 + z
    sibling = (y, x, o, z)
    up, down = (z + 1) % 4, (z + 3) % 4
    z_peers = [(y, x, c, up), (y, x, o, up), (y, x, c, down), (y, x, o, down)]

    def ring(f, dp, dq):
        if f == 0:
            return ((y + dq) % 4, (x + dp) % 4, c, z)
        return ((y + dp) % 4, (x + dq) % 4, c, z)

    def unit(f, dp, dq, s):
        place = ring(f, dp, dq)
        return ((place[0] * 4 + place[1]) * 2 + s) * 2 + f

    def done(ref, sem):
        pltpu.make_async_copy(ref, ref, sem).wait()

    stages = [
        [(y, x, c, (z + d) % 4) for d in (1, 3, 2)],
        [(y, (x + d) % 4, c, z) for d in (1, 3, 2)],
        [((y + d) % 4, x, c, z) for d in (1, 3, 2)],
        [sibling],
    ]
    spans = [(slot, 1), (c * 64 + y * 16 + x * 4, 4), (c * 64 + y * 16, 16), (c * 64, 64)]

    def spread(stage, ref, sends, recvs):
        first, count = spans[stage]
        part = ref.at[pl.ds(first, count)]
        for peer in stages[stage]:
            pltpu.make_async_remote_copy(part, part, sends.at[stage], recvs.at[stage], device_id=peer, device_id_type=MESH).start()

    def collect(stage, ref, sem):
        count = spans[stage][1] * len(stages[stage])
        done(ref.at[pl.ds(0, count)], sem.at[stage])

    barrier = pltpu.get_barrier_semaphore()
    peers = stages[0] + stages[1] + stages[2] + stages[3] + [z_peers[1], z_peers[3]]
    for peer in peers:
        pl.semaphore_signal(barrier, inc=1, device_id=peer, device_id_type=MESH)

    half_k = pl.ds(pl.multiple_of(16 * h, 16), 16)
    mine = pl.ds(pl.multiple_of(128 * c, 128), 128)
    theirs = pl.ds(pl.multiple_of(128 * o, 128), 128)
    loads = [
        pltpu.make_async_copy(onsite_ref, onsite_v, load_sem.at[0]),
        pltpu.make_async_copy(ids_ref, ids_v, load_sem.at[1]),
        pltpu.make_async_copy(atoms_ref, atoms_v, load_sem.at[2]),
        pltpu.make_async_copy(shift_ref, shift_s, load_sem.at[3]),
        pltpu.make_async_copy(start_ref, where_s.at[0], load_sem.at[4]),
        pltpu.make_async_copy(row_ref, where_s.at[1], load_sem.at[5]),
        pltpu.make_async_copy(col_ref, where_s.at[2], load_sem.at[6]),
    ]
    for load in loads:
        load.start()
    for f in range(2):
        u = unit(f, 0, 0, c)
        pltpu.make_async_copy(blocks_ref.at[pl.ds(16 * f, 16), half_k, mine], held.at[pl.ds(17 * u, 16)], own_sem.at[f]).start()
    loads[0].wait()
    loads[1].wait()
    tiled = jnp.concatenate([ids_v[...]] * 4, axis=1)
    small[0] = onsite_v[:, :128].reshape(2, 16, 128)
    small[1] = onsite_v[:, 128:].reshape(2, 16, 128)
    small[2] = (tiled // 32).astype(F32).astype(BF16).reshape(2, 16, 128)
    small[3] = (tiled % 32).astype(F32).astype(BF16).reshape(2, 16, 128)
    for f in range(2):
        u = unit(f, 0, 0, c)
        pltpu.make_async_copy(small.at[2 * h + c, f], held.at[17 * u + 16], own_sem.at[f]).start()
    pl.semaphore_wait(barrier, len(peers))
    for f in range(2):
        u = unit(f, 0, 0, c)
        pltpu.make_async_remote_copy(blocks_ref.at[pl.ds(16 * f, 16), half_k, theirs], held.at[pl.ds(17 * u, 16)], sib_send, recv_sem.at[u], device_id=sibling, device_id_type=MESH).start()
        pltpu.make_async_remote_copy(small.at[2 * h + o, f], held.at[17 * u + 16], sib_send, recv_sem.at[u], device_id=sibling, device_id_type=MESH).start()

    def send(f, u, dp, dq):
        pltpu.make_async_remote_copy(held.at[pl.ds(17 * u, 17)], held.at[pl.ds(17 * u, 17)], send_sem, recv_sem.at[u], device_id=ring(f, dp, dq), device_id_type=MESH).start()

    def arrived(u):
        done(held.at[pl.ds(17 * u, 17)], recv_sem.at[u])

    def near(f, u):
        send(f, u, 1, 0)
        send(f, u, 3, 0)

    def far(f, u):
        send(f, u, 0, 1)
        send(f, u, 0, 3)

    for f in range(2):
        u = unit(f, 0, 0, c)
        done(held.at[pl.ds(17 * u, 17)], own_sem.at[f])
        near(f, u)
    for f in range(2):
        u = unit(f, 0, 0, o)
        arrived(u)
        near(f, u)
    for s in (c, o):
        for f in range(2):
            far(f, unit(f, 0, 0, s))
    for load in loads[2:]:
        load.wait()
    for i in range(TASKS):
        pltpu.make_async_copy(basis_ref.at[i], basis_v.at[i], basis_sem.at[i]).start()
    atoms = atoms_v[...]
    wants_v[5] = jnp.concatenate([atoms, atoms + lax.shift_right_logical(atoms, 4)], axis=1)
    want_to = [z_peers[2], z_peers[3], z_peers[0], z_peers[1], sibling]
    for slot_to, peer in enumerate(want_to):
        pltpu.make_async_remote_copy(wants_v.at[5], wants_v.at[slot_to], want_send, want_recv, device_id=peer, device_id_type=MESH).start()
    lane1 = iota((1, 128), 1)
    where = jnp.zeros((1, 128), I32)
    for v in range(3):
        for t in range(TASKS):
            where = jnp.where(lane1 == 4 * v + t, where_s[v, t], where)
    wheres[pl.ds(slot, 1), :] = where
    spread(0, wheres, where_send, where_recv)

    def take_near(first):
        s = c if first else o
        for f in range(2):
            u = unit(f, 3, 0, s)
            arrived(u)
            if first:
                send(f, u, 1, 0)
            far(f, u)
            u = unit(f, 1, 0, s)
            arrived(u)
            if not first:
                send(f, u, 3, 0)
            far(f, u)

    def take_far(dp, first):
        s = c if first else o
        for f in range(2):
            u = unit(f, dp, 3, s)
            arrived(u)
            if first:
                send(f, u, 0, 1)
            u = unit(f, dp, 1, s)
            arrived(u)
            if not first:
                send(f, u, 0, 3)

    take_near(True)
    take_near(False)
    collect(0, wheres, where_recv)
    spread(1, wheres, where_send, where_recv)
    take_far(0, True)
    take_far(0, False)
    for s in (c, o):
        for f in range(2):
            u = unit(f, 2, 0, s)
            arrived(u)
            far(f, u)
    collect(1, wheres, where_recv)
    spread(2, wheres, where_send, where_recv)
    for dp in (3, 1, 2):
        take_far(dp, True)
        take_far(dp, False)
    collect(2, wheres, where_recv)
    spread(3, wheres, where_send, where_recv)
    others = pl.ds(0, 5)
    done(wants_v.at[others], want_recv)
    moved = pltpu.make_async_copy(wants_v, wants_s, move_sem)
    moved.start()
    for dp in range(4):
        for f in range(2):
            for s in (c, o):
                arrived(unit(f, dp, 2, s))
    for u in range(64):
        flat[pl.ds(16 * u, 16), :] = held[17 * u + 16].astype(F32)
    moved.wait()

    def pick(slot, t, j):
        return held[wants_s[slot, t, j + NNB]], flat[pl.ds(wants_s[slot, t, j], 1), :]

    for t in range(TASKS):
        for i in range(4):
            part = i // 2

            def one(r, carry, i=i, t=t, part=part):
                to_z[i, 16 * t + r], rows_f[i, pl.ds(16 * t + r, 1), :] = pick(i, t, 16 * part + r)
                return carry

            lax.fori_loop(0, 16, one, 0, unroll=True)
            rows_z[i, pl.ds(16 * t, 16), :] = rows_f[i, pl.ds(16 * t, 16), :].astype(BF16)
            at = pl.ds(64 * part + 16 * t, 16)
            pltpu.make_async_remote_copy(to_z.at[i, pl.ds(16 * t, 16)], got.at[h, c, at], z_send, z_recv.at[i, t], device_id=z_peers[i], device_id_type=MESH).start()
            pltpu.make_async_remote_copy(rows_z.at[i, pl.ds(16 * t, 16)], gots.at[h, c, at], zs_send.at[1], zs_recv.at[i, t], device_id=z_peers[i], device_id_type=MESH).start()
    for t in range(TASKS):
        for part in range(2):
            first = 64 * part + 16 * t

            def two(r, carry, t=t, part=part, first=first):
                to_sib[first + r], rows_f[4, pl.ds(16 * part + r, 1), :] = pick(4, t, 16 * part + r)
                return carry

            def three(r, carry, t=t, part=part, first=first):
                got[h, c, first + r], rows_f[5, pl.ds(16 * part + r, 1), :] = pick(5, t, 16 * part + r)
                return carry

            lax.fori_loop(0, 16, two, 0, unroll=True)
            at = pl.ds(first, 16)
            rows_sib[at, :] = rows_f[4, pl.ds(16 * part, 16), :].astype(BF16)
            pltpu.make_async_remote_copy(to_sib.at[at], got.at[h, c, at], zs_send.at[0], z_recv.at[4, t], device_id=sibling, device_id_type=MESH).start()
            pltpu.make_async_remote_copy(rows_sib.at[at], gots.at[h, c, at], zs_send.at[2], zs_recv.at[4, t], device_id=sibling, device_id_type=MESH).start()
            lax.fori_loop(0, 16, three, 0, unroll=True)
            gots[h, c, at, :] = rows_f[5, pl.ds(16 * part, 16), :].astype(BF16)

    fill_constants(perm)
    collect(3, wheres, where_recv)
    list_ref[...] = slab_list(wheres, (z * SLAB - 3).astype(F32))

    def wait_task(t):
        for i in range(4):
            done(got.at[0, 0, pl.ds(0, 16)], z_recv.at[i, t])
            done(gots.at[0, 0, pl.ds(0, 16)], zs_recv.at[i, t])
        done(got.at[0, 0, pl.ds(0, 32)], z_recv.at[4, t])
        done(gots.at[0, 0, pl.ds(0, 32)], zs_recv.at[4, t])

    def assemble_task(t):
        def rows(hh, cc):
            return jnp.concatenate([gots[hh, cc, pl.ds(pl.multiple_of(64 * part + 16 * t, 16), 16), :] for part in range(2)], axis=0).astype(F32)

        def atoms_of():
            eye = iota((NNB, NNB), 0) == iota((NNB, NNB), 1)
            atoms = jnp.sum(jnp.where(eye, atoms_v[pl.ds(t, 1), :].astype(F32), 0.0), axis=1, keepdims=True)
            return jnp.broadcast_to(atoms, (NNB, 128))

        return assemble(
            atoms_of,
            lambda: rows(1, 0) * 32.0 + rows(1, 1),
            lambda: jnp.concatenate([rows(0, 0), rows(0, 1)], axis=1),
            lambda j, hh, cc: got[hh, cc, 64 * (j // 16) + 16 * t + j % 16],
            lambda: shift_s[t], perm, found, mixed, whole, pair, start)

    def iterate_task(t):
        def set_density(density):
            dens_ref[t] = density

        def set_box(box):
            boxes_ref[t, slot] = box

        return iterate(start, middle, late, factor, narrow, set_density, lambda: basis_v.at[t], set_box)

    def spread_box(stage, t):
        spread(stage, boxes_ref.at[t], box_send.at[t], box_recv.at[t])

    def collect_box(stage, t):
        collect(stage, boxes_ref.at[t], box_recv.at[t])

    wait_task(0)
    head, tail = assemble_task(0)
    for step in head + tail:
        step()

    def task(t, carry):
        wait_task(t + 1)
        done(basis_v.at[0], basis_sem.at[t])
        early, rest = iterate_task(t)
        head, tail = assemble_task(t + 1)
        steps = early + rest
        interleaved(steps, head)
        for step in tail:
            step()
        spread_box(0, t)

        return carry

    lax.fori_loop(0, TASKS - 1, task, 0)
    done(basis_v.at[0], basis_sem.at[TASKS - 1])
    early, rest = iterate_task(TASKS - 1)
    steps = early + rest
    earlier = range(TASKS - 1)
    for n, step in enumerate(steps):
        if n in (2, 4, 6):
            stage = n // 2
            for t in earlier:
                collect_box(stage - 1, t)
                spread_box(stage, t)
        step()
    spread_box(0, TASKS - 1)
    for stage in range(1, 4):
        collect_box(stage - 1, TASKS - 1)
        spread_box(stage, TASKS - 1)
    for t in range(TASKS):
        collect_box(3, t)
        for stage in range(4):
            collect(stage, boxes_ref.at[t], box_send.at[t])
    done(held.at[pl.ds(0, 34)], sib_send)
    done(held.at[pl.ds(0, 1020)], send_sem)
    done(wants_v.at[others], want_send)
    for stage in range(4):
        collect(stage, wheres, where_send)
    done(to_z, z_send)
    done(to_sib, zs_send.at[0])
    done(rows_z, zs_send.at[1])
    done(rows_sib, zs_send.at[2])


def run_main(*args):
    any_space = pl.BlockSpec(memory_space=pl.ANY)
    vmem = pl.BlockSpec(memory_space=pltpu.VMEM)
    dma = pltpu.SemaphoreType.DMA
    return pl.pallas_call(
        main_kernel,
        out_shape=(
            jax.ShapeDtypeStruct((TASKS, ORDER, CENTRAL), BF16),
            jax.ShapeDtypeStruct((TASKS, DEVICES, 8, 128), BF16),
            jax.ShapeDtypeStruct((8, 512), I32),
        ),
        in_specs=[any_space] * 9,
        out_specs=(vmem, vmem, vmem),
        scratch_shapes=[
            pltpu.VMEM((64 * 17, 16, 128), BF16),
            pltpu.VMEM((1024, 128), F32),
            pltpu.VMEM((2, 2, 128, 16, 128), BF16),
            pltpu.VMEM((2, 2, 128, 128), BF16),
            pltpu.VMEM((128, 16, 128), BF16),
            pltpu.VMEM((4, 64, 16, 128), BF16),
            pltpu.VMEM((6, 64, 128), F32),
            pltpu.VMEM((128, 128), BF16),
            pltpu.VMEM((4, 64, 128), BF16),
            pltpu.VMEM((4, 2, 16, 128), BF16),
            pltpu.VMEM((32, 256), BF16),
            pltpu.VMEM((32, 32), I32),
            pltpu.VMEM((TASKS, NNB), I32),
            pltpu.VMEM((TASKS, ORDER, POINTS), BF16),
            pltpu.VMEM((6, TASKS, 2 * NNB), I32),
            pltpu.SMEM((6, TASKS, 2 * NNB), I32),
            pltpu.SMEM((TASKS,), F32),
            pltpu.SMEM((3, TASKS), I32),
            pltpu.VMEM((DEVICES, 128), I32),
            pltpu.VMEM((ORDER, ORDER), BF16),
            pltpu.VMEM((4, 256, 256), BF16),
            pltpu.VMEM((ORDER, ORDER), BF16),
            pltpu.VMEM((ORDER, ORDER), BF16),
            pltpu.VMEM((ORDER, ORDER), F32),
            pltpu.VMEM((ORDER, ORDER), BF16),
            pltpu.VMEM((ORDER, ORDER), BF16),
            pltpu.VMEM((ORDER, ORDER), BF16),
            pltpu.VMEM((ORDER, ORDER), BF16),
            pltpu.VMEM((ORDER, CENTRAL), BF16),
            dma((7,)), dma((TASKS,)), dma((2,)), dma, dma, dma((64,)), dma, dma, dma, dma, dma((5, TASKS)), dma((3,)), dma((5, TASKS)),
            dma((4,)), dma((4,)), dma((TASKS, 4)), dma((TASKS, 4)),
        ],
        compiler_params=pltpu.CompilerParams(collective_id=0, has_side_effects=True, vmem_limit_bytes=56 << 20),
    )(*args)


def add_kernel(list_ref, boxes_ref, dens_ref, out_ref, dens_out, grid, sem, dens_sem):
    through = pltpu.make_async_copy(dens_ref, dens_out, dens_sem)
    through.start()
    grid[...] = jnp.zeros_like(grid)
    lane = iota((8, 128), 1)

    def add(n, carry):
        for m in range(4):
            at = 4 * n + m
            base, col = list_ref[0, at], list_ref[1, at]
            turned = pltpu.roll(boxes_ref[list_ref[2, at]].astype(F32), col, 1)
            inside = (lane >= col) & (lane < col + 16)
            sums = []
            for l in range(8):
                moved = pltpu.roll(turned, 128 - 16 * l, 1) if l else turned
                sums.append(grid[pl.ds(base + 16 * l - 8 * (l % 2), 8), :] + jnp.where(inside, moved, 0.0))
            for l in range(8):
                grid[pl.ds(base + 16 * l - 8 * (l % 2), 8), :] = sums[l]
        return carry

    lax.fori_loop(0, (list_ref[3, 0] + 3) // 4, add, 0)
    copy = pltpu.make_async_copy(grid.at[pl.ds(3 * ROWS, SLAB * ROWS)], out_ref, sem)
    copy.start()
    copy.wait()
    through.wait()


def add_boxes(listed, boxes, dens):
    any_space = pl.BlockSpec(memory_space=pl.ANY)
    vmem = pl.BlockSpec(memory_space=pltpu.VMEM)
    return pl.pallas_call(
        add_kernel,
        out_shape=(
            jax.ShapeDtypeStruct((SLAB * ROWS, COLS), F32),
            jax.ShapeDtypeStruct(dens.shape, dens.dtype),
        ),
        in_specs=[pl.BlockSpec(memory_space=pltpu.SMEM), vmem, vmem],
        out_specs=(any_space, any_space),
        scratch_shapes=[
            pltpu.VMEM(((SLAB + 10) * ROWS, COLS), F32),
            pltpu.SemaphoreType.DMA,
            pltpu.SemaphoreType.DMA,
        ],
    )(listed, boxes, dens)


def on_device(*args):
    dens, boxes, listed = run_main(*args)
    rho, dens = add_boxes(listed, boxes.reshape(TASKS * DEVICES, 8, 128), dens)
    return dens, rho.reshape(SLAB, ROWS, COLS)


def solution(mesh):
    torus = Mesh(mesh.devices.reshape(4, 4, 2, mesh.shape["grid"]), AXES)
    atoms, both = P(AXES[:3]), P(AXES)
    return jax.shard_map(
        on_device,
        mesh=torus,
        in_specs=(atoms, atoms, atoms, both, both, both, both, both, both),
        out_specs=(both, P("grid")),
        check_vma=False,
    )
```

```python
import jax
import jax.numpy as jnp
from jax import lax
from jax.experimental import pallas as pl
from jax.experimental.pallas import tpu as pltpu
from jax.sharding import Mesh
from jax.sharding import PartitionSpec as P

F32, BF16, I32 = jnp.float32, jnp.bfloat16, jnp.int32
BS, KNB, NNB, ORDER, CENTRAL, POINTS, ITERS = 16, 32, 32, 512, 128, 1024, 3
SLAB, ROWS, COLS, BOXP = 64, 32, 128, 4
DEVICES, TASKS, TOGETHER = 128, 4, 16
AXES = ("atoms_0", "atoms_1", "atoms_2", "grid")
MESH = pl.DeviceIdType.MESH


def iota(shape, dim):
    return lax.broadcasted_iota(I32, shape, dim)


def fill_constants(perm):
    rows, cols = iota((ORDER, ORDER), 0), iota((ORDER, ORDER), 1)
    hit = (rows // BS == cols % NNB) & (rows % BS == cols // NNB)
    perm[...] = hit.astype(F32).astype(BF16)


def assemble(atoms_of, ids_of, onsite_of, tile_of, shift_of, perm, found, mixed, whole, pair, start):
    keep = {}
    lane = iota((NNB, 128), 1)

    def prepare():
        keep["ids"], keep["onsite"], keep["atoms"] = ids_of(), onsite_of(), atoms_of()

    def find(g):
        picks = []
        for jj in range(8):
            j = 8 * g + jj
            hit = (keep["ids"][j : j + 1, :] == keep["atoms"]) & (lane // KNB == jj % 4)
            hit = hit.astype(F32)
            none = jnp.zeros((NNB, 128), F32)
            picks.append(jnp.concatenate([hit, none] if jj < 4 else [none, hit], axis=1))
        pick = jnp.concatenate(picks, axis=0).astype(BF16)
        tiles = [jnp.concatenate([tile_of(8 * g + j, h, 0), tile_of(8 * g + j, h, 1)], axis=1) for j in range(8) for h in range(2)]
        got = jnp.dot(pick, jnp.concatenate(tiles, axis=0), preferred_element_type=F32)
        row = iota((8, 256), 0)
        for jj in range(8):
            j = 8 * g + jj
            part = got[NNB * jj : NNB * (jj + 1)]
            own = 8 * (j // 8)
            line = part[own : own + 8] + jnp.where(row == j % 8, keep["onsite"][j : j + 1, :], 0.0)
            pieces = [part[:own]] * (own > 0) + [line] + [part[own + 8 :]] * (own + 8 < NNB)
            found[g, pl.ds(NNB * jj, NNB), :] = jnp.concatenate(pieces, axis=0).astype(BF16)

    def turn(g, half):
        block = lane // BS
        tiles = []
        for j in range(8):
            tile = found[g, pl.ds(NNB * j, NNB), pl.ds(128 * half, 128)]
            tiles.append(pltpu.roll(tile, BS * j, 1) if j else tile)
        tiles = [tiles[-q % 8] for q in range(8)]
        for step in (1, 2, 4):
            odd = (block // step) % 2 == 1
            tiles = [jnp.where(odd, tiles[(q - step) % 8], tiles[q]) for q in range(8)]
        for a in range(8):
            tile = pltpu.roll(tiles[a], 128 - BS * a, 1) if a else tiles[a]
            mixed[pl.ds((8 * half + a) * NNB, NNB), pl.ds(128 * g, 128)] = tile

    def order():
        whole[...] = jnp.dot(perm[...], mixed[...], preferred_element_type=F32).astype(BF16)

    def fold(r):
        rows = pl.ds(128 * r, 128)
        twice = whole[rows, :].astype(F32) + whole[:, rows].T.astype(F32)
        eye = iota((128, 128), 0) == iota((128, 128), 1)
        low, high = 128 * r, 128 * (r + 1)
        diagonal = twice[:, low:high] - jnp.where(eye, 2.0 * shift_of(), 0.0)
        pieces = [twice[:, :low]] * (r > 0) + [diagonal] + [twice[:, high:]] * (r < 3)
        twice = jnp.concatenate(pieces, axis=1)
        pair[rows, :] = twice
        part = jnp.sum(jnp.abs(twice).reshape(16, 8, ORDER), axis=0)
        keep["sum"] = part if r == 0 else keep["sum"] + part

    def limit():
        sums = jnp.sum(keep["sum"], axis=0, keepdims=True)
        bound = 0.5 * jnp.max(sums, axis=1, keepdims=True) + 1e-6
        keep["scale"] = 0.5 / bound

    def scale(r):
        rows = pl.ds(128 * r, 128)
        start[rows, :] = (pair[rows, :] * keep["scale"]).astype(BF16)

    steps = [prepare]
    for g in range(4):
        steps += [lambda g=g: find(g)] + [lambda g=g, half=half: turn(g, half) for half in range(2)]
    steps += [order]
    steps += [lambda r=r: fold(r) for r in range(4)] + [limit]
    return steps, [lambda r=r: scale(r) for r in range(4)]


def less_half(product, first):
    pieces = []
    width = product.shape[1]
    for r in range(ORDER // 128):
        rows = product[128 * r : 128 * (r + 1)]
        lead = 128 * r - first
        if 0 <= lead < width:
            eye = iota((128, 128), 0) == iota((128, 128), 1)
            cut = jnp.where(eye, 1.5, 0.0) - 0.5 * rows[:, lead : lead + 128]
            parts = [-0.5 * rows[:, :lead]] * (lead > 0) + [cut] + [-0.5 * rows[:, lead + 128 :]] * (lead + 128 < width)
            pieces.append(jnp.concatenate(parts, axis=1))
        else:
            pieces.append(-0.5 * rows)
    return jnp.concatenate(pieces, axis=0).astype(BF16)


def iterate(start, middle, late, factor, narrow, set_density, basis_of, set_box):
    keep = {}

    def square(source):
        factor[...] = less_half(jnp.dot(source[...], source[...], preferred_element_type=F32), 0)

    def multiply(source, target):
        target[...] = jnp.dot(source[...], factor[...], preferred_element_type=F32).astype(BF16)

    def last_factor():
        narrow[...] = less_half(jnp.dot(late[...], late[:, :CENTRAL], preferred_element_type=F32), 0)

    def last_product():
        last = jnp.dot(late[...], narrow[...], preferred_element_type=F32)
        eye = iota((CENTRAL, CENTRAL), 0) == iota((CENTRAL, CENTRAL), 1)
        top = 0.5 * (jnp.where(eye, 1.0, 0.0) - last[:CENTRAL])
        density = jnp.concatenate([top, 0.5 * (0.0 - last[CENTRAL:])], axis=0).astype(BF16)
        set_density(density)
        keep["density"] = density.T

    def collocate(n):
        basis = basis_of()
        cols = pl.ds(512 * n, 512)
        weights = jnp.dot(keep["density"], basis[:, cols], preferred_element_type=F32)
        part = jnp.sum(weights * basis[:CENTRAL, cols].astype(F32), axis=0, keepdims=True)
        keep.setdefault("values", []).append(part)

    def finish():
        set_box(pack_box(jnp.concatenate(keep["values"], axis=1)))

    early = [lambda: square(start), lambda: multiply(start, middle)]
    rest = [lambda: square(middle), lambda: multiply(middle, late), last_factor, last_product]
    rest += [lambda n=n: collocate(n) for n in range(2)] + [finish]
    return early, rest


def interleaved(first, second):
    marks = [((k + 0.5) / len(first), 0, k) for k in range(len(first))] + [((k + 0.5) / len(second), 1, k) for k in range(len(second))]
    for _, which, k in sorted(marks):
        (first, second)[which][k]()


def pack_box(values):
    box = jnp.concatenate([values[:, 128 * l : 128 * (l + 1)] for l in range(8)], axis=0)
    row, lane = iota((8, 128), 0), iota((8, 128), 1)
    for step in (1, 2, 4):
        high_row, high_lane = (row // step) % 2 == 1, (lane // (BS * step)) % 2 == 1
        from_below = pltpu.roll(pltpu.roll(box, 8 - step, 0), BS * step, 1)
        from_above = pltpu.roll(pltpu.roll(box, step, 0), 128 - BS * step, 1)
        crossed = jnp.where(high_row, from_above, from_below)
        box = jnp.where(high_row == high_lane, box, crossed)
    return box.astype(BF16)


def slab_list(wheres, first):
    rows = wheres[...].astype(F32)
    lane = iota((DEVICES, 128), 1)
    start = rows - first
    hit = ((start >= 0) & (start < SLAB + 3) & (lane < TASKS)).astype(F32)
    below = (iota((DEVICES, DEVICES), 1) < iota((DEVICES, DEVICES), 0)).astype(F32).astype(BF16)
    before = jnp.dot(below, hit.astype(BF16), preferred_element_type=F32)
    totals = jnp.sum(hit, axis=0, keepdims=True)
    turned = rows.T
    slots = iota((DEVICES, 512), 1).astype(F32)
    base = jnp.zeros((1, 1), F32)
    listed = jnp.zeros((8, 512), F32)
    line = iota((8, 128), 0)
    device = iota((8, 128), 1).astype(F32)
    for t in range(TASKS):
        chosen = (before[:, t : t + 1] + base == slots) & (hit[:, t : t + 1] > 0.5)
        values = jnp.where(line == 3, device, jnp.where(line == 4, float(t), 0.0))
        for v in range(3):
            values = jnp.where(line == v, turned[4 * v + t : 4 * v + t + 1, :], values)
        listed += jnp.dot(values.astype(BF16), chosen.astype(F32).astype(BF16), preferred_element_type=F32)
        base = base + totals[:, t : t + 1]
    row, slot = iota((8, 512), 0), iota((8, 512), 1).astype(F32)
    eights = jnp.floor(listed[1:2] * 0.125) * 8.0
    base_row = (listed[0:1] - first) * ROWS + eights
    lines = [
        jnp.where(slot[0:1] < base, base_row, (SLAB + 6.0) * ROWS),
        listed[2:3],
        listed[4:5] * DEVICES + listed[3:4],
        base,
        listed[1:2] - eights,
    ]
    out = jnp.zeros((8, 512), F32)
    for v, values in enumerate(lines):
        out = jnp.where(row == v, values, out)
    return out.astype(I32)


def main_kernel(blocks_ref, onsite_ref, ids_ref, atoms_ref, shift_ref, basis_ref, start_ref, row_ref, col_ref,
                dens_ref, boxes_ref, list_ref,
                held, flat, got, gots, to_sib, to_z, rows_f, rows_sib, rows_z, small, onsite_v, ids_v, atoms_v, basis_v,
                wants_v, wants_s, shift_s, where_s, where_v, wheres, perm, found, mixed, whole, pair, start, middle, late, factor, narrow,
                load_sem, basis_sem, own_sem, sib_send, send_sem, recv_sem, want_send, want_recv, move_sem, here_sem, z_send, z_recv, zs_send, zs_recv,
                where_send, where_recv, over_send, over_recv, box_send, box_recv):
    y, x, c, z = (lax.axis_index(a) for a in AXES)
    h, o = z % 2, 1 - c
    slot = c * 64 + y * 16 + x * 4 + z
    sibling = (y, x, o, z)
    up, down = (z + 1) % 4, (z + 3) % 4
    z_peers = [(y, x, c, up), (y, x, o, up), (y, x, c, down), (y, x, o, down)]

    def ring(f, dp, dq):
        if f == 0:
            return ((y + dq) % 4, (x + dp) % 4, c, z)
        return ((y + dp) % 4, (x + dq) % 4, c, z)

    def unit(f, dp, dq, s):
        place = ring(f, dp, dq)
        return ((place[0] * 4 + place[1]) * 2 + s) * 2 + f

    def done(ref, sem):
        pltpu.make_async_copy(ref, ref, sem).wait()

    def for_others(act, cores=1):
        def block(b, carry, skip=0):
            for d in range(skip, 4 * cores):
                act(((y + b // 4) % 4, (x + b % 4) % 4, (c + d // 4) % 2, (z + d % 4) % 4))
            return carry

        lax.fori_loop(1, 16, block, 0)
        block(0, 0, 1)

    barrier = pltpu.get_barrier_semaphore()
    near = [
        [(y, x, c, (z + d) % 4) for d in (1, 3, 2)],
        [(y, (x + d) % 4, c, z) for d in (1, 3, 2)],
        [((y + d) % 4, x, c, z) for d in (1, 3, 2)],
        [sibling],
    ]
    peers = near[0] + near[1] + near[2] + near[3] + [z_peers[1], z_peers[3]]
    for peer in peers:
        pl.semaphore_signal(barrier, inc=1, device_id=peer, device_id_type=MESH)

    def tell(stage):
        for peer in near[stage]:
            pl.semaphore_signal(here_sem.at[stage], inc=1, device_id=peer, device_id_type=MESH)

    def told(stage):
        pl.semaphore_wait(here_sem.at[stage], len(near[stage]))


    half_k = pl.ds(pl.multiple_of(16 * h, 16), 16)
    mine = pl.ds(pl.multiple_of(128 * c, 128), 128)
    theirs = pl.ds(pl.multiple_of(128 * o, 128), 128)
    loads = [
        pltpu.make_async_copy(onsite_ref, onsite_v, load_sem.at[0]),
        pltpu.make_async_copy(ids_ref, ids_v, load_sem.at[1]),
        pltpu.make_async_copy(atoms_ref, atoms_v, load_sem.at[2]),
        pltpu.make_async_copy(shift_ref, shift_s, load_sem.at[3]),
        pltpu.make_async_copy(start_ref, where_s.at[0], load_sem.at[4]),
        pltpu.make_async_copy(row_ref, where_s.at[1], load_sem.at[5]),
        pltpu.make_async_copy(col_ref, where_s.at[2], load_sem.at[6]),
    ]
    for load in loads:
        load.start()
    for f in range(2):
        u = unit(f, 0, 0, c)
        pltpu.make_async_copy(blocks_ref.at[pl.ds(16 * f, 16), half_k, mine], held.at[pl.ds(17 * u, 16)], own_sem.at[f]).start()
    loads[0].wait()
    loads[1].wait()
    tiled = jnp.concatenate([ids_v[...]] * 4, axis=1)
    small[0] = onsite_v[:, :128].reshape(2, 16, 128)
    small[1] = onsite_v[:, 128:].reshape(2, 16, 128)
    small[2] = (tiled // 32).astype(F32).astype(BF16).reshape(2, 16, 128)
    small[3] = (tiled % 32).astype(F32).astype(BF16).reshape(2, 16, 128)
    for f in range(2):
        u = unit(f, 0, 0, c)
        pltpu.make_async_copy(small.at[2 * h + c, f], held.at[17 * u + 16], own_sem.at[f]).start()
    pl.semaphore_wait(barrier, len(peers))
    tell(0)
    for f in range(2):
        u = unit(f, 0, 0, c)
        pltpu.make_async_remote_copy(blocks_ref.at[pl.ds(16 * f, 16), half_k, theirs], held.at[pl.ds(17 * u, 16)], sib_send, recv_sem.at[u], device_id=sibling, device_id_type=MESH).start()
        pltpu.make_async_remote_copy(small.at[2 * h + o, f], held.at[17 * u + 16], sib_send, recv_sem.at[u], device_id=sibling, device_id_type=MESH).start()

    def send(f, u, dp, dq):
        pltpu.make_async_remote_copy(held.at[pl.ds(17 * u, 17)], held.at[pl.ds(17 * u, 17)], send_sem, recv_sem.at[u], device_id=ring(f, dp, dq), device_id_type=MESH).start()

    def arrived(u):
        done(held.at[pl.ds(17 * u, 17)], recv_sem.at[u])

    def beside(f, u):
        send(f, u, 1, 0)
        send(f, u, 3, 0)

    def far(f, u):
        send(f, u, 0, 1)
        send(f, u, 0, 3)

    for f in range(2):
        u = unit(f, 0, 0, c)
        done(held.at[pl.ds(17 * u, 17)], own_sem.at[f])
        beside(f, u)
    for f in range(2):
        u = unit(f, 0, 0, o)
        arrived(u)
        beside(f, u)
    for s in (c, o):
        for f in range(2):
            far(f, unit(f, 0, 0, s))
    for load in loads[2:]:
        load.wait()
    for i in range(TASKS):
        pltpu.make_async_copy(basis_ref.at[i], basis_v.at[i], basis_sem.at[i]).start()
    atoms = atoms_v[...]
    wants_v[5] = jnp.concatenate([atoms, atoms + lax.shift_right_logical(atoms, 4)], axis=1)
    want_to = [z_peers[2], z_peers[3], z_peers[0], z_peers[1], sibling]
    for slot_to, peer in enumerate(want_to):
        pltpu.make_async_remote_copy(wants_v.at[5], wants_v.at[slot_to], want_send, want_recv, device_id=peer, device_id_type=MESH).start()
    lane1 = iota((1, 128), 1)
    where = jnp.zeros((1, 128), I32)
    for v in range(3):
        for t in range(TASKS):
            where = jnp.where(lane1 == 4 * v + t, where_s[v, t], where)
    where_v[...] = where
    wheres[pl.ds(slot, 1), :] = where

    def take_near(first):
        s = c if first else o
        for f in range(2):
            u = unit(f, 3, 0, s)
            arrived(u)
            if first:
                send(f, u, 1, 0)
            far(f, u)
            u = unit(f, 1, 0, s)
            arrived(u)
            if not first:
                send(f, u, 3, 0)
            far(f, u)

    def take_far(dp, first):
        s = c if first else o
        for f in range(2):
            u = unit(f, dp, 3, s)
            arrived(u)
            if first:
                send(f, u, 0, 1)
            u = unit(f, dp, 1, s)
            arrived(u)
            if not first:
                send(f, u, 0, 3)

    take_near(True)
    told(0)
    tell(1)
    take_near(False)
    told(1)
    tell(2)
    take_far(0, True)
    told(2)
    tell(3)
    take_far(0, False)
    told(3)
    for s in (c, o):
        for f in range(2):
            u = unit(f, 2, 0, s)
            arrived(u)
            far(f, u)
    for dp in (3, 1, 2):
        take_far(dp, True)
        take_far(dp, False)
    for_others(lambda peer: pltpu.make_async_remote_copy(where_v, wheres.at[pl.ds(slot, 1)], where_send, where_recv, device_id=peer, device_id_type=MESH).start())
    others = pl.ds(0, 5)
    done(wants_v.at[others], want_recv)
    moved = pltpu.make_async_copy(wants_v, wants_s, move_sem)
    moved.start()
    for dp in range(4):
        for f in range(2):
            for s in (c, o):
                arrived(unit(f, dp, 2, s))
    for u in range(64):
        flat[pl.ds(16 * u, 16), :] = held[17 * u + 16].astype(F32)
    moved.wait()

    def pick(slot, t, j):
        return held[wants_s[slot, t, j + NNB]], flat[pl.ds(wants_s[slot, t, j], 1), :]

    for t in range(TASKS):
        for i in range(4):
            part = i // 2

            def one(r, carry, i=i, t=t, part=part):
                to_z[i, 16 * t + r], rows_f[i, pl.ds(16 * t + r, 1), :] = pick(i, t, 16 * part + r)
                return carry

            lax.fori_loop(0, 16, one, 0, unroll=True)
            rows_z[i, pl.ds(16 * t, 16), :] = rows_f[i, pl.ds(16 * t, 16), :].astype(BF16)
            at = pl.ds(64 * part + 16 * t, 16)
            pltpu.make_async_remote_copy(to_z.at[i, pl.ds(16 * t, 16)], got.at[h, c, at], z_send, z_recv.at[i, t], device_id=z_peers[i], device_id_type=MESH).start()
            pltpu.make_async_remote_copy(rows_z.at[i, pl.ds(16 * t, 16)], gots.at[h, c, at], zs_send.at[1], zs_recv.at[i, t], device_id=z_peers[i], device_id_type=MESH).start()
    for t in range(TASKS):
        for part in range(2):
            first = 64 * part + 16 * t

            def two(r, carry, t=t, part=part, first=first):
                to_sib[first + r], rows_f[4, pl.ds(16 * part + r, 1), :] = pick(4, t, 16 * part + r)
                return carry

            def three(r, carry, t=t, part=part, first=first):
                got[h, c, first + r], rows_f[5, pl.ds(16 * part + r, 1), :] = pick(5, t, 16 * part + r)
                return carry

            lax.fori_loop(0, 16, two, 0, unroll=True)
            at = pl.ds(first, 16)
            rows_sib[at, :] = rows_f[4, pl.ds(16 * part, 16), :].astype(BF16)
            pltpu.make_async_remote_copy(to_sib.at[at], got.at[h, c, at], zs_send.at[0], z_recv.at[4, t], device_id=sibling, device_id_type=MESH).start()
            pltpu.make_async_remote_copy(rows_sib.at[at], gots.at[h, c, at], zs_send.at[2], zs_recv.at[4, t], device_id=sibling, device_id_type=MESH).start()
            lax.fori_loop(0, 16, three, 0, unroll=True)
            gots[h, c, at, :] = rows_f[5, pl.ds(16 * part, 16), :].astype(BF16)

    side = pl.ds(pl.multiple_of(64 * c, 64), 64)
    done(wheres.at[pl.ds(0, DEVICES // 2 - 1)], where_recv)
    pltpu.make_async_remote_copy(wheres.at[side], wheres.at[side], over_send, over_recv, device_id=sibling, device_id_type=MESH).start()
    fill_constants(perm)
    done(wheres.at[pl.ds(0, 64)], over_recv)
    list_ref[...] = slab_list(wheres, (z * SLAB - 3).astype(F32))

    def wait_task(t):
        for i in range(4):
            done(got.at[0, 0, pl.ds(0, 16)], z_recv.at[i, t])
            done(gots.at[0, 0, pl.ds(0, 16)], zs_recv.at[i, t])
        done(got.at[0, 0, pl.ds(0, 32)], z_recv.at[4, t])
        done(gots.at[0, 0, pl.ds(0, 32)], zs_recv.at[4, t])

    def assemble_task(t):
        def rows(hh, cc):
            return jnp.concatenate([gots[hh, cc, pl.ds(pl.multiple_of(64 * part + 16 * t, 16), 16), :] for part in range(2)], axis=0).astype(F32)

        def atoms_of():
            eye = iota((NNB, NNB), 0) == iota((NNB, NNB), 1)
            atoms = jnp.sum(jnp.where(eye, atoms_v[pl.ds(t, 1), :].astype(F32), 0.0), axis=1, keepdims=True)
            return jnp.broadcast_to(atoms, (NNB, 128))

        return assemble(
            atoms_of,
            lambda: rows(1, 0) * 32.0 + rows(1, 1),
            lambda: jnp.concatenate([rows(0, 0), rows(0, 1)], axis=1),
            lambda j, hh, cc: got[hh, cc, 64 * (j // 16) + 16 * t + j % 16],
            lambda: shift_s[t], perm, found, mixed, whole, pair, start)

    def iterate_task(t):
        def set_density(density):
            dens_ref[t] = density

        def set_box(box):
            boxes_ref[t, slot] = box

        return iterate(start, middle, late, factor, narrow, set_density, lambda: basis_v.at[t], set_box)

    def send_box(part, peer, t, stage):
        pltpu.make_async_remote_copy(boxes_ref.at[t, part], boxes_ref.at[t, part], box_send.at[t, stage], box_recv.at[t, stage], device_id=peer, device_id_type=MESH).start()

    def box_done(t, stage, count, sem):
        done(boxes_ref.at[t, pl.ds(0, count)], sem.at[t, stage])

    z_span = pl.ds(c * 64 + y * 16 + x * 4, 4)

    wait_task(0)
    head, tail = assemble_task(0)
    for step in head + tail:
        step()

    def task(t, carry):
        wait_task(t + 1)
        done(basis_v.at[0], basis_sem.at[t])
        early, rest = iterate_task(t)
        head, tail = assemble_task(t + 1)
        steps = early + rest
        interleaved(steps, head)
        for step in tail:
            step()
        for d in (1, 3, 2):
            send_box(pl.ds(slot, 1), (y, x, c, (z + d) % 4), t, 0)

        return carry

    lax.fori_loop(0, TASKS - 1, task, 0)
    done(basis_v.at[0], basis_sem.at[TASKS - 1])
    for t in range(TASKS - 1):
        box_done(t, 0, 3, box_recv)
        for d in range(1, 16):
            send_box(z_span, ((y + d // 4) % 4, (x + d % 4) % 4, c, z), t, 1)
    early, rest = iterate_task(TASKS - 1)
    for step in early + rest:
        step()
    for_others(lambda peer: send_box(pl.ds(slot, 1), peer, TASKS - 1, 0), 2)
    for t in range(TASKS - 1):
        box_done(t, 1, 60, box_recv)
        send_box(pl.ds(c * 64, 64), sibling, t, 2)
    for t in range(TASKS - 1):
        box_done(t, 2, 64, box_recv)
        box_done(t, 0, 3, box_send)
        box_done(t, 1, 60, box_send)
        box_done(t, 2, 64, box_send)
    box_done(TASKS - 1, 0, DEVICES - 1, box_recv)
    box_done(TASKS - 1, 0, DEVICES - 1, box_send)
    done(held.at[pl.ds(0, 34)], sib_send)
    done(held.at[pl.ds(0, 1020)], send_sem)
    done(wants_v.at[others], want_send)
    done(wheres.at[pl.ds(0, DEVICES // 2 - 1)], where_send)
    done(wheres.at[pl.ds(0, 64)], over_send)
    done(to_z, z_send)
    done(to_sib, zs_send.at[0])
    done(rows_z, zs_send.at[1])
    done(rows_sib, zs_send.at[2])


def run_main(*args):
    any_space = pl.BlockSpec(memory_space=pl.ANY)
    vmem = pl.BlockSpec(memory_space=pltpu.VMEM)
    dma = pltpu.SemaphoreType.DMA
    return pl.pallas_call(
        main_kernel,
        out_shape=(
            jax.ShapeDtypeStruct((TASKS, ORDER, CENTRAL), BF16),
            jax.ShapeDtypeStruct((TASKS, DEVICES, 8, 128), BF16),
            jax.ShapeDtypeStruct((8, 512), I32),
        ),
        in_specs=[any_space] * 9,
        out_specs=(vmem, vmem, vmem),
        scratch_shapes=[
            pltpu.VMEM((64 * 17, 16, 128), BF16),
            pltpu.VMEM((1024, 128), F32),
            pltpu.VMEM((2, 2, 128, 16, 128), BF16),
            pltpu.VMEM((2, 2, 128, 128), BF16),
            pltpu.VMEM((128, 16, 128), BF16),
            pltpu.VMEM((4, 64, 16, 128), BF16),
            pltpu.VMEM((6, 64, 128), F32),
            pltpu.VMEM((128, 128), BF16),
            pltpu.VMEM((4, 64, 128), BF16),
            pltpu.VMEM((4, 2, 16, 128), BF16),
            pltpu.VMEM((32, 256), BF16),
            pltpu.VMEM((32, 32), I32),
            pltpu.VMEM((TASKS, NNB), I32),
            pltpu.VMEM((TASKS, ORDER, POINTS), BF16),
            pltpu.VMEM((6, TASKS, 2 * NNB), I32),
            pltpu.SMEM((6, TASKS, 2 * NNB), I32),
            pltpu.SMEM((TASKS,), F32),
            pltpu.SMEM((3, TASKS), I32),
            pltpu.VMEM((1, 128), I32),
            pltpu.VMEM((DEVICES, 128), I32),
            pltpu.VMEM((ORDER, ORDER), BF16),
            pltpu.VMEM((4, 256, 256), BF16),
            pltpu.VMEM((ORDER, ORDER), BF16),
            pltpu.VMEM((ORDER, ORDER), BF16),
            pltpu.VMEM((ORDER, ORDER), F32),
            pltpu.VMEM((ORDER, ORDER), BF16),
            pltpu.VMEM((ORDER, ORDER), BF16),
            pltpu.VMEM((ORDER, ORDER), BF16),
            pltpu.VMEM((ORDER, ORDER), BF16),
            pltpu.VMEM((ORDER, CENTRAL), BF16),
            dma((7,)), dma((TASKS,)), dma((2,)), dma, dma, dma((64,)), dma, dma, dma, pltpu.SemaphoreType.REGULAR((4,)), dma, dma((5, TASKS)), dma((3,)), dma((5, TASKS)),
            dma, dma, dma, dma, dma((TASKS, 3)), dma((TASKS, 3)),
        ],
        compiler_params=pltpu.CompilerParams(collective_id=0, has_side_effects=True, vmem_limit_bytes=56 << 20),
    )(*args)


def add_kernel(list_ref, boxes_ref, dens_ref, out_ref, dens_out, grid, sem, dens_sem):
    through = pltpu.make_async_copy(dens_ref, dens_out, dens_sem)
    through.start()
    grid[...] = jnp.zeros_like(grid)
    lane = iota((8, 128), 1)

    line = iota((8, 128), 0)

    def add(n, carry):
        for m in range(TOGETHER):
            at = TOGETHER * n + m
            base, col, down = pl.multiple_of(list_ref[0, at], 8), list_ref[1, at], list_ref[4, at]
            turned = pltpu.roll(pltpu.roll(boxes_ref[list_ref[2, at]].astype(F32), col, 1), down, 0)
            inside = (lane >= col) & (lane < col + 16)
            upper, lower = inside & (line >= down), inside & (line < down)
            pieces = [pltpu.roll(turned, 128 - 16 * l, 1) if l else turned for l in range(8)]
            sums = {}
            for k in range(BOXP):
                first, second = pieces[2 * k], pieces[2 * k + 1]
                parts = [
                    jnp.where(upper, first, 0.0),
                    jnp.where(upper, second, jnp.where(lower, first, 0.0)),
                    jnp.where(lower, second, 0.0),
                ]
                for n8, part in enumerate(parts):
                    off = ROWS * k + 8 * n8
                    sums[off] = grid[pl.ds(base + off, 8), :] + part
            for off, total in sums.items():
                grid[pl.ds(base + off, 8), :] = total
        return carry

    lax.fori_loop(0, (list_ref[3, 0] + TOGETHER - 1) // TOGETHER, add, 0)
    copy = pltpu.make_async_copy(grid.at[pl.ds(3 * ROWS, SLAB * ROWS)], out_ref, sem)
    copy.start()
    copy.wait()
    through.wait()


def add_boxes(listed, boxes, dens):
    any_space = pl.BlockSpec(memory_space=pl.ANY)
    vmem = pl.BlockSpec(memory_space=pltpu.VMEM)
    return pl.pallas_call(
        add_kernel,
        out_shape=(
            jax.ShapeDtypeStruct((SLAB * ROWS, COLS), F32),
            jax.ShapeDtypeStruct(dens.shape, dens.dtype),
        ),
        in_specs=[pl.BlockSpec(memory_space=pltpu.SMEM), vmem, vmem],
        out_specs=(any_space, any_space),
        scratch_shapes=[
            pltpu.VMEM(((SLAB + 10) * ROWS, COLS), F32),
            pltpu.SemaphoreType.DMA,
            pltpu.SemaphoreType.DMA,
        ],
    )(listed, boxes, dens)


def on_device(*args):
    dens, boxes, listed = run_main(*args)
    rho, dens = add_boxes(listed, boxes.reshape(TASKS * DEVICES, 8, 128), dens)
    return dens, rho.reshape(SLAB, ROWS, COLS)


def solution(mesh):
    torus = Mesh(mesh.devices.reshape(4, 4, 2, mesh.shape["grid"]), AXES)
    atoms, both = P(AXES[:3]), P(AXES)
    return jax.shard_map(
        on_device,
        mesh=torus,
        in_specs=(atoms, atoms, atoms, both, both, both, both, both, both),
        out_specs=(both, P("grid")),
        check_vma=False,
    )
```

```python
import jax
import jax.numpy as jnp
from jax import lax
from jax.experimental import pallas as pl
from jax.experimental.pallas import tpu as pltpu
from jax.sharding import Mesh
from jax.sharding import PartitionSpec as P

F32, BF16, I32 = jnp.float32, jnp.bfloat16, jnp.int32
BS, KNB, NNB, ORDER, CENTRAL, POINTS, ITERS = 16, 32, 32, 512, 128, 1024, 3
SLAB, ROWS, COLS, BOXP = 64, 32, 128, 4
DEVICES, TASKS, TOGETHER, LISTED = 128, 4, 24, 640
AXES = ("atoms_0", "atoms_1", "atoms_2", "grid")
MESH = pl.DeviceIdType.MESH


def iota(shape, dim):
    return lax.broadcasted_iota(I32, shape, dim)


def fill_constants(perm):
    rows, cols = iota((ORDER, ORDER), 0), iota((ORDER, ORDER), 1)
    hit = (rows // BS == cols % NNB) & (rows % BS == cols // NNB)
    perm[...] = hit.astype(F32).astype(BF16)


def assemble(atoms_of, ids_of, onsite_of, tile_of, shift_of, perm, found, mixed, whole, pair, start):
    keep = {}
    lane = iota((NNB, 128), 1)

    def prepare():
        keep["ids"], keep["onsite"], keep["atoms"] = ids_of(), onsite_of(), atoms_of()

    def find(g):
        picks = []
        for jj in range(8):
            j = 8 * g + jj
            hit = (keep["ids"][j : j + 1, :] == keep["atoms"]) & (lane // KNB == jj % 4)
            hit = hit.astype(F32)
            none = jnp.zeros((NNB, 128), F32)
            picks.append(jnp.concatenate([hit, none] if jj < 4 else [none, hit], axis=1))
        pick = jnp.concatenate(picks, axis=0).astype(BF16)
        tiles = [jnp.concatenate([tile_of(8 * g + j, h, 0), tile_of(8 * g + j, h, 1)], axis=1) for j in range(8) for h in range(2)]
        got = jnp.dot(pick, jnp.concatenate(tiles, axis=0), preferred_element_type=F32)
        row = iota((8, 256), 0)
        for jj in range(8):
            j = 8 * g + jj
            part = got[NNB * jj : NNB * (jj + 1)]
            own = 8 * (j // 8)
            line = part[own : own + 8] + jnp.where(row == j % 8, keep["onsite"][j : j + 1, :], 0.0)
            pieces = [part[:own]] * (own > 0) + [line] + [part[own + 8 :]] * (own + 8 < NNB)
            found[g, pl.ds(NNB * jj, NNB), :] = jnp.concatenate(pieces, axis=0).astype(BF16)

    def turn(g, half):
        block = lane // BS
        tiles = []
        for j in range(8):
            tile = found[g, pl.ds(NNB * j, NNB), pl.ds(128 * half, 128)]
            tiles.append(pltpu.roll(tile, BS * j, 1) if j else tile)
        tiles = [tiles[-q % 8] for q in range(8)]
        for step in (1, 2, 4):
            odd = (block // step) % 2 == 1
            tiles = [jnp.where(odd, tiles[(q - step) % 8], tiles[q]) for q in range(8)]
        for a in range(8):
            tile = pltpu.roll(tiles[a], 128 - BS * a, 1) if a else tiles[a]
            mixed[pl.ds((8 * half + a) * NNB, NNB), pl.ds(128 * g, 128)] = tile

    def order():
        whole[...] = jnp.dot(perm[...], mixed[...], preferred_element_type=F32).astype(BF16)

    def fold(r):
        rows = pl.ds(128 * r, 128)
        twice = whole[rows, :].astype(F32) + whole[:, rows].T.astype(F32)
        eye = iota((128, 128), 0) == iota((128, 128), 1)
        low, high = 128 * r, 128 * (r + 1)
        diagonal = twice[:, low:high] - jnp.where(eye, 2.0 * shift_of(), 0.0)
        pieces = [twice[:, :low]] * (r > 0) + [diagonal] + [twice[:, high:]] * (r < 3)
        twice = jnp.concatenate(pieces, axis=1)
        pair[rows, :] = twice
        part = jnp.sum(jnp.abs(twice).reshape(16, 8, ORDER), axis=0)
        keep["sum"] = part if r == 0 else keep["sum"] + part

    def limit():
        sums = jnp.sum(keep["sum"], axis=0, keepdims=True)
        bound = 0.5 * jnp.max(sums, axis=1, keepdims=True) + 1e-6
        keep["scale"] = 0.5 / bound

    def scale(r):
        rows = pl.ds(128 * r, 128)
        start[rows, :] = (pair[rows, :] * keep["scale"]).astype(BF16)

    steps = [prepare]
    for g in range(4):
        steps += [lambda g=g: find(g)] + [lambda g=g, half=half: turn(g, half) for half in range(2)]
    steps += [order]
    steps += [lambda r=r: fold(r) for r in range(4)] + [limit]
    return steps, [lambda r=r: scale(r) for r in range(4)]


def less_half(product, first):
    pieces = []
    width = product.shape[1]
    for r in range(ORDER // 128):
        rows = product[128 * r : 128 * (r + 1)]
        lead = 128 * r - first
        if 0 <= lead < width:
            eye = iota((128, 128), 0) == iota((128, 128), 1)
            cut = jnp.where(eye, 1.5, 0.0) - 0.5 * rows[:, lead : lead + 128]
            parts = [-0.5 * rows[:, :lead]] * (lead > 0) + [cut] + [-0.5 * rows[:, lead + 128 :]] * (lead + 128 < width)
            pieces.append(jnp.concatenate(parts, axis=1))
        else:
            pieces.append(-0.5 * rows)
    return jnp.concatenate(pieces, axis=0).astype(BF16)


def iterate(start, middle, late, factor, narrow, set_density, basis_of, set_box):
    keep = {}

    def square(source):
        factor[...] = less_half(jnp.dot(source[...], source[...], preferred_element_type=F32), 0)

    def multiply(source, target):
        target[...] = jnp.dot(source[...], factor[...], preferred_element_type=F32).astype(BF16)

    def last_factor():
        narrow[...] = less_half(jnp.dot(late[...], late[:, :CENTRAL], preferred_element_type=F32), 0)

    def last_product():
        last = jnp.dot(late[...], narrow[...], preferred_element_type=F32)
        eye = iota((CENTRAL, CENTRAL), 0) == iota((CENTRAL, CENTRAL), 1)
        top = 0.5 * (jnp.where(eye, 1.0, 0.0) - last[:CENTRAL])
        density = jnp.concatenate([top, 0.5 * (0.0 - last[CENTRAL:])], axis=0).astype(BF16)
        set_density(density)
        keep["density"] = density.T

    def collocate(n):
        basis = basis_of()
        cols = pl.ds(512 * n, 512)
        weights = jnp.dot(keep["density"], basis[:, cols], preferred_element_type=F32)
        part = jnp.sum(weights * basis[:CENTRAL, cols].astype(F32), axis=0, keepdims=True)
        keep.setdefault("values", []).append(part)

    def finish():
        set_box(pack_box(jnp.concatenate(keep["values"], axis=1)))

    early = [lambda: square(start), lambda: multiply(start, middle)]
    rest = [lambda: square(middle), lambda: multiply(middle, late), last_factor, last_product]
    rest += [lambda n=n: collocate(n) for n in range(2)] + [finish]
    return early, rest


def interleaved(first, second):
    marks = [((k + 0.5) / len(first), 0, k) for k in range(len(first))] + [((k + 0.5) / len(second), 1, k) for k in range(len(second))]
    for _, which, k in sorted(marks):
        (first, second)[which][k]()


def pack_box(values):
    box = jnp.concatenate([values[:, 128 * l : 128 * (l + 1)] for l in range(8)], axis=0)
    row, lane = iota((8, 128), 0), iota((8, 128), 1)
    for step in (1, 2, 4):
        high_row, high_lane = (row // step) % 2 == 1, (lane // (BS * step)) % 2 == 1
        from_below = pltpu.roll(pltpu.roll(box, 8 - step, 0), BS * step, 1)
        from_above = pltpu.roll(pltpu.roll(box, step, 0), 128 - BS * step, 1)
        crossed = jnp.where(high_row, from_above, from_below)
        box = jnp.where(high_row == high_lane, box, crossed)
    return box.astype(BF16)


def slab_list(wheres, first):
    rows = wheres[...].astype(F32)
    lane = iota((DEVICES, 128), 1)
    start = rows - first
    hit = ((start >= 0) & (start < SLAB + 3) & (lane < TASKS)).astype(F32)
    below = (iota((DEVICES, DEVICES), 1) < iota((DEVICES, DEVICES), 0)).astype(F32).astype(BF16)
    before = jnp.dot(below, hit.astype(BF16), preferred_element_type=F32)
    totals = jnp.sum(hit, axis=0, keepdims=True)
    turned = rows.T
    slots = iota((DEVICES, LISTED), 1).astype(F32)
    base = jnp.zeros((1, 1), F32)
    listed = jnp.zeros((8, LISTED), F32)
    line = iota((8, 128), 0)
    device = iota((8, 128), 1).astype(F32)
    for t in range(TASKS):
        chosen = (before[:, t : t + 1] + base == slots) & (hit[:, t : t + 1] > 0.5)
        values = jnp.where(line == 3, device, jnp.where(line == 4, float(t), 0.0))
        for v in range(3):
            values = jnp.where(line == v, turned[4 * v + t : 4 * v + t + 1, :], values)
        listed += jnp.dot(values.astype(BF16), chosen.astype(F32).astype(BF16), preferred_element_type=F32)
        base = base + totals[:, t : t + 1]
    row, slot = iota((8, LISTED), 0), iota((8, LISTED), 1).astype(F32)
    eights = jnp.floor(listed[1:2] * 0.125) * 8.0
    base_row = (listed[0:1] - first) * ROWS + eights
    lines = [
        jnp.where(slot[0:1] < base, base_row, (SLAB + 6.0) * ROWS),
        listed[2:3],
        listed[4:5] * DEVICES + listed[3:4],
        base,
        listed[1:2] - eights,
    ]
    out = jnp.zeros((8, LISTED), F32)
    for v, values in enumerate(lines):
        out = jnp.where(row == v, values, out)
    return out.astype(I32)


def main_kernel(blocks_ref, onsite_ref, ids_ref, atoms_ref, shift_ref, basis_ref, start_ref, row_ref, col_ref,
                dens_ref, boxes_ref, list_ref,
                held, flat, got, gots, to_sib, to_z, rows_f, rows_sib, rows_z, small, onsite_v, ids_v, atoms_v, basis_v,
                wants_v, wants_s, shift_s, where_s, where_v, wheres, perm, found, mixed, whole, pair, start, middle, late, factor, narrow,
                load_sem, basis_sem, own_sem, sib_send, send_sem, recv_sem, want_send, want_recv, move_sem, here_sem, z_send, z_recv, zs_send, zs_recv,
                where_send, where_recv, over_send, over_recv, box_send, box_recv):
    y, x, c, z = (lax.axis_index(a) for a in AXES)
    h, o = z % 2, 1 - c
    slot = c * 64 + y * 16 + x * 4 + z
    sibling = (y, x, o, z)
    up, down = (z + 1) % 4, (z + 3) % 4
    z_peers = [(y, x, c, up), (y, x, o, up), (y, x, c, down), (y, x, o, down)]

    def ring(f, dp, dq):
        if f == 0:
            return ((y + dq) % 4, (x + dp) % 4, c, z)
        return ((y + dp) % 4, (x + dq) % 4, c, z)

    def unit(f, dp, dq, s):
        place = ring(f, dp, dq)
        return ((place[0] * 4 + place[1]) * 2 + s) * 2 + f

    def done(ref, sem):
        pltpu.make_async_copy(ref, ref, sem).wait()

    def for_others(act, cores=1):
        def block(b, carry, skip=0):
            for d in range(skip, 4 * cores):
                act(((y + b // 4) % 4, (x + b % 4) % 4, (c + d // 4) % 2, (z + d % 4) % 4))
            return carry

        lax.fori_loop(1, 16, block, 0)
        block(0, 0, 1)

    barrier = pltpu.get_barrier_semaphore()
    near = [
        [(y, x, c, (z + d) % 4) for d in (1, 3, 2)],
        [(y, (x + d) % 4, c, z) for d in (1, 3, 2)],
        [((y + d) % 4, x, c, z) for d in (1, 3, 2)],
        [sibling],
    ]
    peers = near[0] + near[1] + near[2] + near[3] + [z_peers[1], z_peers[3]]
    for peer in peers:
        pl.semaphore_signal(barrier, inc=1, device_id=peer, device_id_type=MESH)

    def tell(stage):
        for peer in near[stage]:
            pl.semaphore_signal(here_sem.at[stage], inc=1, device_id=peer, device_id_type=MESH)

    def told(stage):
        pl.semaphore_wait(here_sem.at[stage], len(near[stage]))


    half_k = pl.ds(pl.multiple_of(16 * h, 16), 16)
    mine = pl.ds(pl.multiple_of(128 * c, 128), 128)
    theirs = pl.ds(pl.multiple_of(128 * o, 128), 128)
    loads = [
        pltpu.make_async_copy(onsite_ref, onsite_v, load_sem.at[0]),
        pltpu.make_async_copy(ids_ref, ids_v, load_sem.at[1]),
        pltpu.make_async_copy(atoms_ref, atoms_v, load_sem.at[2]),
        pltpu.make_async_copy(shift_ref, shift_s, load_sem.at[3]),
        pltpu.make_async_copy(start_ref, where_s.at[0], load_sem.at[4]),
        pltpu.make_async_copy(row_ref, where_s.at[1], load_sem.at[5]),
        pltpu.make_async_copy(col_ref, where_s.at[2], load_sem.at[6]),
    ]
    for load in loads:
        load.start()
    for f in range(2):
        u = unit(f, 0, 0, c)
        pltpu.make_async_copy(blocks_ref.at[pl.ds(16 * f, 16), half_k, mine], held.at[pl.ds(17 * u, 16)], own_sem.at[f]).start()
    loads[0].wait()
    loads[1].wait()
    tiled = jnp.concatenate([ids_v[...]] * 4, axis=1)
    small[0] = onsite_v[:, :128].reshape(2, 16, 128)
    small[1] = onsite_v[:, 128:].reshape(2, 16, 128)
    small[2] = (tiled // 32).astype(F32).astype(BF16).reshape(2, 16, 128)
    small[3] = (tiled % 32).astype(F32).astype(BF16).reshape(2, 16, 128)
    for f in range(2):
        u = unit(f, 0, 0, c)
        pltpu.make_async_copy(small.at[2 * h + c, f], held.at[17 * u + 16], own_sem.at[f]).start()
    pl.semaphore_wait(barrier, len(peers))
    tell(0)
    for f in range(2):
        u = unit(f, 0, 0, c)
        pltpu.make_async_remote_copy(blocks_ref.at[pl.ds(16 * f, 16), half_k, theirs], held.at[pl.ds(17 * u, 16)], sib_send, recv_sem.at[u], device_id=sibling, device_id_type=MESH).start()
        pltpu.make_async_remote_copy(small.at[2 * h + o, f], held.at[17 * u + 16], sib_send, recv_sem.at[u], device_id=sibling, device_id_type=MESH).start()

    def send(f, u, dp, dq):
        pltpu.make_async_remote_copy(held.at[pl.ds(17 * u, 17)], held.at[pl.ds(17 * u, 17)], send_sem, recv_sem.at[u], device_id=ring(f, dp, dq), device_id_type=MESH).start()

    def arrived(u):
        done(held.at[pl.ds(17 * u, 17)], recv_sem.at[u])

    def beside(f, u):
        send(f, u, 1, 0)
        send(f, u, 3, 0)

    def far(f, u):
        send(f, u, 0, 1)
        send(f, u, 0, 3)

    for f in range(2):
        u = unit(f, 0, 0, c)
        done(held.at[pl.ds(17 * u, 17)], own_sem.at[f])
        beside(f, u)
    for f in range(2):
        u = unit(f, 0, 0, o)
        arrived(u)
        beside(f, u)
    for s in (c, o):
        for f in range(2):
            far(f, unit(f, 0, 0, s))
    for load in loads[2:]:
        load.wait()
    for i in range(TASKS):
        pltpu.make_async_copy(basis_ref.at[i], basis_v.at[i], basis_sem.at[i]).start()
    atoms = atoms_v[...]
    wants_v[5] = jnp.concatenate([atoms, atoms + lax.shift_right_logical(atoms, 4)], axis=1)
    want_to = [z_peers[2], z_peers[3], z_peers[0], z_peers[1], sibling]
    for slot_to, peer in enumerate(want_to):
        pltpu.make_async_remote_copy(wants_v.at[5], wants_v.at[slot_to], want_send, want_recv, device_id=peer, device_id_type=MESH).start()
    lane1 = iota((1, 128), 1)
    where = jnp.zeros((1, 128), I32)
    for v in range(3):
        for t in range(TASKS):
            where = jnp.where(lane1 == 4 * v + t, where_s[v, t], where)
    where_v[...] = where
    wheres[pl.ds(slot, 1), :] = where

    def take_near(first):
        s = c if first else o
        for f in range(2):
            u = unit(f, 3, 0, s)
            arrived(u)
            if first:
                send(f, u, 1, 0)
            far(f, u)
            u = unit(f, 1, 0, s)
            arrived(u)
            if not first:
                send(f, u, 3, 0)
            far(f, u)

    def take_far(dp, first):
        s = c if first else o
        for f in range(2):
            u = unit(f, dp, 3, s)
            arrived(u)
            if first:
                send(f, u, 0, 1)
            u = unit(f, dp, 1, s)
            arrived(u)
            if not first:
                send(f, u, 0, 3)

    take_near(True)
    told(0)
    tell(1)
    take_near(False)
    told(1)
    tell(2)
    take_far(0, True)
    told(2)
    tell(3)
    take_far(0, False)
    told(3)
    for s in (c, o):
        for f in range(2):
            u = unit(f, 2, 0, s)
            arrived(u)
            far(f, u)
    for dp in (3, 1, 2):
        take_far(dp, True)
        take_far(dp, False)
    for_others(lambda peer: pltpu.make_async_remote_copy(where_v, wheres.at[pl.ds(slot, 1)], where_send, where_recv, device_id=peer, device_id_type=MESH).start())
    others = pl.ds(0, 5)
    done(wants_v.at[others], want_recv)
    moved = pltpu.make_async_copy(wants_v, wants_s, move_sem)
    moved.start()
    fill_constants(perm)
    for dp in range(4):
        for f in range(2):
            for s in (c, o):
                arrived(unit(f, dp, 2, s))
    for u in range(64):
        flat[pl.ds(16 * u, 16), :] = held[17 * u + 16].astype(F32)
    moved.wait()

    def pick(slot, t, j):
        return held[wants_s[slot, t, j + NNB]], flat[pl.ds(wants_s[slot, t, j], 1), :]

    for t in range(TASKS):
        for i in range(4):
            part = i // 2

            def one(r, carry, i=i, t=t, part=part):
                to_z[i, 16 * t + r], rows_f[i, pl.ds(16 * t + r, 1), :] = pick(i, t, 16 * part + r)
                return carry

            lax.fori_loop(0, 16, one, 0, unroll=True)
            rows_z[i, pl.ds(16 * t, 16), :] = rows_f[i, pl.ds(16 * t, 16), :].astype(BF16)
            at = pl.ds(64 * part + 16 * t, 16)
            pltpu.make_async_remote_copy(to_z.at[i, pl.ds(16 * t, 16)], got.at[h, c, at], z_send, z_recv.at[i, t], device_id=z_peers[i], device_id_type=MESH).start()
            pltpu.make_async_remote_copy(rows_z.at[i, pl.ds(16 * t, 16)], gots.at[h, c, at], zs_send.at[1], zs_recv.at[i, t], device_id=z_peers[i], device_id_type=MESH).start()
    for t in range(TASKS):
        for part in range(2):
            first = 64 * part + 16 * t

            def two(r, carry, t=t, part=part, first=first):
                to_sib[first + r], rows_f[4, pl.ds(16 * part + r, 1), :] = pick(4, t, 16 * part + r)
                return carry

            def three(r, carry, t=t, part=part, first=first):
                got[h, c, first + r], rows_f[5, pl.ds(16 * part + r, 1), :] = pick(5, t, 16 * part + r)
                return carry

            lax.fori_loop(0, 16, two, 0, unroll=True)
            at = pl.ds(first, 16)
            rows_sib[at, :] = rows_f[4, pl.ds(16 * part, 16), :].astype(BF16)
            pltpu.make_async_remote_copy(to_sib.at[at], got.at[h, c, at], zs_send.at[0], z_recv.at[4, t], device_id=sibling, device_id_type=MESH).start()
            pltpu.make_async_remote_copy(rows_sib.at[at], gots.at[h, c, at], zs_send.at[2], zs_recv.at[4, t], device_id=sibling, device_id_type=MESH).start()
            lax.fori_loop(0, 16, three, 0, unroll=True)
            gots[h, c, at, :] = rows_f[5, pl.ds(16 * part, 16), :].astype(BF16)

    side = pl.ds(pl.multiple_of(64 * c, 64), 64)
    done(wheres.at[pl.ds(0, DEVICES // 2 - 1)], where_recv)
    pltpu.make_async_remote_copy(wheres.at[side], wheres.at[side], over_send, over_recv, device_id=sibling, device_id_type=MESH).start()
    done(wheres.at[pl.ds(0, 64)], over_recv)
    list_ref[...] = slab_list(wheres, (z * SLAB - 3).astype(F32))

    def wait_task(t):
        for i in range(4):
            done(got.at[0, 0, pl.ds(0, 16)], z_recv.at[i, t])
            done(gots.at[0, 0, pl.ds(0, 16)], zs_recv.at[i, t])
        done(got.at[0, 0, pl.ds(0, 32)], z_recv.at[4, t])
        done(gots.at[0, 0, pl.ds(0, 32)], zs_recv.at[4, t])

    def assemble_task(t):
        def rows(hh, cc):
            return jnp.concatenate([gots[hh, cc, pl.ds(pl.multiple_of(64 * part + 16 * t, 16), 16), :] for part in range(2)], axis=0).astype(F32)

        def atoms_of():
            eye = iota((NNB, NNB), 0) == iota((NNB, NNB), 1)
            atoms = jnp.sum(jnp.where(eye, atoms_v[pl.ds(t, 1), :].astype(F32), 0.0), axis=1, keepdims=True)
            return jnp.broadcast_to(atoms, (NNB, 128))

        return assemble(
            atoms_of,
            lambda: rows(1, 0) * 32.0 + rows(1, 1),
            lambda: jnp.concatenate([rows(0, 0), rows(0, 1)], axis=1),
            lambda j, hh, cc: got[hh, cc, 64 * (j // 16) + 16 * t + j % 16],
            lambda: shift_s[t], perm, found, mixed, whole, pair, start)

    def iterate_task(t):
        def set_density(density):
            dens_ref[t] = density

        def set_box(box):
            boxes_ref[t, slot] = box

        return iterate(start, middle, late, factor, narrow, set_density, lambda: basis_v.at[t], set_box)

    def send_box(part, peer, t, stage):
        pltpu.make_async_remote_copy(boxes_ref.at[t, part], boxes_ref.at[t, part], box_send.at[t, stage], box_recv.at[t, stage], device_id=peer, device_id_type=MESH).start()

    def box_done(t, stage, count, sem):
        done(boxes_ref.at[t, pl.ds(0, count)], sem.at[t, stage])

    z_span = pl.ds(c * 64 + y * 16 + x * 4, 4)

    wait_task(0)
    head, tail = assemble_task(0)
    for step in head + tail:
        step()

    def task(t, carry):
        wait_task(t + 1)
        done(basis_v.at[0], basis_sem.at[t])
        early, rest = iterate_task(t)
        head, tail = assemble_task(t + 1)
        steps = early + rest
        interleaved(steps, head)
        for step in tail:
            step()
        for d in (1, 3, 2):
            send_box(pl.ds(slot, 1), (y, x, c, (z + d) % 4), t, 0)

        return carry

    lax.fori_loop(0, TASKS - 1, task, 0)
    done(basis_v.at[0], basis_sem.at[TASKS - 1])
    early, rest = iterate_task(TASKS - 1)
    for step in early + rest[:2]:
        step()
    for t in range(TASKS - 1):
        box_done(t, 0, 3, box_recv)
        for d in range(1, 16):
            send_box(z_span, ((y + d // 4) % 4, (x + d % 4) % 4, c, z), t, 1)
    for step in rest[2:]:
        step()
    for_others(lambda peer: send_box(pl.ds(slot, 1), peer, TASKS - 1, 0), 2)
    for t in range(TASKS - 1):
        box_done(t, 1, 60, box_recv)
        send_box(pl.ds(c * 64, 64), sibling, t, 2)
    for t in range(TASKS - 1):
        box_done(t, 2, 64, box_recv)
        box_done(t, 0, 3, box_send)
        box_done(t, 1, 60, box_send)
        box_done(t, 2, 64, box_send)
    box_done(TASKS - 1, 0, DEVICES - 1, box_recv)
    box_done(TASKS - 1, 0, DEVICES - 1, box_send)
    done(held.at[pl.ds(0, 34)], sib_send)
    done(held.at[pl.ds(0, 1020)], send_sem)
    done(wants_v.at[others], want_send)
    done(wheres.at[pl.ds(0, DEVICES // 2 - 1)], where_send)
    done(wheres.at[pl.ds(0, 64)], over_send)
    done(to_z, z_send)
    done(to_sib, zs_send.at[0])
    done(rows_z, zs_send.at[1])
    done(rows_sib, zs_send.at[2])


def run_main(*args):
    any_space = pl.BlockSpec(memory_space=pl.ANY)
    vmem = pl.BlockSpec(memory_space=pltpu.VMEM)
    dma = pltpu.SemaphoreType.DMA
    return pl.pallas_call(
        main_kernel,
        out_shape=(
            jax.ShapeDtypeStruct((TASKS, ORDER, CENTRAL), BF16),
            jax.ShapeDtypeStruct((TASKS, DEVICES, 8, 128), BF16),
            jax.ShapeDtypeStruct((8, LISTED), I32),
        ),
        in_specs=[any_space] * 9,
        out_specs=(vmem, vmem, vmem),
        scratch_shapes=[
            pltpu.VMEM((64 * 17, 16, 128), BF16),
            pltpu.VMEM((1024, 128), F32),
            pltpu.VMEM((2, 2, 128, 16, 128), BF16),
            pltpu.VMEM((2, 2, 128, 128), BF16),
            pltpu.VMEM((128, 16, 128), BF16),
            pltpu.VMEM((4, 64, 16, 128), BF16),
            pltpu.VMEM((6, 64, 128), F32),
            pltpu.VMEM((128, 128), BF16),
            pltpu.VMEM((4, 64, 128), BF16),
            pltpu.VMEM((4, 2, 16, 128), BF16),
            pltpu.VMEM((32, 256), BF16),
            pltpu.VMEM((32, 32), I32),
            pltpu.VMEM((TASKS, NNB), I32),
            pltpu.VMEM((TASKS, ORDER, POINTS), BF16),
            pltpu.VMEM((6, TASKS, 2 * NNB), I32),
            pltpu.SMEM((6, TASKS, 2 * NNB), I32),
            pltpu.SMEM((TASKS,), F32),
            pltpu.SMEM((3, TASKS), I32),
            pltpu.VMEM((1, 128), I32),
            pltpu.VMEM((DEVICES, 128), I32),
            pltpu.VMEM((ORDER, ORDER), BF16),
            pltpu.VMEM((4, 256, 256), BF16),
            pltpu.VMEM((ORDER, ORDER), BF16),
            pltpu.VMEM((ORDER, ORDER), BF16),
            pltpu.VMEM((ORDER, ORDER), F32),
            pltpu.VMEM((ORDER, ORDER), BF16),
            pltpu.VMEM((ORDER, ORDER), BF16),
            pltpu.VMEM((ORDER, ORDER), BF16),
            pltpu.VMEM((ORDER, ORDER), BF16),
            pltpu.VMEM((ORDER, CENTRAL), BF16),
            dma((7,)), dma((TASKS,)), dma((2,)), dma, dma, dma((64,)), dma, dma, dma, pltpu.SemaphoreType.REGULAR((4,)), dma, dma((5, TASKS)), dma((3,)), dma((5, TASKS)),
            dma, dma, dma, dma, dma((TASKS, 3)), dma((TASKS, 3)),
        ],
        compiler_params=pltpu.CompilerParams(collective_id=0, has_side_effects=True, vmem_limit_bytes=56 << 20),
    )(*args)


def add_kernel(list_ref, boxes_ref, dens_ref, out_ref, dens_out, grid, sem, dens_sem):
    through = pltpu.make_async_copy(dens_ref, dens_out, dens_sem)
    through.start()
    grid[...] = jnp.zeros_like(grid)
    lane = iota((8, 128), 1)

    line = iota((8, 128), 0)

    def add(n, carry):
        for m in range(TOGETHER):
            at = TOGETHER * n + m
            base, col, down = pl.multiple_of(list_ref[0, at], 8), list_ref[1, at], list_ref[4, at]
            turned = pltpu.roll(pltpu.roll(boxes_ref[list_ref[2, at]].astype(F32), col, 1), down, 0)
            inside = (lane >= col) & (lane < col + 16)
            upper, lower = inside & (line >= down), inside & (line < down)
            pieces = [pltpu.roll(turned, 128 - 16 * l, 1) if l else turned for l in range(8)]
            sums = {}
            for k in range(BOXP):
                first, second = pieces[2 * k], pieces[2 * k + 1]
                parts = [
                    jnp.where(upper, first, 0.0),
                    jnp.where(upper, second, jnp.where(lower, first, 0.0)),
                    jnp.where(lower, second, 0.0),
                ]
                for n8, part in enumerate(parts):
                    off = ROWS * k + 8 * n8
                    sums[off] = grid[pl.ds(base + off, 8), :] + part
            for off, total in sums.items():
                grid[pl.ds(base + off, 8), :] = total
        return carry

    lax.fori_loop(0, (list_ref[3, 0] + TOGETHER - 1) // TOGETHER, add, 0)
    copy = pltpu.make_async_copy(grid.at[pl.ds(3 * ROWS, SLAB * ROWS)], out_ref, sem)
    copy.start()
    copy.wait()
    through.wait()


def add_boxes(listed, boxes, dens):
    any_space = pl.BlockSpec(memory_space=pl.ANY)
    vmem = pl.BlockSpec(memory_space=pltpu.VMEM)
    return pl.pallas_call(
        add_kernel,
        out_shape=(
            jax.ShapeDtypeStruct((SLAB * ROWS, COLS), F32),
            jax.ShapeDtypeStruct(dens.shape, dens.dtype),
        ),
        in_specs=[pl.BlockSpec(memory_space=pltpu.SMEM), vmem, vmem],
        out_specs=(any_space, any_space),
        scratch_shapes=[
            pltpu.VMEM(((SLAB + 10) * ROWS, COLS), F32),
            pltpu.SemaphoreType.DMA,
            pltpu.SemaphoreType.DMA,
        ],
    )(listed, boxes, dens)


def on_device(*args):
    dens, boxes, listed = run_main(*args)
    rho, dens = add_boxes(listed, boxes.reshape(TASKS * DEVICES, 8, 128), dens)
    return dens, rho.reshape(SLAB, ROWS, COLS)


def solution(mesh):
    torus = Mesh(mesh.devices.reshape(4, 4, 2, mesh.shape["grid"]), AXES)
    atoms, both = P(AXES[:3]), P(AXES)
    return jax.shard_map(
        on_device,
        mesh=torus,
        in_specs=(atoms, atoms, atoms, both, both, both, both, both, both),
        out_specs=(both, P("grid")),
        check_vma=False,
    )
```

```python
import jax
import jax.numpy as jnp
from jax import lax
from jax.experimental import pallas as pl
from jax.experimental.pallas import tpu as pltpu
from jax.sharding import Mesh
from jax.sharding import PartitionSpec as P

F32, BF16, I32 = jnp.float32, jnp.bfloat16, jnp.int32
BS, KNB, NNB, ORDER, CENTRAL, POINTS, ITERS = 16, 32, 32, 512, 128, 1024, 3
SLAB, ROWS, COLS, BOXP = 64, 32, 128, 4
DEVICES, TASKS, TOGETHER, LISTED = 128, 4, 24, 640
AXES = ("atoms_0", "atoms_1", "atoms_2", "grid")
MESH = pl.DeviceIdType.MESH


def iota(shape, dim):
    return lax.broadcasted_iota(I32, shape, dim)


def fill_constants(perm):
    rows, cols = iota((ORDER, ORDER), 0), iota((ORDER, ORDER), 1)
    hit = (rows // BS == cols % NNB) & (rows % BS == cols // NNB)
    perm[...] = hit.astype(F32).astype(BF16)


def assemble(atoms_of, ids_of, onsite_of, tile_of, shift_of, perm, found, mixed, whole, pair, start):
    keep = {}
    lane = iota((NNB, 128), 1)

    def prepare():
        keep["ids"], keep["onsite"], keep["atoms"] = ids_of(), onsite_of(), atoms_of()

    def find(g):
        picks = []
        for jj in range(8):
            j = 8 * g + jj
            hit = (keep["ids"][j : j + 1, :] == keep["atoms"]) & (lane // KNB == jj % 4)
            hit = hit.astype(F32)
            none = jnp.zeros((NNB, 128), F32)
            picks.append(jnp.concatenate([hit, none] if jj < 4 else [none, hit], axis=1))
        pick = jnp.concatenate(picks, axis=0).astype(BF16)
        tiles = [jnp.concatenate([tile_of(8 * g + j, h, 0), tile_of(8 * g + j, h, 1)], axis=1) for j in range(8) for h in range(2)]
        got = jnp.dot(pick, jnp.concatenate(tiles, axis=0), preferred_element_type=F32)
        row = iota((8, 256), 0)
        for jj in range(8):
            j = 8 * g + jj
            part = got[NNB * jj : NNB * (jj + 1)]
            own = 8 * (j // 8)
            line = part[own : own + 8] + jnp.where(row == j % 8, keep["onsite"][j : j + 1, :], 0.0)
            pieces = [part[:own]] * (own > 0) + [line] + [part[own + 8 :]] * (own + 8 < NNB)
            found[g, pl.ds(NNB * jj, NNB), :] = jnp.concatenate(pieces, axis=0).astype(BF16)

    def turn(g, half):
        block = lane // BS
        tiles = []
        for j in range(8):
            tile = found[g, pl.ds(NNB * j, NNB), pl.ds(128 * half, 128)]
            tiles.append(pltpu.roll(tile, BS * j, 1) if j else tile)
        tiles = [tiles[-q % 8] for q in range(8)]
        for step in (1, 2, 4):
            odd = (block // step) % 2 == 1
            tiles = [jnp.where(odd, tiles[(q - step) % 8], tiles[q]) for q in range(8)]
        for a in range(8):
            tile = pltpu.roll(tiles[a], 128 - BS * a, 1) if a else tiles[a]
            mixed[pl.ds((8 * half + a) * NNB, NNB), pl.ds(128 * g, 128)] = tile

    def order():
        whole[...] = jnp.dot(perm[...], mixed[...], preferred_element_type=F32).astype(BF16)

    def fold(r):
        rows = pl.ds(128 * r, 128)
        twice = whole[rows, :].astype(F32) + whole[:, rows].T.astype(F32)
        eye = iota((128, 128), 0) == iota((128, 128), 1)
        low, high = 128 * r, 128 * (r + 1)
        diagonal = twice[:, low:high] - jnp.where(eye, 2.0 * shift_of(), 0.0)
        pieces = [twice[:, :low]] * (r > 0) + [diagonal] + [twice[:, high:]] * (r < 3)
        twice = jnp.concatenate(pieces, axis=1)
        pair[rows, :] = twice
        part = jnp.sum(jnp.abs(twice).reshape(16, 8, ORDER), axis=0)
        keep["sum"] = part if r == 0 else keep["sum"] + part

    def limit():
        sums = jnp.sum(keep["sum"], axis=0, keepdims=True)
        bound = 0.5 * jnp.max(sums, axis=1, keepdims=True) + 1e-6
        keep["scale"] = 0.5 / bound

    def scale(r):
        rows = pl.ds(128 * r, 128)
        start[rows, :] = (pair[rows, :] * keep["scale"]).astype(BF16)

    steps = [prepare]
    for g in range(4):
        steps += [lambda g=g: find(g)] + [lambda g=g, half=half: turn(g, half) for half in range(2)]
    steps += [order]
    steps += [lambda r=r: fold(r) for r in range(4)] + [limit]
    return steps, [lambda r=r: scale(r) for r in range(4)]


def less_half(product, first):
    pieces = []
    width = product.shape[1]
    for r in range(ORDER // 128):
        rows = product[128 * r : 128 * (r + 1)]
        lead = 128 * r - first
        if 0 <= lead < width:
            eye = iota((128, 128), 0) == iota((128, 128), 1)
            cut = jnp.where(eye, 1.5, 0.0) - 0.5 * rows[:, lead : lead + 128]
            parts = [-0.5 * rows[:, :lead]] * (lead > 0) + [cut] + [-0.5 * rows[:, lead + 128 :]] * (lead + 128 < width)
            pieces.append(jnp.concatenate(parts, axis=1))
        else:
            pieces.append(-0.5 * rows)
    return jnp.concatenate(pieces, axis=0).astype(BF16)


def iterate(start, middle, late, factor, narrow, set_density, basis_of, set_box):
    keep = {}

    def square(source):
        factor[...] = less_half(jnp.dot(source[...], source[...], preferred_element_type=F32), 0)

    def multiply(source, target):
        target[...] = jnp.dot(source[...], factor[...], preferred_element_type=F32).astype(BF16)

    def last_factor():
        narrow[...] = less_half(jnp.dot(late[...], late[:, :CENTRAL], preferred_element_type=F32), 0)

    def last_product():
        last = jnp.dot(late[...], narrow[...], preferred_element_type=F32)
        eye = iota((CENTRAL, CENTRAL), 0) == iota((CENTRAL, CENTRAL), 1)
        top = 0.5 * (jnp.where(eye, 1.0, 0.0) - last[:CENTRAL])
        density = jnp.concatenate([top, 0.5 * (0.0 - last[CENTRAL:])], axis=0).astype(BF16)
        set_density(density)
        keep["density"] = density.T

    def collocate(n):
        basis = basis_of()
        cols = pl.ds(512 * n, 512)
        weights = jnp.dot(keep["density"], basis[:, cols], preferred_element_type=F32)
        part = jnp.sum(weights * basis[:CENTRAL, cols].astype(F32), axis=0, keepdims=True)
        keep.setdefault("values", []).append(part)

    def finish():
        set_box(pack_box(jnp.concatenate(keep["values"], axis=1)))

    early = [lambda: square(start), lambda: multiply(start, middle)]
    rest = [lambda: square(middle), lambda: multiply(middle, late), last_factor, last_product]
    rest += [lambda n=n: collocate(n) for n in range(2)] + [finish]
    return early, rest


def interleaved(first, second):
    marks = [((k + 0.5) / len(first), 0, k) for k in range(len(first))] + [((k + 0.5) / len(second), 1, k) for k in range(len(second))]
    for _, which, k in sorted(marks):
        (first, second)[which][k]()


def pack_box(values):
    box = jnp.concatenate([values[:, 128 * l : 128 * (l + 1)] for l in range(8)], axis=0)
    row, lane = iota((8, 128), 0), iota((8, 128), 1)
    for step in (1, 2, 4):
        high_row, high_lane = (row // step) % 2 == 1, (lane // (BS * step)) % 2 == 1
        from_below = pltpu.roll(pltpu.roll(box, 8 - step, 0), BS * step, 1)
        from_above = pltpu.roll(pltpu.roll(box, step, 0), 128 - BS * step, 1)
        crossed = jnp.where(high_row, from_above, from_below)
        box = jnp.where(high_row == high_lane, box, crossed)
    return box.astype(BF16)


def slab_list(wheres, first):
    rows = wheres[...].astype(F32)
    lane = iota((DEVICES, 128), 1)
    start = rows - first
    hit = ((start >= 0) & (start < SLAB + 3) & (lane < TASKS)).astype(F32)
    below = (iota((DEVICES, DEVICES), 1) < iota((DEVICES, DEVICES), 0)).astype(F32).astype(BF16)
    before = jnp.dot(below, hit.astype(BF16), preferred_element_type=F32)
    totals = jnp.sum(hit, axis=0, keepdims=True)
    turned = rows.T
    slots = iota((DEVICES, LISTED), 1).astype(F32)
    base = jnp.zeros((1, 1), F32)
    listed = jnp.zeros((8, LISTED), F32)
    line = iota((8, 128), 0)
    device = iota((8, 128), 1).astype(F32)
    for t in range(TASKS):
        chosen = (before[:, t : t + 1] + base == slots) & (hit[:, t : t + 1] > 0.5)
        values = jnp.where(line == 3, device, jnp.where(line == 4, float(t), 0.0))
        for v in range(3):
            values = jnp.where(line == v, turned[4 * v + t : 4 * v + t + 1, :], values)
        listed += jnp.dot(values.astype(BF16), chosen.astype(F32).astype(BF16), preferred_element_type=F32)
        base = base + totals[:, t : t + 1]
    row, slot = iota((8, LISTED), 0), iota((8, LISTED), 1).astype(F32)
    eights = jnp.floor(listed[1:2] * 0.125) * 8.0
    base_row = (listed[0:1] - first) * ROWS + eights
    lines = [
        jnp.where(slot[0:1] < base, base_row, (SLAB + 6.0) * ROWS),
        listed[2:3],
        listed[4:5] * DEVICES + listed[3:4],
        base,
        listed[1:2] - eights,
    ]
    out = jnp.zeros((8, LISTED), F32)
    for v, values in enumerate(lines):
        out = jnp.where(row == v, values, out)
    return out.astype(I32)


def main_kernel(blocks_ref, onsite_ref, ids_ref, atoms_ref, shift_ref, basis_ref, start_ref, row_ref, col_ref,
                dens_ref, boxes_ref, list_ref,
                held, flat, got, gots, to_sib, to_z, rows_f, rows_sib, rows_z, small, onsite_v, ids_v, atoms_v, basis_v,
                wants_v, wants_s, shift_s, where_s, where_v, wheres, perm, found, mixed, whole, pair, start, middle, late, factor, narrow,
                load_sem, basis_sem, own_sem, sib_send, send_sem, recv_sem, want_send, want_recv, move_sem, here_sem, z_send, z_recv, zs_send, zs_recv,
                where_send, where_recv, over_send, over_recv, box_send, box_recv):
    y, x, c, z = (lax.axis_index(a) for a in AXES)
    h, o = z % 2, 1 - c
    slot = c * 64 + y * 16 + x * 4 + z
    sibling = (y, x, o, z)
    up, down = (z + 1) % 4, (z + 3) % 4
    z_peers = [(y, x, c, up), (y, x, o, up), (y, x, c, down), (y, x, o, down)]

    def ring(f, dp, dq):
        if f == 0:
            return ((y + dq) % 4, (x + dp) % 4, c, z)
        return ((y + dp) % 4, (x + dq) % 4, c, z)

    def unit(f, dp, dq, s):
        place = ring(f, dp, dq)
        return ((place[0] * 4 + place[1]) * 2 + s) * 2 + f

    def done(ref, sem):
        pltpu.make_async_copy(ref, ref, sem).wait()

    def for_others(act, cores=1):
        def block(b, carry, skip=0):
            for d in range(skip, 4 * cores):
                act(((y + b // 4) % 4, (x + b % 4) % 4, (c + d // 4) % 2, (z + d % 4) % 4))
            return carry

        lax.fori_loop(1, 16, block, 0)
        block(0, 0, 1)

    barrier = pltpu.get_barrier_semaphore()
    near = [
        [(y, x, c, (z + d) % 4) for d in (1, 3, 2)],
        [(y, (x + d) % 4, c, z) for d in (1, 3, 2)],
        [((y + d) % 4, x, c, z) for d in (1, 3, 2)],
        [sibling],
    ]
    peers = near[0] + near[1] + near[2] + near[3] + [z_peers[1], z_peers[3]]
    for peer in peers:
        pl.semaphore_signal(barrier, inc=1, device_id=peer, device_id_type=MESH)

    def tell(stage):
        for peer in near[stage]:
            pl.semaphore_signal(here_sem.at[stage], inc=1, device_id=peer, device_id_type=MESH)

    def told(stage):
        pl.semaphore_wait(here_sem.at[stage], len(near[stage]))


    half_k = pl.ds(pl.multiple_of(16 * h, 16), 16)
    mine = pl.ds(pl.multiple_of(128 * c, 128), 128)
    theirs = pl.ds(pl.multiple_of(128 * o, 128), 128)
    loads = [
        pltpu.make_async_copy(onsite_ref, onsite_v, load_sem.at[0]),
        pltpu.make_async_copy(ids_ref, ids_v, load_sem.at[1]),
        pltpu.make_async_copy(atoms_ref, atoms_v, load_sem.at[2]),
        pltpu.make_async_copy(shift_ref, shift_s, load_sem.at[3]),
        pltpu.make_async_copy(start_ref, where_s.at[0], load_sem.at[4]),
        pltpu.make_async_copy(row_ref, where_s.at[1], load_sem.at[5]),
        pltpu.make_async_copy(col_ref, where_s.at[2], load_sem.at[6]),
    ]
    for load in loads:
        load.start()
    for f in range(2):
        u = unit(f, 0, 0, c)
        pltpu.make_async_copy(blocks_ref.at[pl.ds(16 * f, 16), half_k, mine], held.at[pl.ds(17 * u, 16)], own_sem.at[f]).start()
    loads[0].wait()
    loads[1].wait()
    tiled = jnp.concatenate([ids_v[...]] * 4, axis=1)
    small[0] = onsite_v[:, :128].reshape(2, 16, 128)
    small[1] = onsite_v[:, 128:].reshape(2, 16, 128)
    small[2] = (tiled // 32).astype(F32).astype(BF16).reshape(2, 16, 128)
    small[3] = (tiled % 32).astype(F32).astype(BF16).reshape(2, 16, 128)
    for f in range(2):
        u = unit(f, 0, 0, c)
        pltpu.make_async_copy(small.at[2 * h + c, f], held.at[17 * u + 16], own_sem.at[f]).start()
    pl.semaphore_wait(barrier, len(peers))
    tell(0)
    for f in range(2):
        u = unit(f, 0, 0, c)
        pltpu.make_async_remote_copy(blocks_ref.at[pl.ds(16 * f, 16), half_k, theirs], held.at[pl.ds(17 * u, 16)], sib_send, recv_sem.at[u], device_id=sibling, device_id_type=MESH).start()
        pltpu.make_async_remote_copy(small.at[2 * h + o, f], held.at[17 * u + 16], sib_send, recv_sem.at[u], device_id=sibling, device_id_type=MESH).start()

    def send(f, u, dp, dq):
        pltpu.make_async_remote_copy(held.at[pl.ds(17 * u, 17)], held.at[pl.ds(17 * u, 17)], send_sem, recv_sem.at[u], device_id=ring(f, dp, dq), device_id_type=MESH).start()

    def arrived(u):
        done(held.at[pl.ds(17 * u, 17)], recv_sem.at[u])

    def beside(f, u):
        send(f, u, 1, 0)
        send(f, u, 3, 0)

    def far(f, u):
        send(f, u, 0, 1)
        send(f, u, 0, 3)

    for f in range(2):
        u = unit(f, 0, 0, c)
        done(held.at[pl.ds(17 * u, 17)], own_sem.at[f])
        beside(f, u)
    for f in range(2):
        far(f, unit(f, 0, 0, c))
    for f in range(2):
        u = unit(f, 0, 0, o)
        arrived(u)
        beside(f, u)
    for f in range(2):
        far(f, unit(f, 0, 0, o))
    for load in loads[2:]:
        load.wait()
    for i in range(TASKS):
        pltpu.make_async_copy(basis_ref.at[i], basis_v.at[i], basis_sem.at[i]).start()
    atoms = atoms_v[...]
    wants_v[5] = jnp.concatenate([atoms, atoms + lax.shift_right_logical(atoms, 4)], axis=1)
    want_to = [z_peers[2], z_peers[3], z_peers[0], z_peers[1], sibling]
    for slot_to, peer in enumerate(want_to):
        pltpu.make_async_remote_copy(wants_v.at[5], wants_v.at[slot_to], want_send, want_recv, device_id=peer, device_id_type=MESH).start()
    lane1 = iota((1, 128), 1)
    where = jnp.zeros((1, 128), I32)
    for v in range(3):
        for t in range(TASKS):
            where = jnp.where(lane1 == 4 * v + t, where_s[v, t], where)
    where_v[...] = where
    wheres[pl.ds(slot, 1), :] = where

    def take_near(first):
        s = c if first else o
        for f in range(2):
            u = unit(f, 3, 0, s)
            arrived(u)
            if first:
                send(f, u, 1, 0)
            far(f, u)
            u = unit(f, 1, 0, s)
            arrived(u)
            if not first:
                send(f, u, 3, 0)
            far(f, u)

    def take_far(dp, first):
        s = c if first else o
        for f in range(2):
            u = unit(f, dp, 3, s)
            arrived(u)
            if first:
                send(f, u, 0, 1)
            u = unit(f, dp, 1, s)
            arrived(u)
            if not first:
                send(f, u, 0, 3)

    take_near(True)
    told(0)
    tell(1)
    take_near(False)
    told(1)
    tell(2)
    take_far(0, True)
    told(2)
    tell(3)
    take_far(0, False)
    told(3)
    for s in (c, o):
        for f in range(2):
            u = unit(f, 2, 0, s)
            arrived(u)
            far(f, u)
    for dp in (3, 1, 2):
        take_far(dp, True)
        take_far(dp, False)
    for_others(lambda peer: pltpu.make_async_remote_copy(where_v, wheres.at[pl.ds(slot, 1)], where_send, where_recv, device_id=peer, device_id_type=MESH).start())
    others = pl.ds(0, 5)
    done(wants_v.at[others], want_recv)
    moved = pltpu.make_async_copy(wants_v, wants_s, move_sem)
    moved.start()
    fill_constants(perm)
    for dp in range(4):
        for f in range(2):
            for s in (c, o):
                arrived(unit(f, dp, 2, s))
    for u in range(64):
        flat[pl.ds(16 * u, 16), :] = held[17 * u + 16].astype(F32)
    moved.wait()

    def pick(slot, t, j):
        return held[wants_s[slot, t, j + NNB]], flat[pl.ds(wants_s[slot, t, j], 1), :]

    for t in range(TASKS):
        for i in range(4):
            part = i // 2

            def one(r, carry, i=i, t=t, part=part):
                to_z[i, 16 * t + r], rows_f[i, pl.ds(16 * t + r, 1), :] = pick(i, t, 16 * part + r)
                return carry

            lax.fori_loop(0, 16, one, 0, unroll=True)
            rows_z[i, pl.ds(16 * t, 16), :] = rows_f[i, pl.ds(16 * t, 16), :].astype(BF16)
            at = pl.ds(64 * part + 16 * t, 16)
            pltpu.make_async_remote_copy(to_z.at[i, pl.ds(16 * t, 16)], got.at[h, c, at], z_send, z_recv.at[i, t], device_id=z_peers[i], device_id_type=MESH).start()
            pltpu.make_async_remote_copy(rows_z.at[i, pl.ds(16 * t, 16)], gots.at[h, c, at], zs_send.at[1], zs_recv.at[i, t], device_id=z_peers[i], device_id_type=MESH).start()
    for t in range(TASKS):
        for part in range(2):
            first = 64 * part + 16 * t

            def two(r, carry, t=t, part=part, first=first):
                to_sib[first + r], rows_f[4, pl.ds(16 * part + r, 1), :] = pick(4, t, 16 * part + r)
                return carry

            def three(r, carry, t=t, part=part, first=first):
                got[h, c, first + r], rows_f[5, pl.ds(16 * part + r, 1), :] = pick(5, t, 16 * part + r)
                return carry

            lax.fori_loop(0, 16, two, 0, unroll=True)
            at = pl.ds(first, 16)
            rows_sib[at, :] = rows_f[4, pl.ds(16 * part, 16), :].astype(BF16)
            pltpu.make_async_remote_copy(to_sib.at[at], got.at[h, c, at], zs_send.at[0], z_recv.at[4, t], device_id=sibling, device_id_type=MESH).start()
            pltpu.make_async_remote_copy(rows_sib.at[at], gots.at[h, c, at], zs_send.at[2], zs_recv.at[4, t], device_id=sibling, device_id_type=MESH).start()
            lax.fori_loop(0, 16, three, 0, unroll=True)
            gots[h, c, at, :] = rows_f[5, pl.ds(16 * part, 16), :].astype(BF16)

    side = pl.ds(pl.multiple_of(64 * c, 64), 64)
    done(wheres.at[pl.ds(0, DEVICES // 2 - 1)], where_recv)
    pltpu.make_async_remote_copy(wheres.at[side], wheres.at[side], over_send, over_recv, device_id=sibling, device_id_type=MESH).start()

    def wait_task(t):
        for i in range(4):
            done(got.at[0, 0, pl.ds(0, 16)], z_recv.at[i, t])
            done(gots.at[0, 0, pl.ds(0, 16)], zs_recv.at[i, t])
        done(got.at[0, 0, pl.ds(0, 32)], z_recv.at[4, t])
        done(gots.at[0, 0, pl.ds(0, 32)], zs_recv.at[4, t])

    def assemble_task(t):
        def rows(hh, cc):
            return jnp.concatenate([gots[hh, cc, pl.ds(pl.multiple_of(64 * part + 16 * t, 16), 16), :] for part in range(2)], axis=0).astype(F32)

        def atoms_of():
            eye = iota((NNB, NNB), 0) == iota((NNB, NNB), 1)
            atoms = jnp.sum(jnp.where(eye, atoms_v[pl.ds(t, 1), :].astype(F32), 0.0), axis=1, keepdims=True)
            return jnp.broadcast_to(atoms, (NNB, 128))

        return assemble(
            atoms_of,
            lambda: rows(1, 0) * 32.0 + rows(1, 1),
            lambda: jnp.concatenate([rows(0, 0), rows(0, 1)], axis=1),
            lambda j, hh, cc: got[hh, cc, 64 * (j // 16) + 16 * t + j % 16],
            lambda: shift_s[t], perm, found, mixed, whole, pair, start)

    def iterate_task(t):
        def set_density(density):
            dens_ref[t] = density

        def set_box(box):
            boxes_ref[t, slot] = box

        return iterate(start, middle, late, factor, narrow, set_density, lambda: basis_v.at[t], set_box)

    def send_box(part, peer, t, stage):
        pltpu.make_async_remote_copy(boxes_ref.at[t, part], boxes_ref.at[t, part], box_send.at[t, stage], box_recv.at[t, stage], device_id=peer, device_id_type=MESH).start()

    def box_done(t, stage, count, sem):
        done(boxes_ref.at[t, pl.ds(0, count)], sem.at[t, stage])

    z_span = pl.ds(c * 64 + y * 16 + x * 4, 4)

    wait_task(0)
    head, tail = assemble_task(0)
    for step in head + tail:
        step()

    def task(t, carry):
        wait_task(t + 1)
        done(basis_v.at[0], basis_sem.at[t])
        early, rest = iterate_task(t)
        head, tail = assemble_task(t + 1)
        steps = early + rest
        interleaved(steps, head)
        for step in tail:
            step()
        for d in (1, 3, 2):
            send_box(pl.ds(slot, 1), (y, x, c, (z + d) % 4), t, 0)

        return carry

    lax.fori_loop(0, TASKS - 1, task, 0)
    done(basis_v.at[0], basis_sem.at[TASKS - 1])
    early, rest = iterate_task(TASKS - 1)
    for step in early + rest[:2]:
        step()
    for t in range(TASKS - 1):
        box_done(t, 0, 3, box_recv)
        for d in range(1, 16):
            send_box(z_span, ((y + d // 4) % 4, (x + d % 4) % 4, c, z), t, 1)
    for step in rest[2:]:
        step()
    for_others(lambda peer: send_box(pl.ds(slot, 1), peer, TASKS - 1, 0), 2)
    done(wheres.at[pl.ds(0, 64)], over_recv)
    list_ref[...] = slab_list(wheres, (z * SLAB - 3).astype(F32))
    for t in range(TASKS - 1):
        box_done(t, 1, 60, box_recv)
        send_box(pl.ds(c * 64, 64), sibling, t, 2)
    for t in range(TASKS - 1):
        box_done(t, 2, 64, box_recv)
        box_done(t, 0, 3, box_send)
        box_done(t, 1, 60, box_send)
        box_done(t, 2, 64, box_send)
    box_done(TASKS - 1, 0, DEVICES - 1, box_recv)
    box_done(TASKS - 1, 0, DEVICES - 1, box_send)
    done(held.at[pl.ds(0, 34)], sib_send)
    done(held.at[pl.ds(0, 1020)], send_sem)
    done(wants_v.at[others], want_send)
    done(wheres.at[pl.ds(0, DEVICES // 2 - 1)], where_send)
    done(wheres.at[pl.ds(0, 64)], over_send)
    done(to_z, z_send)
    done(to_sib, zs_send.at[0])
    done(rows_z, zs_send.at[1])
    done(rows_sib, zs_send.at[2])


def run_main(*args):
    any_space = pl.BlockSpec(memory_space=pl.ANY)
    vmem = pl.BlockSpec(memory_space=pltpu.VMEM)
    dma = pltpu.SemaphoreType.DMA
    return pl.pallas_call(
        main_kernel,
        out_shape=(
            jax.ShapeDtypeStruct((TASKS, ORDER, CENTRAL), BF16),
            jax.ShapeDtypeStruct((TASKS, DEVICES, 8, 128), BF16),
            jax.ShapeDtypeStruct((8, LISTED), I32),
        ),
        in_specs=[any_space] * 9,
        out_specs=(vmem, vmem, vmem),
        scratch_shapes=[
            pltpu.VMEM((64 * 17, 16, 128), BF16),
            pltpu.VMEM((1024, 128), F32),
            pltpu.VMEM((2, 2, 128, 16, 128), BF16),
            pltpu.VMEM((2, 2, 128, 128), BF16),
            pltpu.VMEM((128, 16, 128), BF16),
            pltpu.VMEM((4, 64, 16, 128), BF16),
            pltpu.VMEM((6, 64, 128), F32),
            pltpu.VMEM((128, 128), BF16),
            pltpu.VMEM((4, 64, 128), BF16),
            pltpu.VMEM((4, 2, 16, 128), BF16),
            pltpu.VMEM((32, 256), BF16),
            pltpu.VMEM((32, 32), I32),
            pltpu.VMEM((TASKS, NNB), I32),
            pltpu.VMEM((TASKS, ORDER, POINTS), BF16),
            pltpu.VMEM((6, TASKS, 2 * NNB), I32),
            pltpu.SMEM((6, TASKS, 2 * NNB), I32),
            pltpu.SMEM((TASKS,), F32),
            pltpu.SMEM((3, TASKS), I32),
            pltpu.VMEM((1, 128), I32),
            pltpu.VMEM((DEVICES, 128), I32),
            pltpu.VMEM((ORDER, ORDER), BF16),
            pltpu.VMEM((4, 256, 256), BF16),
            pltpu.VMEM((ORDER, ORDER), BF16),
            pltpu.VMEM((ORDER, ORDER), BF16),
            pltpu.VMEM((ORDER, ORDER), F32),
            pltpu.VMEM((ORDER, ORDER), BF16),
            pltpu.VMEM((ORDER, ORDER), BF16),
            pltpu.VMEM((ORDER, ORDER), BF16),
            pltpu.VMEM((ORDER, ORDER), BF16),
            pltpu.VMEM((ORDER, CENTRAL), BF16),
            dma((7,)), dma((TASKS,)), dma((2,)), dma, dma, dma((64,)), dma, dma, dma, pltpu.SemaphoreType.REGULAR((4,)), dma, dma((5, TASKS)), dma((3,)), dma((5, TASKS)),
            dma, dma, dma, dma, dma((TASKS, 3)), dma((TASKS, 3)),
        ],
        compiler_params=pltpu.CompilerParams(collective_id=0, has_side_effects=True, vmem_limit_bytes=56 << 20),
    )(*args)


def add_kernel(list_ref, boxes_ref, dens_ref, out_ref, dens_out, grid, sem, dens_sem):
    through = pltpu.make_async_copy(dens_ref, dens_out, dens_sem)
    through.start()
    grid[...] = jnp.zeros_like(grid)
    lane = iota((8, 128), 1)

    line = iota((8, 128), 0)

    def add(n, carry):
        for m in range(TOGETHER):
            at = TOGETHER * n + m
            base, col, down = pl.multiple_of(list_ref[0, at], 8), list_ref[1, at], list_ref[4, at]
            turned = pltpu.roll(pltpu.roll(boxes_ref[list_ref[2, at]].astype(F32), col, 1), down, 0)
            inside = (lane >= col) & (lane < col + 16)
            upper, lower = inside & (line >= down), inside & (line < down)
            pieces = [pltpu.roll(turned, 128 - 16 * l, 1) if l else turned for l in range(8)]
            sums = {}
            for k in range(BOXP):
                first, second = pieces[2 * k], pieces[2 * k + 1]
                parts = [
                    jnp.where(upper, first, 0.0),
                    jnp.where(upper, second, jnp.where(lower, first, 0.0)),
                    jnp.where(lower, second, 0.0),
                ]
                for n8, part in enumerate(parts):
                    off = ROWS * k + 8 * n8
                    sums[off] = grid[pl.ds(base + off, 8), :] + part
            for off, total in sums.items():
                grid[pl.ds(base + off, 8), :] = total
        return carry

    lax.fori_loop(0, (list_ref[3, 0] + TOGETHER - 1) // TOGETHER, add, 0)
    copy = pltpu.make_async_copy(grid.at[pl.ds(3 * ROWS, SLAB * ROWS)], out_ref, sem)
    copy.start()
    copy.wait()
    through.wait()


def add_boxes(listed, boxes, dens):
    any_space = pl.BlockSpec(memory_space=pl.ANY)
    vmem = pl.BlockSpec(memory_space=pltpu.VMEM)
    return pl.pallas_call(
        add_kernel,
        out_shape=(
            jax.ShapeDtypeStruct((SLAB * ROWS, COLS), F32),
            jax.ShapeDtypeStruct(dens.shape, dens.dtype),
        ),
        in_specs=[pl.BlockSpec(memory_space=pltpu.SMEM), vmem, vmem],
        out_specs=(any_space, any_space),
        scratch_shapes=[
            pltpu.VMEM(((SLAB + 10) * ROWS, COLS), F32),
            pltpu.SemaphoreType.DMA,
            pltpu.SemaphoreType.DMA,
        ],
    )(listed, boxes, dens)


def on_device(*args):
    dens, boxes, listed = run_main(*args)
    rho, dens = add_boxes(listed, boxes.reshape(TASKS * DEVICES, 8, 128), dens)
    return dens, rho.reshape(SLAB, ROWS, COLS)


def solution(mesh):
    torus = Mesh(mesh.devices.reshape(4, 4, 2, mesh.shape["grid"]), AXES)
    atoms, both = P(AXES[:3]), P(AXES)
    return jax.shard_map(
        on_device,
        mesh=torus,
        in_specs=(atoms, atoms, atoms, both, both, both, both, both, both),
        out_specs=(both, P("grid")),
        check_vma=False,
    )
```
